32 devices in a mesh: fsdp: 8 (over z, x), seq: 4 (over y, core).
Axes of the slice: x: 2, y: 2, z: 4, core: 2. Of those that a mesh axis runs over, the one named last changes fastest.
Arguments:
- hidden_in: bfloat16 [2, 8, 1024, 768], P(None, 'fsdp', 'seq'), may hold values from -6 to 6
- cotangent: bfloat16 [2, 8, 1024, 768], P(None, 'fsdp', 'seq'), may hold values from -6 to 6
- attn_gain: bfloat16 [2, 768], P(None, 'fsdp'), may hold values from 0.5 to 1.5
- query_weight: bfloat16 [2, 768, 768], P(None, 'fsdp'), may hold values from -0.21875 to 0.21875
- key_weight: bfloat16 [2, 768, 768], P(None, 'fsdp'), may hold values from -0.21875 to 0.21875
- value_weight: bfloat16 [2, 768, 768], P(None, 'fsdp'), may hold values from -0.21875 to 0.21875
- out_weight: bfloat16 [2, 768, 768], P(None, 'fsdp'), may hold values from -0.875 to 0.875
- ffn_gain: bfloat16 [2, 768], P(None, 'fsdp'), may hold values from 0.5 to 1.5
- gate_weight: bfloat16 [2, 768, 2048], P(None, 'fsdp'), may hold values from -0.21875 to 0.21875
- up_weight: bfloat16 [2, 768, 2048], P(None, 'fsdp'), may hold values from -0.21875 to 0.21875
- down_weight: bfloat16 [2, 2048, 768], P(None, 'fsdp'), may hold values from -0.125 to 0.125
Outputs:
- layer_out: float32 [2, 8, 1024, 768], P(None, 'fsdp', 'seq')
- input_grad: float32 [2, 8, 1024, 768], P(None, 'fsdp', 'seq')
- grad_attn_gain: float32 [2, 768], P(None, 'fsdp')
- grad_query: float32 [2, 768, 768], P(None, 'fsdp')
- grad_key: float32 [2, 768, 768], P(None, 'fsdp')
- grad_value: float32 [2, 768, 768], P(None, 'fsdp')
- grad_out_weight: float32 [2, 768, 768], P(None, 'fsdp')
- grad_ffn_gain: float32 [2, 768], P(None, 'fsdp')
- grad_gate: float32 [2, 768, 2048], P(None, 'fsdp')
- grad_up: float32 [2, 768, 2048], P(None, 'fsdp')
- grad_down: float32 [2, 2048, 768], P(None, 'fsdp')
The draws below stay inside these ranges and needn't reach their ends.
All inputs are finite; a program needn't handle non-finite values.
Results may differ from the reference program's by a relative error of at most 0.029.
Values may be sent and summed in bfloat16 or wider, within the bound.
No kernel may reach another device: no remote copies, remote signals or barrier semaphores. Data moves between devices by JAX's collectives and lax.ppermute only.
A program may use at most 256 MiB of HBM per device.

```python
import math
import jax
import jax.numpy as jnp
from jax import lax

D = 768
H = 12
HD = 64
FF = 2048
MB = 2
LEN = 1024
BATCH = 8


def block_scale(stream_key, dims, cuts, least, top_value):
    loudness = 1.0
    for position, parts in cuts:
        draws = jax.random.uniform(jax.random.fold_in(jax.random.fold_in(stream_key, 6), position), (parts,), jnp.float32, least / len(cuts), top_value / len(cuts))
        loudness = loudness * jnp.repeat(jnp.exp(draws), dims[position] // parts).reshape((-1,) + (1,) * (len(dims) - 1 - position))
    return loudness


def centred(rng, dims, width, limit, split=(), held_as=jnp.bfloat16):
    values = jax.random.normal(rng, dims, jnp.float32) * width
    if len(split) > 0:
        values = block_scale(rng, dims, split, -0.22, 0.18) * values
    return jnp.clip(values, min=-limit, max=limit).astype(held_as)


def setup_inputs(seed: int = 0) -> dict:
    key_list = jax.random.split(jax.random.key(seed), 12)
    return {
        "hidden_in": centred(key_list[0], (MB, BATCH, LEN, D), 1.0, 6.0, ((1, 8), (2, 4))),
        "cotangent": centred(key_list[1], (MB, BATCH, LEN, D), 1.0, 6.0, ((1, 8), (2, 4))),
        "attn_gain": jnp.clip(1.0 + 0.1 * jax.random.normal(key_list[2], (2, D), jnp.float32), 0.5, 1.5).astype(jnp.bfloat16),
        "query_weight": centred(key_list[3], (2, D, D), D ** -0.5, 0.21875, ((1, 8),)),
        "key_weight": centred(key_list[4], (2, D, D), D ** -0.5, 0.21875, ((1, 8),)),
        "value_weight": centred(key_list[5], (2, D, D), D ** -0.5, 0.21875, ((1, 8),)),
        "out_weight": centred(key_list[6], (2, D, D), (D // 16) ** -0.5, 0.875, ((1, 8),)),
        "ffn_gain": jnp.clip(1.0 + 0.1 * jax.random.normal(key_list[7], (2, D), jnp.float32), 0.5, 1.5).astype(jnp.bfloat16),
        "gate_weight": centred(key_list[8], (2, D, FF), D ** -0.5, 0.21875, ((1, 8),)),
        "up_weight": centred(key_list[9], (2, D, FF), D ** -0.5, 0.21875, ((1, 8),)),
        "down_weight": centred(key_list[10], (2, FF, D), FF ** -0.5, 0.125, ((1, 8),)),
    }


highest = lax.Precision.HIGHEST
epsilon = 1e-05
masked_value = -1e+30

@jax.custom_vjp
def low(v):
    return lax.optimization_barrier(v.astype(jnp.bfloat16)).astype(jnp.float32)

@jax.custom_vjp
def low_back(v):
    return v

def low_keep(v):
    return (low(v), None)

def low_pass(kept, grad):
    return (grad,)

def back_keep(v):
    return (v, None)

def back_low(kept, grad):
    return (low(grad),)
low.defvjp(low_keep, low_pass)
low_back.defvjp(back_keep, back_low)

def rotate(values, positions, direction):
    half_dim = values.shape[-1] // 2
    freq_rates = jnp.exp(jnp.arange(half_dim, dtype=jnp.float32) * (-2.0 * math.log(10000.0) / values.shape[-1]))
    angles = positions.astype(jnp.float32)[:, None] * freq_rates[None, :]
    cosine = jnp.cos(angles)[:, None, :]
    sine_part = direction * jnp.sin(angles)[:, None, :]
    first_half = values[..., :half_dim]
    second = values[..., half_dim:]
    return jnp.concatenate([first_half * cosine - second * sine_part, second * cosine + first_half * sine_part], -1)

def normalize(values, norm_gain):
    return values * lax.rsqrt(lax.optimization_barrier(jnp.mean(values * values, -1, keepdims=True)) + epsilon) * norm_gain

def matmul(left_side, right_side):
    return jnp.dot(left_side, right_side, precision=highest)

def attention(normed_in, w_query, w_key, w_value, w_out):
    positions = jnp.arange(LEN, dtype=jnp.int32)
    entry_low = low(normed_in)
    query_all = low(rotate(low_back(matmul(entry_low, w_query)).reshape(LEN, H, HD), positions, 1.0))
    key_all = low(rotate(low_back(matmul(entry_low, w_key)).reshape(LEN, H, HD), positions, 1.0))
    value_all = low(low_back(matmul(entry_low, w_value))).reshape(LEN, H, HD)
    block_rows = min(512, LEN)
    score_scale = HD ** (-0.5)
    columns = jnp.arange(LEN, dtype=jnp.int32)

    def one_block(row_start):
        query_part = lax.dynamic_slice_in_dim(query_all, row_start, block_rows, 0)
        scores = low_back(jnp.einsum('qhd,khd->hqk', query_part, key_all, precision=highest)) * score_scale
        row_ids = row_start + jnp.arange(block_rows, dtype=jnp.int32)
        allowed = columns[None, None, :] <= row_ids[None, :, None]
        scores = jnp.where(allowed, scores, masked_value)
        row_top = lax.optimization_barrier(jnp.max(scores, -1, keepdims=True))
        weights = jnp.exp(scores - row_top)
        probs = weights / lax.optimization_barrier(jnp.sum(weights, -1, keepdims=True))
        return jnp.einsum('hqk,khd->qhd', low(probs), value_all, precision=highest)
    row_starts = (jnp.arange(LEN // block_rows, dtype=jnp.int32) * block_rows).astype(jnp.int32)
    mixed_out = lax.map(jax.checkpoint(one_block), row_starts).reshape(LEN, D)
    merged = low(low_back(mixed_out))
    return low_back(matmul(merged, w_out))

def feed_forward(normed_in, w_gate, w_up, w_down):
    entry_low = low(normed_in)
    gate_pre = low_back(matmul(entry_low, w_gate))
    up_pre = low_back(matmul(entry_low, w_up))
    hidden = low(jax.nn.silu(gate_pre) * up_pre)
    return low_back(matmul(hidden, w_down))

def two_layers(inputs, params):
    gains_a, w_query, w_key, w_value, w_out, gains_f, w_gate, w_up, w_down = params
    summed = inputs + attention(inputs, w_query[0], w_key[0], w_value[0], w_out[0])
    normed = normalize(summed, gains_a[0])
    middle = normalize(normed + feed_forward(normed, w_gate[0], w_up[0], w_down[0]), gains_f[0])
    second_sum = middle + attention(normalize(middle, gains_a[1]), w_query[1], w_key[1], w_value[1], w_out[1])
    return second_sum + feed_forward(normalize(second_sum, gains_f[1]), w_gate[1], w_up[1], w_down[1])

def reference(hidden_in, cotangent, attn_gain, query_weight, key_weight, value_weight, out_weight, ffn_gain, gate_weight, up_weight, down_weight):
    params = tuple((item.astype(jnp.float32) for item in (attn_gain, query_weight, key_weight, value_weight, out_weight, ffn_gain, gate_weight, up_weight, down_weight)))
    inputs = hidden_in.astype(jnp.float32).reshape(MB * BATCH, LEN, D)
    grads_in = cotangent.astype(jnp.float32).reshape(MB * BATCH, LEN, D)

    def one_sequence(totals, pair):
        sequence, grad_seq = pair
        result, pullback = jax.vjp(two_layers, sequence, params)
        grad_input, grad_params = pullback(grad_seq)
        totals = tuple((total_part + grad_part for total_part, grad_part in zip(totals, grad_params)))
        return (totals, (result, grad_input))
    zeros_init = tuple((jnp.zeros_like(item) for item in params))
    totals, outputs = lax.scan(one_sequence, zeros_init, (inputs, grads_in))
    results, grad_inputs = outputs
    return (results.reshape(MB, BATCH, LEN, D), grad_inputs.reshape(MB, BATCH, LEN, D), totals[0], totals[1], totals[2], totals[3], totals[4], totals[5], totals[6], totals[7], totals[8])
```

```python
import math

import jax
import jax.numpy as jnp
from jax import lax
from jax.experimental import pallas as pl
from jax.experimental.pallas import tpu as pltpu
from jax.sharding import PartitionSpec as P

HD = 64
LANES = 128
epsilon = 1e-05
masked_value = -1e30
bf16 = jnp.bfloat16
f32 = jnp.float32
MIB = 1 << 20


def rope_tables(positions):
    half_dim = HD // 2
    rates = jnp.exp(jnp.arange(half_dim, dtype=f32) * (-2.0 * math.log(10000.0) / HD))
    angles = positions.astype(f32)[:, None] * rates[None, :]
    repeat = LANES // half_dim
    return jnp.tile(jnp.cos(angles), (1, repeat)), jnp.tile(jnp.sin(angles), (1, repeat))


def turn(values, cosine, sine):
    lane = lax.broadcasted_iota(jnp.int32, values.shape, 1)
    first = (lane % HD) < HD // 2
    back = pltpu.roll(values, LANES - HD // 2, 1)
    ahead = pltpu.roll(values, HD // 2, 1)
    return values * cosine + jnp.where(first, -back, ahead) * sine


def qkv_kernel(act_ref, w_ref, cos_ref, sin_ref, q_ref, kv_ref):
    step = pl.program_id(0)
    width = w_ref.shape[2]
    prod = jnp.dot(act_ref[...], w_ref[0], preferred_element_type=f32)
    tiles = pl.num_programs(0) // 3

    def turned():
        return jnp.concatenate(
            [
                turn(prod[:, i : i + LANES], cos_ref[...], sin_ref[...]).astype(bf16)
                for i in range(0, width, LANES)
            ],
            1,
        )

    @pl.when(step < tiles)
    def _():
        q_ref[...] = turned()

    @pl.when((step >= tiles) & (step < 2 * tiles))
    def _():
        kv_ref[0] = turned()

    @pl.when(step >= 2 * tiles)
    def _():
        kv_ref[0] = prod.astype(bf16)


def project_qkv(act, w_attn, cosine, sine):
    rows, width = act.shape
    tile = 256 if width % 256 == 0 else width
    tiles = width // tile
    return pl.pallas_call(
        qkv_kernel,
        grid=(3 * tiles,),
        in_specs=[
            pl.BlockSpec((rows, width), lambda j: (0, 0)),
            pl.BlockSpec((1, width, tile), lambda j: (j // tiles, 0, j % tiles)),
            pl.BlockSpec((rows, LANES), lambda j: (0, 0)),
            pl.BlockSpec((rows, LANES), lambda j: (0, 0)),
        ],
        out_specs=[
            pl.BlockSpec((rows, tile), lambda j: (0, jnp.minimum(j, tiles - 1))),
            pl.BlockSpec(
                (1, rows, tile),
                lambda j: (
                    jnp.maximum(j - tiles, 0) // tiles,
                    0,
                    jnp.maximum(j - tiles, 0) % tiles,
                ),
            ),
        ],
        out_shape=[
            jax.ShapeDtypeStruct((rows, width), bf16),
            jax.ShapeDtypeStruct((2, rows, width), bf16),
        ],
        compiler_params=pltpu.CompilerParams(vmem_limit_bytes=24 * MIB),
        cost_estimate=pl.CostEstimate(
            flops=6 * rows * width * width, bytes_accessed=10 * width * width, transcendentals=0
        ),
    )(act, w_attn, cosine, sine)


def key_tiles(role, block_index, own, other):
    if role == 0:
        table = [(own, 0), (other, 0), (other, 1), (own, 1)]
    else:
        table = [(other, 0), (own, 0), (own, 1), (other, 1)]
    return table[: block_index + 1]


NT = (((1,), (1,)), ((), ()))
TN = (((0,), (0,)), ((), ()))


def attn_fwd_kernel(role_ref, q_ref, ko_ref, vo_ref, kt_ref, vt_ref, o_ref, lse_ref):
    rows = q_ref.shape[0] // 2
    own, other = (ko_ref, vo_ref), (kt_ref, vt_ref)

    def one(role, j):
        block_index = (role, 3 - role)[j]
        tiles = key_tiles(role, block_index, own, other)
        q = q_ref[j * rows : (j + 1) * rows, :] * jnp.asarray(HD**-0.5, bf16)
        lane = lax.broadcasted_iota(jnp.int32, q.shape, 1)
        key_id = lax.broadcasted_iota(jnp.int32, (rows, rows), 0)
        query_id = lax.broadcasted_iota(jnp.int32, (rows, rows), 1)
        outs = []
        for h in range(2):
            qm = jnp.where((lane >= HD) if h else (lane < HD), q, jnp.zeros_like(q))
            scores = []
            top = None
            for t, ((k_ref, _), i) in enumerate(tiles):
                k = k_ref[0, i * rows : (i + 1) * rows, :]
                s = lax.dot_general(k, qm, NT, preferred_element_type=f32)
                if t == block_index:
                    s = jnp.where(key_id <= query_id, s, masked_value)
                scores.append(s)
                tile_top = jnp.max(s, 0, keepdims=True)
                top = tile_top if top is None else jnp.maximum(top, tile_top)
            total = None
            mixed = None
            for s, ((_, v_ref), i) in zip(scores, tiles):
                p = jnp.exp(s - top)
                part = jnp.sum(p, 0, keepdims=True)
                total = part if total is None else total + part
                v = v_ref[0, i * rows : (i + 1) * rows, :]
                m = lax.dot_general(v, p.astype(bf16), TN, preferred_element_type=f32)
                mixed = m if mixed is None else mixed + m
            outs.append(mixed[h * HD : (h + 1) * HD, :] * (1.0 / total))
            lse_ref[0, h : h + 1, j * rows : (j + 1) * rows] = top + jnp.log(total)
        o_ref[j * rows : (j + 1) * rows, :] = jnp.concatenate(outs, 0).T.astype(bf16)

    for role in range(2):

        @pl.when(role_ref[0] == role)
        def _(role=role):
            for j in range(2):
                one(role, j)


def attn_forward(role, q, kv_own, kv_other):
    rows, width = q.shape
    pairs = width // LANES
    smem = pl.BlockSpec(memory_space=pltpu.SMEM)
    act = pl.BlockSpec((rows, LANES), lambda i: (0, i))

    def kv(which):
        return pl.BlockSpec((1, rows, LANES), lambda i: (which, 0, i))

    return pl.pallas_call(
        attn_fwd_kernel,
        grid=(pairs,),
        in_specs=[smem, act, kv(0), kv(1), kv(0), kv(1)],
        out_specs=[act, pl.BlockSpec((1, 2, rows), lambda i: (i, 0, 0))],
        out_shape=[
            jax.ShapeDtypeStruct((rows, width), bf16),
            jax.ShapeDtypeStruct((pairs, 2, rows), f32),
        ],
        compiler_params=pltpu.CompilerParams(vmem_limit_bytes=32 * MIB),
        cost_estimate=pl.CostEstimate(
            flops=16 * rows * rows * width, bytes_accessed=14 * rows * width, transcendentals=0
        ),
    )(role, q, kv_own, kv_own, kv_other, kv_other)


def attn_bwd_kernel(
    role_ref, q_ref, ko_ref, vo_ref, kt_ref, vt_ref, lse_ref, o_ref, do_ref,
    cos_ref, sin_ref, cost_ref, sint_ref, dq_ref, down_ref, doth_ref, acc_ref,
):
    rows = q_ref.shape[0] // 2
    own, other = (0, ko_ref, vo_ref), (1, kt_ref, vt_ref)

    def one(role, j, seen):
        block_index = (role, 3 - role)[j]
        tiles = key_tiles(role, block_index, own, other)
        here = slice(j * rows, (j + 1) * rows)
        q = q_ref[here, :] * jnp.asarray(HD**-0.5, bf16)
        do = do_ref[here, :]
        lane = lax.broadcasted_iota(jnp.int32, q.shape, 1)
        key_id = lax.broadcasted_iota(jnp.int32, (rows, rows), 0)
        query_id = lax.broadcasted_iota(jnp.int32, (rows, rows), 1)
        both = (do.astype(f32) * o_ref[here, :].astype(f32)).T
        dqs = [None, None]
        for h in range(2):
            mine = (lane >= HD) if h else (lane < HD)
            qm = jnp.where(mine, q, jnp.zeros_like(q))
            dom = jnp.where(mine, do, jnp.zeros_like(do))
            lse = lse_ref[0, h : h + 1, here]
            delta = jnp.sum(both[h * HD : (h + 1) * HD, :], 0, keepdims=True)
            for t, ((which, k_ref, v_ref), i) in enumerate(tiles):
                there = slice(i * rows, (i + 1) * rows)
                k, v = k_ref[0, there, :], v_ref[0, there, :]
                s = lax.dot_general(k, qm, NT, preferred_element_type=f32)
                p = jnp.exp(s - lse)
                if t == block_index:
                    p = jnp.where(key_id <= query_id, p, 0.0)
                dp = lax.dot_general(v, dom, NT, preferred_element_type=f32)
                ds = (p * (dp - delta)).astype(bf16)
                dv = jnp.dot(p.astype(bf16), dom, preferred_element_type=f32)
                dk = jnp.dot(ds, qm, preferred_element_type=f32)
                dq = lax.dot_general(k, ds, TN, preferred_element_type=f32)
                dqs[h] = dq if dqs[h] is None else dqs[h] + dq
                key = (which, i)
                if key in seen:
                    acc_ref[which, 0, there, :] += dk
                    acc_ref[which, 1, there, :] += dv
                else:
                    seen.add(key)
                    acc_ref[which, 0, there, :] = dk
                    acc_ref[which, 1, there, :] = dv
        grad = jnp.concatenate([dqs[0][:HD, :], dqs[1][HD:, :]], 0).T * (HD**-0.5)
        dq_ref[here, :] = turn(grad, cos_ref[here, :], -sin_ref[here, :]).astype(bf16)

    for role in range(2):

        @pl.when(role_ref[0] == role)
        def _(role=role):
            seen = set()
            for j in range(2):
                one(role, j, seen)
            for which in range(2):
                for i in range(2):
                    if (which, i) not in seen:
                        zeros = jnp.zeros((2, rows, LANES), f32)
                        acc_ref[which, :, i * rows : (i + 1) * rows, :] = zeros

    down_ref[0] = turn(acc_ref[0, 0], cos_ref[...], -sin_ref[...]).astype(bf16)
    down_ref[1] = acc_ref[0, 1].astype(bf16)
    doth_ref[0] = turn(acc_ref[1, 0], cost_ref[...], -sint_ref[...]).astype(bf16)
    doth_ref[1] = acc_ref[1, 1].astype(bf16)


def attn_backward(role, q, kv_own, kv_other, lse, o, do, tables, tables_other):
    rows, width = q.shape
    pairs = width // LANES
    smem = pl.BlockSpec(memory_space=pltpu.SMEM)
    act = pl.BlockSpec((rows, LANES), lambda i: (0, i))
    tab = pl.BlockSpec((rows, LANES), lambda i: (0, 0))
    two = pl.BlockSpec((2, rows, LANES), lambda i: (0, 0, i))

    def kv(which):
        return pl.BlockSpec((1, rows, LANES), lambda i: (which, 0, i))

    return pl.pallas_call(
        attn_bwd_kernel,
        grid=(pairs,),
        in_specs=[
            smem, act, kv(0), kv(1), kv(0), kv(1),
            pl.BlockSpec((1, 2, rows), lambda i: (i, 0, 0)), act, act, tab, tab, tab, tab,
        ],
        out_specs=[act, two, two],
        out_shape=[
            jax.ShapeDtypeStruct((rows, width), bf16),
            jax.ShapeDtypeStruct((2, rows, width), bf16),
            jax.ShapeDtypeStruct((2, rows, width), bf16),
        ],
        scratch_shapes=[pltpu.VMEM((2, 2, rows, LANES), f32)],
        compiler_params=pltpu.CompilerParams(vmem_limit_bytes=32 * MIB),
        cost_estimate=pl.CostEstimate(
            flops=40 * rows * rows * width, bytes_accessed=24 * rows * width, transcendentals=0
        ),
    )(role, q, kv_own, kv_own, kv_other, kv_other, lse, o, do, *tables, *tables_other)


def place_kernel(plan, piece_count, unit_ref, *refs):
    pieces, outs, sems = refs[:piece_count], refs[piece_count:-1], refs[-1]
    copies = []
    for a, piece in enumerate(pieces):
        for k in range(piece.shape[0]):
            unit = unit_ref[a * piece.shape[0] + k]
            for w, (out_index, slot, start, size) in enumerate(plan):
                row = pl.multiple_of(unit * size, 16)
                dst = outs[out_index]
                dst = dst.at[slot, pl.ds(row, size), :]
                copies.append(
                    pltpu.make_async_copy(
                        piece.at[k, start : start + size, :],
                        dst,
                        sems.at[a, k, w],
                    )
                )
    for copy in copies:
        copy.start()
    for copy in copies:
        copy.wait()


def place(plan, out_shapes, units, pieces):
    anyspace = pl.BlockSpec(memory_space=pl.ANY)
    size = sum(math.prod(s) for s in out_shapes)
    return pl.pallas_call(
        lambda *refs: place_kernel(plan, len(pieces), *refs),
        in_specs=[pl.BlockSpec(memory_space=pltpu.SMEM)] + [anyspace] * len(pieces),
        out_specs=[anyspace] * len(out_shapes),
        out_shape=[jax.ShapeDtypeStruct(s, bf16) for s in out_shapes],
        scratch_shapes=[
            pltpu.SemaphoreType.DMA((len(pieces), pieces[0].shape[0], len(plan)))
        ],
        cost_estimate=pl.CostEstimate(
            flops=0, bytes_accessed=4 * size, transcendentals=0
        ),
    )(units, *pieces)


class Places:
    def __init__(self):
        self.count = lax.axis_size("fsdp")
        self.seq = lax.axis_size("seq")
        self.f = lax.axis_index("fsdp")
        self.s = lax.axis_index("seq")
        self.far, self.near = self.f // 2, self.f % 2
        self.shifts = self.count // 2
        self.core = self.s % 2
        self.y = self.s // 2

    def over_far(self, value, k):
        pairs = [(i, (i + 2 * k) % self.count) for i in range(self.count)]
        return lax.ppermute(value, "fsdp", pairs)

    def over_near(self, value):
        return lax.ppermute(value, "fsdp", [(i, i ^ 1) for i in range(self.count)])

    def over_core(self, value):
        return lax.ppermute(value, "seq", [(i, i ^ 1) for i in range(self.seq)])

    def over_y(self, value):
        return lax.ppermute(value, "seq", [(i, i ^ 2) for i in range(self.seq)])

    def mirror(self, value):
        last = self.seq - 1
        return lax.ppermute(value, "seq", [(i, last - i) for i in range(self.seq)])


def after(value, *others):
    return lax.optimization_barrier((value,) + others)[0]


def pick(value, index, axis):
    return lax.dynamic_index_in_dim(value, index, axis, keepdims=False)


def gather_group(at, own, gate=None):
    if gate is not None:
        own = after(own, *gate)
    got = [own] + [at.over_far(own, k) for k in range(1, at.shifts)]
    here = jnp.stack(got)
    there = at.over_near(here)
    token = tuple(g[:8, :LANES] for g in got[1:])
    return [here, there, at.over_core(here), at.over_core(there)], token


def units_of(at):
    far = (at.far - jnp.arange(at.shifts, dtype=jnp.int32)) % at.shifts
    out = []
    for core in (at.core, 1 - at.core):
        for near in (at.near, 1 - at.near):
            out.append((far * 2 + near) * 2 + core)
    return jnp.concatenate(out).astype(jnp.int32)


def fetch_weights(at, attn, gains, gate_up, down):
    _, _, p, d = attn.shape
    ff = gate_up.shape[3]
    q = down.shape[1]
    if p % 32 or q % 32:

        def whole(value, axis):
            return lax.all_gather(value, "fsdp", axis=axis, tiled=True)

        attn, gate_up, down = whole(attn, 2), whole(gate_up, 2), whole(down, 1)
        gains = whole(gains, 1)
        return [(attn[l], gate_up[l], down[l]) for l in range(2)], gains
    ph, qh = p // 2, q // 2

    def half(value, axis):
        size = value.shape[axis] // 2
        return lax.dynamic_slice_in_dim(value, at.core * size, size, axis)

    attn_half = half(attn, 2)
    gu_half = half(gate_up, 2)
    down_half = half(down, 1)
    units = units_of(at)
    gain_rows = jnp.zeros((16, d), bf16).at[0, : 4 * p].set(gains.reshape(4 * p))
    first = jnp.concatenate([attn_half[0].reshape(4 * ph, d), gain_rows])
    g1, t1 = gather_group(at, first)
    g2, t2 = gather_group(at, gu_half[0].reshape(2 * ph, ff))
    third = jnp.concatenate([down_half[0], attn_half[1].reshape(4 * ph, d)])
    g3, t3 = gather_group(at, third, t1)
    g4, t4 = gather_group(at, gu_half[1].reshape(2 * ph, ff), t2)
    g5, _ = gather_group(at, down_half[1], t3)

    attn_plan = [(0, i, i * ph, ph) for i in range(4)]
    gu_plan = [(0, i, i * ph, ph) for i in range(2)]
    (attn0,) = place(attn_plan, [(4, d, d)], units, g1)
    (gu0,) = place(gu_plan, [(2, d, ff)], units, g2)
    plan3 = [(0, 0, 0, qh)] + [(1, i, qh + i * ph, ph) for i in range(4)]
    down0, attn1 = place(plan3, [(1, ff, d), (4, d, d)], units, g3)
    (gu1,) = place(gu_plan, [(2, d, ff)], units, g4)
    (down1,) = place([(0, 0, 0, qh)], [(1, ff, d)], units, g5)

    rows = jnp.concatenate([g1[0][:, 4 * ph, : 4 * p], g1[1][:, 4 * ph, : 4 * p]])
    shard = jnp.arange(at.count, dtype=jnp.int32)
    index = ((shard % 2) ^ at.near) * at.shifts + (at.far - shard // 2) % at.shifts
    select = jax.nn.one_hot(index, at.count, dtype=f32)
    gains_all = jnp.dot(select, rows.astype(f32), precision=lax.Precision.HIGHEST)
    gains_all = gains_all.reshape(at.count, 4, p).transpose(1, 0, 2).reshape(4, d)
    return [(attn0, gu0, down0[0]), (attn1, gu1, down1[0])], gains_all


def halves(at, grad, which):
    size = grad.shape[-1] // 2
    return lax.dynamic_slice_in_dim(grad, which * size, size, grad.ndim - 1)


def weight_grad(left, grad):
    return lax.dot_general(left, grad, TN, preferred_element_type=f32)


def reduce_group(at, pairs):
    rows = pairs[0][0].shape[1]
    cols = pairs[0][1].shape[1]
    if (rows // at.count) % 32:
        total = jnp.stack([weight_grad(a, g).astype(bf16) for a, g in pairs])
        total = lax.psum_scatter(total, "fsdp", scatter_dimension=1, tiled=True)
        return lax.psum(total, "seq").astype(f32)
    n = len(pairs)
    part = rows // at.count
    shape = (n, at.shifts, 2, part, cols // 2)
    theirs = jnp.stack(
        [weight_grad(a, halves(at, g, 1 - at.core)).astype(bf16) for a, g in pairs]
    )
    got = at.over_core(theirs)
    mine = jnp.stack(
        [
            (weight_grad(a, halves(at, g, at.core)) + got[i].astype(f32)).astype(bf16)
            for i, (a, g) in enumerate(pairs)
        ]
    ).reshape(shape)
    got = at.over_near(pick(mine, 1 - at.near, 2))
    keep = pick(mine, at.near, 2)

    def slot(k):
        index = (at.far + k) % at.shifts
        total = pick(keep, index, 1).astype(f32) + pick(got, index, 1).astype(f32)
        return total

    total = slot(0)
    for k in range(1, at.shifts):
        total = total + at.over_far(slot(k).astype(bf16), k).astype(f32)
    total = total.astype(bf16)
    total = total.astype(f32) + at.over_y(total).astype(f32)
    total = total.astype(bf16)
    other = at.over_core(total)
    return jnp.where(
        at.core == 0,
        jnp.concatenate([total, other], -1),
        jnp.concatenate([other, total], -1),
    ).astype(f32)


def reduce_gains(at, grads):
    d = grads.shape[1]
    part = d // at.count
    if part % 32:
        total = lax.psum_scatter(grads, "fsdp", scatter_dimension=1, tiled=True)
        return lax.psum(total, "seq")
    value = grads.reshape(4, at.shifts, 2, part).transpose(2, 1, 0, 3)
    value = value.reshape(2, at.shifts, 4 * part)
    value = value + at.over_core(value)
    keep = pick(value, at.near, 0) + at.over_near(pick(value, 1 - at.near, 0))
    parts = [pick(keep, (at.far + k) % at.shifts, 0)[None] for k in range(at.shifts)]
    total = parts[0]
    for k in range(1, at.shifts):
        total = total + at.over_far(parts[k], k)
    total = total + at.over_y(total)
    return total.reshape(4, part)


def normalize(values, gain):
    return values * lax.rsqrt(jnp.mean(values * values, -1, keepdims=True) + epsilon) * gain


def normalize_back(values, gain, grad):
    scale = lax.rsqrt(jnp.mean(values * values, -1, keepdims=True) + epsilon)
    unit = values * scale
    inner = grad * gain
    out = scale * (inner - unit * jnp.mean(inner * unit, -1, keepdims=True))
    return out, jnp.sum(grad * unit, 0)


def project(left, weight):
    return jnp.dot(left, weight, preferred_element_type=f32)


def project_back(grad, weight):
    return lax.dot_general(grad, weight, NT, preferred_element_type=f32)


def attend(at, act, w_attn, role, tables):
    q, kv = project_qkv(act, w_attn, *tables)
    kv_other = at.over_core(kv)
    o, lse = attn_forward(role, q, kv, kv_other)
    return project(o, w_attn[3]), (act, q, kv, kv_other, lse, o)


def attend_back(at, grad_low, state, w_attn, role, tables, tables_other):
    act, q, kv, kv_other, lse, o = state
    do = project_back(grad_low, w_attn[3]).astype(bf16)
    dq, dkv, dkv_other = attn_backward(
        role, q, kv, kv_other, lse, o, do, tables, tables_other
    )
    got = at.over_core(dkv_other)
    dkv = (dkv.astype(f32) + got.astype(f32)).astype(bf16)
    grad_in = (
        project_back(dq, w_attn[0])
        + project_back(dkv[0], w_attn[1])
        + project_back(dkv[1], w_attn[2])
    )
    return grad_in, [(act, dq), (act, dkv[0]), (act, dkv[1]), (o, grad_low)]


def feed(act, w_gu, w_down):
    gate = project(act, w_gu[0])
    up = project(act, w_gu[1])
    sig = jax.nn.sigmoid(gate)
    silu = gate * sig
    hidden = (silu * up).astype(bf16)
    slope = (up * sig * (1.0 + gate * (1.0 - sig))).astype(bf16)
    return project(hidden, w_down), (act, silu.astype(bf16), slope, hidden)


def feed_back(grad_low, state, w_gu, w_down):
    act, silu, slope, hidden = state
    grad_hidden = project_back(grad_low, w_down)
    grad_gate = (grad_hidden * slope.astype(f32)).astype(bf16)
    grad_up = (grad_hidden * silu.astype(f32)).astype(bf16)
    grad_in = project_back(grad_gate, w_gu[0]) + project_back(grad_up, w_gu[1])
    return grad_in, [(act, grad_gate), (act, grad_up)], [(hidden, grad_low)]


def per_device(
    hidden_in,
    cotangent,
    attn_gain,
    query_weight,
    key_weight,
    value_weight,
    out_weight,
    ffn_gain,
    gate_weight,
    up_weight,
    down_weight,
):
    at = Places()
    rows = hidden_in.shape[2]
    assert hidden_in.shape[0] == 2 and at.seq == 4

    low = jnp.minimum(at.s, 3 - at.s)
    role = low.astype(jnp.int32).reshape(1)
    first_is_own = at.s < 2

    def spread(value):
        own = pick(value[:, 0], at.y, 0)
        got = at.mirror(pick(value[:, 0], 1 - at.y, 0))
        return jnp.concatenate(
            [jnp.where(first_is_own, own, got), jnp.where(first_is_own, got, own)]
        )

    def collect(value):
        first, second = value[:rows], value[rows:]
        own = jnp.where(first_is_own, first, second)
        got = at.mirror(jnp.where(first_is_own, second, first).astype(bf16)).astype(f32)
        zero = at.y == 0
        return jnp.stack([jnp.where(zero, own, got), jnp.where(zero, got, own)])[:, None]

    def tables_of(first):
        steps = jnp.arange(rows, dtype=jnp.int32)
        return rope_tables(
            jnp.concatenate([first * rows + steps, (3 - first) * rows + steps])
        )

    tables, tables_other = tables_of(low), tables_of(1 - low)

    act = spread(hidden_in)
    weights, gains = fetch_weights(
        at,
        jnp.stack([query_weight, key_weight, value_weight, out_weight], 1),
        jnp.concatenate([attn_gain, ffn_gain]),
        jnp.stack([gate_weight, up_weight], 1),
        down_weight,
    )
    (attn0, gu0, down0), (attn1, gu1, down1) = weights
    gain_a0, gain_a1, gain_f0, gain_f1 = (gains[i].astype(f32) for i in range(4))
    cot = spread(cotangent)

    attended, attn_state0 = attend(at, act, attn0, role, tables)
    sum0 = act.astype(f32) + attended
    mid0 = normalize(sum0, gain_a0)
    fed, ffn_state0 = feed(mid0.astype(bf16), gu0, down0)
    sum1 = mid0 + fed
    z = normalize(sum1, gain_f0)
    attended, attn_state1 = attend(
        at, normalize(z, gain_a1).astype(bf16), attn1, role, tables
    )
    sum2 = z + attended
    fed, ffn_state1 = feed(normalize(sum2, gain_f1).astype(bf16), gu1, down1)
    layer_out = collect(sum2 + fed)

    grad = cot.astype(f32)
    grad_in, gu_pairs1, down_pairs1 = feed_back(cot, ffn_state1, gu1, down1)
    back, dgain_f1 = normalize_back(sum2, gain_f1, grad_in)
    grad = grad + back
    gu_grad1 = reduce_group(at, gu_pairs1)
    down_grad1 = reduce_group(at, down_pairs1)
    grad_in, attn_pairs1 = attend_back(
        at, grad.astype(bf16), attn_state1, attn1, role, tables, tables_other
    )
    back, dgain_a1 = normalize_back(z, gain_a1, grad_in)
    grad = grad + back
    attn_grad1 = reduce_group(at, attn_pairs1)
    grad, dgain_f0 = normalize_back(sum1, gain_f0, grad)
    grad_in, gu_pairs0, down_pairs0 = feed_back(grad.astype(bf16), ffn_state0, gu0, down0)
    gu_grad0 = reduce_group(at, gu_pairs0)
    down_grad0 = reduce_group(at, down_pairs0)
    grad, dgain_a0 = normalize_back(sum0, gain_a0, grad + grad_in)
    gain_grads = reduce_gains(at, jnp.stack([dgain_a0, dgain_a1, dgain_f0, dgain_f1]))
    grad_in, attn_pairs0 = attend_back(
        at, grad.astype(bf16), attn_state0, attn0, role, tables, tables_other
    )
    input_grad = collect(grad + grad_in)
    attn_grad0 = reduce_group(at, attn_pairs0)

    attn_grad = [jnp.stack([attn_grad0[i], attn_grad1[i]]) for i in range(4)]
    gu_grad = [jnp.stack([gu_grad0[i], gu_grad1[i]]) for i in range(2)]
    return (
        layer_out,
        input_grad,
        gain_grads[:2],
        attn_grad[0],
        attn_grad[1],
        attn_grad[2],
        attn_grad[3],
        gain_grads[2:],
        gu_grad[0],
        gu_grad[1],
        jnp.stack([down_grad0[0], down_grad1[0]]),
    )


def solution(mesh):
    tokens = P(None, "fsdp", "seq", None)
    gain = P(None, "fsdp")
    weight = P(None, "fsdp", None)
    return jax.shard_map(
        per_device,
        mesh=mesh,
        in_specs=(tokens, tokens, gain) + (weight,) * 4 + (gain,) + (weight,) * 3,
        out_specs=(tokens, tokens, gain) + (weight,) * 4 + (gain,) + (weight,) * 3,
        check_vma=False,
    )
```

```python
import math

import jax
import jax.numpy as jnp
from jax import lax
from jax.experimental import pallas as pl
from jax.experimental.pallas import tpu as pltpu
from jax.sharding import PartitionSpec as P

HD = 64
LANES = 128
epsilon = 1e-05
masked_value = -1e30
bf16 = jnp.bfloat16
f32 = jnp.float32
MIB = 1 << 20
CHUNK = 256
FREE = pl.CostEstimate(flops=1, bytes_accessed=1, transcendentals=0)
NT = (((1,), (1,)), ((), ()))
TN = (((0,), (0,)), ((), ()))


def rope_tables(positions):
    half_dim = HD // 2
    rates = jnp.exp(jnp.arange(half_dim, dtype=f32) * (-2.0 * math.log(10000.0) / HD))
    angles = positions.astype(f32)[:, None] * rates[None, :]
    repeat = LANES // half_dim
    return jnp.tile(jnp.cos(angles), (1, repeat)), jnp.tile(jnp.sin(angles), (1, repeat))


def turn(values, cosine, sine):
    lane = lax.broadcasted_iota(jnp.int32, values.shape, 1)
    first = (lane % HD) < HD // 2
    back = pltpu.roll(values, LANES - HD // 2, 1)
    ahead = pltpu.roll(values, HD // 2, 1)
    return values * cosine + jnp.where(first, -back, ahead) * sine


def in_vmem(kernel, outs, operands, scalars=(), scratch=(), limit=6):
    smem = [pl.BlockSpec(memory_space=pltpu.SMEM)] * len(scalars)
    vmem = pl.BlockSpec(memory_space=pltpu.VMEM)
    moved = sum(v.size * v.dtype.itemsize for v in operands)
    moved += sum(math.prod(shape) * jnp.dtype(dtype).itemsize for shape, dtype in outs)
    room = limit * MIB + moved
    return pl.pallas_call(
        kernel,
        in_specs=smem + [vmem] * len(operands),
        out_specs=[vmem] * len(outs),
        out_shape=[jax.ShapeDtypeStruct(shape, dtype) for shape, dtype in outs],
        scratch_shapes=list(scratch),
        compiler_params=pltpu.CompilerParams(vmem_limit_bytes=room),
        cost_estimate=FREE,
    )(*scalars, *operands)


def chunks(size, step=CHUNK):
    return [slice(i, min(i + step, size)) for i in range(0, size, step)]


def root(values):
    return lax.rsqrt(jnp.mean(values * values, -1, keepdims=True) + epsilon)


def norm_back(values, gain, grad):
    scale = root(values)
    unit = values * scale
    inner = grad * gain
    out = scale * (inner - unit * jnp.mean(inner * unit, -1, keepdims=True))
    return out, jnp.sum(grad * unit, 0, keepdims=True)


def dot(left, right):
    return jnp.dot(left, right, preferred_element_type=f32)


def dot_nt(left, right):
    return lax.dot_general(left, right, NT, preferred_element_type=f32)


def dot_tn(left, right):
    return lax.dot_general(left, right, TN, preferred_element_type=f32)


def qkv_kernel(act_ref, w_ref, cos_ref, sin_ref, q_ref, kv_ref):
    act = act_ref[...]
    for i in range(3):
        for cols in chunks(act.shape[1]):
            prod = dot(act, w_ref[i, :, cols])
            for at in range(cols.start, cols.stop, LANES):
                part = prod[:, at - cols.start : at - cols.start + LANES]
                if i < 2:
                    part = turn(part, cos_ref[...], sin_ref[...])
                part = part.astype(bf16)
                if i == 0:
                    q_ref[:, at : at + LANES] = part
                else:
                    kv_ref[i - 1, :, at : at + LANES] = part


def project_qkv(act, w_qkv, tables):
    rows, width = act.shape
    outs = [((rows, width), bf16), ((2, rows, width), bf16)]
    return in_vmem(qkv_kernel, outs, (act, w_qkv, *tables))


def out_kernel(which, o_ref, w_ref, resid_ref, gain_ref, sum_ref, act_ref):
    o = o_ref[...]
    for cols in chunks(o.shape[1]):
        sum_ref[:, cols] = resid_ref[:, cols].astype(f32) + dot(o, w_ref[:, cols])
    total = sum_ref[...]
    act_ref[...] = (total * root(total) * gain_ref[which : which + 1, :]).astype(bf16)


def project_out(which, o, w_out, resid, gains):
    shape = o.shape
    return in_vmem(
        lambda *refs: out_kernel(which, *refs),
        [(shape, f32), (shape, bf16)],
        (o, w_out, resid, gains),
    )


def ffn_in_kernel(act_ref, w_ref, hidden_ref, silu_ref, slope_ref):
    act = act_ref[...]
    for cols in chunks(hidden_ref.shape[1]):
        gate = dot(act, w_ref[0, :, cols])
        up = dot(act, w_ref[1, :, cols])
        sig = jax.nn.sigmoid(gate)
        silu = gate * sig
        hidden_ref[:, cols] = (silu * up).astype(bf16)
        silu_ref[:, cols] = silu.astype(bf16)
        slope_ref[:, cols] = (up * sig * (1.0 + gate * (1.0 - sig))).astype(bf16)


def ffn_in(act, w_gu):
    shape = (act.shape[0], w_gu.shape[2])
    return in_vmem(ffn_in_kernel, [(shape, bf16)] * 3, (act, w_gu))


def ffn_out_first_kernel(hid_ref, w_ref, sum_ref, gain_ref, next_ref, z_ref, act_ref):
    total = sum_ref[...]
    next_ref[...] = total * root(total) * gain_ref[0:1, :]
    hid = hid_ref[...]
    for cols in chunks(w_ref.shape[1]):
        next_ref[:, cols] += dot(hid, w_ref[:, cols])
    total = next_ref[...]
    z = total * root(total) * gain_ref[2:3, :]
    z_ref[...] = z
    act_ref[...] = (z * root(z) * gain_ref[1:2, :]).astype(bf16)


def ffn_out_first(hidden, w_down, total, gains):
    shape = total.shape
    return in_vmem(
        ffn_out_first_kernel,
        [(shape, f32), (shape, f32), (shape, bf16)],
        (hidden, w_down, total, gains),
    )


def split_rows(start_ref, value_ref, own_ref, send_ref):
    rows = own_ref.shape[0]
    own = pl.multiple_of(start_ref[0], rows)
    send = pl.multiple_of(rows - start_ref[0], rows)
    own_ref[...] = value_ref[pl.ds(own, rows), :]
    send_ref[...] = value_ref[pl.ds(send, rows), :].astype(bf16)


def ffn_out_second_kernel(start_ref, hid_ref, w_ref, sum_ref, own_ref, send_ref, total):
    hid = hid_ref[...]
    for cols in chunks(w_ref.shape[1]):
        total[:, cols] = sum_ref[:, cols] + dot(hid, w_ref[:, cols])
    split_rows(start_ref, total, own_ref, send_ref)


def ffn_out_second(start, hidden, w_down, total):
    rows, width = total.shape
    half = (rows // 2, width)
    return in_vmem(
        ffn_out_second_kernel,
        [(half, f32), (half, bf16)],
        (hidden, w_down, total),
        (start,),
        [pltpu.VMEM(total.shape, f32)],
    )


def ffn_back_kernel(
    post, grad_ref, silu_ref, slope_ref, wd_ref, wgu_ref, wo_ref, sum_ref, gain_ref,
    dgu_ref, total_ref, low_ref, do_ref, dgain_ref,
):
    grad_low = grad_ref[...].astype(bf16)
    for cols in chunks(wd_ref.shape[0]):
        hid = dot_nt(grad_low, wd_ref[cols, :])
        dgu_ref[0, :, cols] = (hid * slope_ref[:, cols].astype(f32)).astype(bf16)
        dgu_ref[1, :, cols] = (hid * silu_ref[:, cols].astype(f32)).astype(bf16)
    for cols in chunks(total_ref.shape[1]):
        back = dot_nt(dgu_ref[0], wgu_ref[0, cols, :])
        back += dot_nt(dgu_ref[1], wgu_ref[1, cols, :])
        total_ref[:, cols] = back
    if post:
        out, dgain = norm_back(
            sum_ref[...], gain_ref[0:1, :], grad_ref[...] + total_ref[...]
        )
    else:
        out, dgain = norm_back(sum_ref[...], gain_ref[3:4, :], total_ref[...])
        out = grad_ref[...].astype(f32) + out
    dgain_ref[...] = dgain
    total_ref[...] = out
    low_ref[...] = out.astype(bf16)
    low = low_ref[...]
    for cols in chunks(total_ref.shape[1]):
        do_ref[:, cols] = dot_nt(low, wo_ref[cols, :]).astype(bf16)


def ffn_back(post, grad, silu, slope, w_down, w_gu, w_out, total, gains):
    shape = total.shape
    outs = [
        ((2,) + silu.shape, bf16), (shape, f32), (shape, bf16), (shape, bf16),
        ((1, shape[1]), f32),
    ]
    return in_vmem(
        lambda *refs: ffn_back_kernel(post, *refs),
        outs,
        (grad, silu, slope, w_down, w_gu, w_out, total, gains),
    )


def join_kernel(a_ref, b_ref, out_ref):
    out_ref[...] = (a_ref[...].astype(f32) + b_ref[...].astype(f32)).astype(bf16)


def join(a, b):
    return in_vmem(join_kernel, [(a.shape, bf16)], (a, b))[0]


def join_parts_kernel(a_ref, dk_ref, dv_ref, cos_ref, sin_ref, out_ref):
    for at in range(0, a_ref.shape[2], LANES):
        cols = slice(at, at + LANES)
        total = a_ref[0, :, cols].astype(f32) + dk_ref[:, cols].astype(f32)
        out_ref[0, :, cols] = turn(total, cos_ref[...], -sin_ref[...]).astype(bf16)
    out_ref[1] = (a_ref[1].astype(f32) + dv_ref[...].astype(f32)).astype(bf16)


def join_parts(a, *rest):
    return in_vmem(join_parts_kernel, [(a.shape, bf16)], (a, *rest))[0]


def in_parts(send, values):
    return [send(v) for v in values]


def qkv_back_product(dq_ref, dkv_ref, w_ref, out_ref, base_ref):
    dq, dk, dv = dq_ref[...], dkv_ref[0], dkv_ref[1]
    for cols in chunks(out_ref.shape[1]):
        back = dot_nt(dq, w_ref[0, cols, :])
        back += dot_nt(dk, w_ref[1, cols, :])
        back += dot_nt(dv, w_ref[2, cols, :])
        if base_ref is not None:
            back += base_ref[:, cols]
        out_ref[:, cols] = back


def qkv_back_second_kernel(
    dq_ref, dkv_ref, w_ref, grad_ref, z_ref, sum_ref, gain_ref,
    out_ref, low_ref, dgain_ref,
):
    qkv_back_product(dq_ref, dkv_ref, w_ref, out_ref, None)
    back, dgain = norm_back(z_ref[...], gain_ref[1:2, :], out_ref[...])
    dgain_ref[0:1, :] = dgain
    out, dgain = norm_back(sum_ref[...], gain_ref[2:3, :], grad_ref[...] + back)
    dgain_ref[1:2, :] = dgain
    out_ref[...] = out
    low_ref[...] = out.astype(bf16)


def qkv_back_second(dq, dkv, w_qkv, grad, z, total, gains):
    shape = grad.shape
    return in_vmem(
        qkv_back_second_kernel,
        [(shape, f32), (shape, bf16), ((2, shape[1]), f32)],
        (dq, dkv, w_qkv, grad, z, total, gains),
    )


def qkv_back_first_kernel(
    start_ref, dq_ref, dkv_ref, w_ref, grad_ref, own_ref, send_ref, total
):
    qkv_back_product(dq_ref, dkv_ref, w_ref, total, grad_ref)
    split_rows(start_ref, total, own_ref, send_ref)


def qkv_back_first(start, dq, dkv, w_qkv, grad):
    rows, width = grad.shape
    half = (rows // 2, width)
    return in_vmem(
        qkv_back_first_kernel,
        [(half, f32), (half, bf16)],
        (dq, dkv, w_qkv, grad),
        (start,),
        [pltpu.VMEM(grad.shape, f32)],
    )


def merge_kernel(y_ref, own_ref, got_ref, out_ref):
    out_ref[y_ref[0], 0] = own_ref[...]
    out_ref[1 - y_ref[0], 0] = got_ref[...].astype(f32)


def merge(y, own, got):
    return in_vmem(merge_kernel, [((2, 1) + own.shape, f32)], (own, got), (y,))[0]


def key_tiles(role, block_index, own, other):
    if role == 0:
        table = [(own, 0), (other, 0), (other, 1), (own, 1)]
    else:
        table = [(other, 0), (own, 0), (own, 1), (other, 1)]
    return table[: block_index + 1]


def attn_fwd_kernel(role_ref, q_ref, ko_ref, vo_ref, kt_ref, vt_ref, o_ref, lse_ref):
    rows = q_ref.shape[0] // 2
    own, other = (ko_ref, vo_ref), (kt_ref, vt_ref)

    def one(role, j):
        block_index = (role, 3 - role)[j]
        tiles = key_tiles(role, block_index, own, other)
        q = q_ref[j * rows : (j + 1) * rows, :] * jnp.asarray(HD**-0.5, bf16)
        lane = lax.broadcasted_iota(jnp.int32, q.shape, 1)
        key_id = lax.broadcasted_iota(jnp.int32, (rows, rows), 0)
        query_id = lax.broadcasted_iota(jnp.int32, (rows, rows), 1)
        outs = []
        for h in range(2):
            qm = jnp.where((lane >= HD) if h else (lane < HD), q, jnp.zeros_like(q))
            scores = []
            top = None
            for t, ((k_ref, _), i) in enumerate(tiles):
                k = k_ref[0, i * rows : (i + 1) * rows, :]
                s = lax.dot_general(k, qm, NT, preferred_element_type=f32)
                if t == block_index:
                    s = jnp.where(key_id <= query_id, s, masked_value)
                scores.append(s)
                tile_top = jnp.max(s, 0, keepdims=True)
                top = tile_top if top is None else jnp.maximum(top, tile_top)
            total = None
            mixed = None
            for s, ((_, v_ref), i) in zip(scores, tiles):
                p = jnp.exp(s - top)
                part = jnp.sum(p, 0, keepdims=True)
                total = part if total is None else total + part
                v = v_ref[0, i * rows : (i + 1) * rows, :]
                m = lax.dot_general(v, p.astype(bf16), TN, preferred_element_type=f32)
                mixed = m if mixed is None else mixed + m
            outs.append(mixed[h * HD : (h + 1) * HD, :] * (1.0 / total))
            lse_ref[0, h : h + 1, j * rows : (j + 1) * rows] = top + jnp.log(total)
        o_ref[j * rows : (j + 1) * rows, :] = jnp.concatenate(outs, 0).T.astype(bf16)

    for role in range(2):

        @pl.when(role_ref[0] == role)
        def _(role=role):
            for j in range(2):
                one(role, j)


def attn_forward(role, q, kv_own, kv_other):
    rows, width = q.shape
    pairs = width // LANES
    smem = pl.BlockSpec(memory_space=pltpu.SMEM)
    act = pl.BlockSpec((rows, LANES), lambda i: (0, i))

    def kv(which):
        return pl.BlockSpec((1, rows, LANES), lambda i: (which, 0, i))

    return pl.pallas_call(
        attn_fwd_kernel,
        grid=(pairs,),
        in_specs=[smem, act, kv(0), kv(1), kv(0), kv(1)],
        out_specs=[act, pl.BlockSpec((1, 2, rows), lambda i: (i, 0, 0))],
        out_shape=[
            jax.ShapeDtypeStruct((rows, width), bf16),
            jax.ShapeDtypeStruct((pairs, 2, rows), f32),
        ],
        compiler_params=pltpu.CompilerParams(vmem_limit_bytes=12 * MIB),
        cost_estimate=FREE,
    )(role, q, kv_own, kv_own, kv_other, kv_other)


def attn_bwd_kernel(
    role_ref, q_ref, ko_ref, vo_ref, kt_ref, vt_ref, lse_ref, o_ref, do_ref,
    cos_ref, sin_ref, dq_ref, down_ref, *rest
):
    *other_refs, acc_ref = rest
    rows = q_ref.shape[0] // 2
    own, other = (0, ko_ref, vo_ref), (1, kt_ref, vt_ref)

    def one(role, j, seen):
        block_index = (role, 3 - role)[j]
        tiles = key_tiles(role, block_index, own, other)
        here = slice(j * rows, (j + 1) * rows)
        q = q_ref[here, :] * jnp.asarray(HD**-0.5, bf16)
        do = do_ref[here, :]
        lane = lax.broadcasted_iota(jnp.int32, q.shape, 1)
        key_id = lax.broadcasted_iota(jnp.int32, (rows, rows), 0)
        query_id = lax.broadcasted_iota(jnp.int32, (rows, rows), 1)
        both = (do.astype(f32) * o_ref[here, :].astype(f32)).T
        dqs = [None, None]
        for h in range(2):
            mine = (lane >= HD) if h else (lane < HD)
            qm = jnp.where(mine, q, jnp.zeros_like(q))
            dom = jnp.where(mine, do, jnp.zeros_like(do))
            lse = lse_ref[0, h : h + 1, here]
            delta = jnp.sum(both[h * HD : (h + 1) * HD, :], 0, keepdims=True)
            for t, ((which, k_ref, v_ref), i) in enumerate(tiles):
                there = slice(i * rows, (i + 1) * rows)
                k, v = k_ref[0, there, :], v_ref[0, there, :]
                s = lax.dot_general(k, qm, NT, preferred_element_type=f32)
                p = jnp.exp(s - lse)
                if t == block_index:
                    p = jnp.where(key_id <= query_id, p, 0.0)
                dp = lax.dot_general(v, dom, NT, preferred_element_type=f32)
                ds = (p * (dp - delta)).astype(bf16)
                dv = jnp.dot(p.astype(bf16), dom, preferred_element_type=f32)
                dk = jnp.dot(ds, qm, preferred_element_type=f32)
                dq = lax.dot_general(k, ds, TN, preferred_element_type=f32)
                dqs[h] = dq if dqs[h] is None else dqs[h] + dq
                key = (which, i)
                if key in seen:
                    acc_ref[which, 0, there, :] += dk
                    acc_ref[which, 1, there, :] += dv
                else:
                    seen.add(key)
                    acc_ref[which, 0, there, :] = dk
                    acc_ref[which, 1, there, :] = dv
        grad = jnp.concatenate([dqs[0][:HD, :], dqs[1][HD:, :]], 0).T * (HD**-0.5)
        dq_ref[here, :] = turn(grad, cos_ref[here, :], -sin_ref[here, :]).astype(bf16)

    for role in range(2):

        @pl.when(role_ref[0] == role)
        def _(role=role):
            seen = set()
            for j in range(2):
                one(role, j, seen)
            for which in range(2):
                for i in range(2):
                    if (which, i) not in seen:
                        zeros = jnp.zeros((2, rows, LANES), f32)
                        acc_ref[which, :, i * rows : (i + 1) * rows, :] = zeros

    down_ref[...] = acc_ref[0].astype(bf16)
    for i, ref in enumerate(other_refs):
        ref[...] = acc_ref[1, i].astype(bf16)


def attn_backward(role, q, kv_own, kv_other, lse, o, do, tables):
    rows, width = q.shape
    pairs = width // LANES
    smem = pl.BlockSpec(memory_space=pltpu.SMEM)
    act = pl.BlockSpec((rows, LANES), lambda i: (0, i))
    tab = pl.BlockSpec((rows, LANES), lambda i: (0, 0))
    two = pl.BlockSpec((2, rows, LANES), lambda i: (0, 0, i))

    def kv(which):
        return pl.BlockSpec((1, rows, LANES), lambda i: (which, 0, i))

    return pl.pallas_call(
        attn_bwd_kernel,
        grid=(pairs,),
        in_specs=[
            smem, act, kv(0), kv(1), kv(0), kv(1),
            pl.BlockSpec((1, 2, rows), lambda i: (i, 0, 0)), act, act, tab, tab,
        ],
        out_specs=[act, two, act, act],
        out_shape=[
            jax.ShapeDtypeStruct((rows, width), bf16),
            jax.ShapeDtypeStruct((2, rows, width), bf16),
        ]
        + [jax.ShapeDtypeStruct((rows, width), bf16)] * 2,
        scratch_shapes=[pltpu.VMEM((2, 2, rows, LANES), f32)],
        compiler_params=pltpu.CompilerParams(vmem_limit_bytes=12 * MIB),
        cost_estimate=FREE,
    )(role, q, kv_own, kv_own, kv_other, kv_other, lse, o, do, *tables)


class Places:
    def __init__(self):
        self.count = lax.axis_size("fsdp")
        self.seq = lax.axis_size("seq")
        self.f = lax.axis_index("fsdp")
        self.s = lax.axis_index("seq")
        self.far, self.near = self.f // 2, self.f % 2
        self.shifts = self.count // 2
        self.core = self.s % 2
        self.y = self.s // 2

    def over_far(self, value):
        groups = [list(range(i, self.count, 2)) for i in range(2)]
        return lax.all_to_all(value, "fsdp", 0, 0, axis_index_groups=groups, tiled=True)

    def over_near(self, value):
        return lax.ppermute(value, "fsdp", [(i, i ^ 1) for i in range(self.count)])

    def over_core(self, value):
        return lax.ppermute(value, "seq", [(i, i ^ 1) for i in range(self.seq)])

    def over_y(self, value):
        return lax.ppermute(value, "seq", [(i, i ^ 2) for i in range(self.seq)])

    def mirror(self, value):
        last = self.seq - 1
        return lax.ppermute(value, "seq", [(i, last - i) for i in range(self.seq)])


def after(value, *others):
    return lax.optimization_barrier((value,) + others)[0]


def pick(value, index, axis):
    return lax.dynamic_index_in_dim(value, index, axis, keepdims=False)


def place_kernel(plans, unit_ref, slot_ref, *refs):
    count = len(plans)
    pieces, outs = refs[:count], refs[count:]
    for a, (piece, plan) in enumerate(zip(pieces, plans)):
        for k in range(piece.shape[0]):
            unit = unit_ref[a * piece.shape[0] + k]
            for out_index, slot, start, size, by_rows in plan:
                number = unit * 2 + slot_ref[a] if by_rows else unit
                row = pl.multiple_of(number * size, 16)
                if isinstance(slot, tuple):
                    slot = slot_ref[a] * slot[0] + slot[1]
                outs[out_index][slot, pl.ds(row, size), :] = piece[k, start : start + size, :]


def place(order, out_shapes, *groups):
    plans, pieces, units, slots = [], [], [], []
    for gather, plan in groups:
        for value, unit, slot in gather.pieces():
            plans.append(plan)
            pieces.append(value)
            units.append(unit)
            slots.append(slot)
    units = jnp.concatenate(units).astype(jnp.int32)
    slots = jnp.stack(slots).astype(jnp.int32)

    def call(*values):
        return in_vmem(
            lambda *refs: place_kernel(plans, *refs),
            [(shape, bf16) for shape in out_shapes],
            values,
            (units, slots),
        )

    return order(call, *pieces)


class Order:
    def __init__(self):
        self.last = ()

    def wait(self, *values):
        self.last = self.last + values

    def __call__(self, function, *operands):
        if self.last:
            operands = (after(operands[0], *self.last),) + operands[1:]
        out = function(*operands)
        self.last = (out[0] if isinstance(out, (tuple, list)) else out,)
        return out


class Gather:
    def __init__(self, at, order, own, by_y=False):
        self.at, self.order, self.own, self.by_y = at, order, own, by_y

    def far(self):
        own = after(self.own, *self.order.last) if self.order.last else self.own
        self.here = self.at.over_far(jnp.broadcast_to(own[None], (self.at.shifts,) + own.shape))

    def arrived(self, value):
        value = after(value, *self.order.last)
        self.order.wait(value)
        return value

    def near(self):
        self.here = self.arrived(self.here)
        self.there = self.at.over_near(self.here)
        if self.by_y:
            self.here_y = self.at.over_y(self.here)
        self.here_core = self.at.over_core(self.here)

    def middle(self):
        self.there = self.arrived(self.there)
        self.there_y = self.at.over_y(self.there)
        self.there_core = self.at.over_core(self.there)
        self.here_y = self.arrived(self.here_y)
        self.here_y_core = self.at.over_core(self.here_y)

    def cores(self):
        if self.by_y:
            self.there_y = self.arrived(self.there_y)
            self.there_y_core = self.at.over_core(self.there_y)
        else:
            self.there = self.arrived(self.there)
            self.there_core = self.at.over_core(self.there)

    def pieces(self):
        at = self.at
        far = jnp.arange(at.shifts, dtype=jnp.int32)
        values = [(self.here, self.there, self.here_core, self.there_core)]
        if self.by_y:
            more = (self.here_y, self.there_y, self.here_y_core, self.there_y_core)
            values.append(more)
        for side, four in enumerate(values):
            for i, value in enumerate(four):
                near, core = at.near ^ (i % 2), at.core ^ (i // 2)
                yield value, (far * 2 + near) * 2 + core, at.y ^ side


class GatherWhole(Gather):
    def far(self):
        rows = self.own.shape[0]
        own = after(self.own, *self.order.last)
        here = lax.all_gather(own, "fsdp", axis=0, tiled=True)
        self.here = here.reshape(self.at.count, rows, here.shape[1])

    def near(self):
        self.here = self.arrived(self.here)
        if self.by_y:
            self.here_y = self.at.over_y(self.here)
        self.here_core = self.at.over_core(self.here)

    def cores(self):
        if self.by_y:
            self.here_y = self.arrived(self.here_y)
            self.here_y_core = self.at.over_core(self.here_y)
        else:
            self.here_core = self.arrived(self.here_core)

    def pieces(self):
        at = self.at
        shard = jnp.arange(at.count, dtype=jnp.int32)
        yield self.here, shard * 2 + at.core, at.y
        yield self.here_core, shard * 2 + 1 - at.core, at.y
        if not self.by_y:
            return
        yield self.here_y, shard * 2 + at.core, 1 - at.y
        yield self.here_y_core, shard * 2 + 1 - at.core, 1 - at.y


class Group:
    def __init__(self, weights, count, extra=0, apart=False):
        self.weights, self.count, self.extra, self.apart = weights, count, extra, apart
        self.cols = [n // 2 for *_, n in weights]
        self.tiles = [c // LANES for c in self.cols]
        self.parts = [w[3] // count for w in weights]
        self.bases, self.offsets = [], []
        base = offset = 0
        for w, tiles, part in zip(weights, self.tiles, self.parts):
            self.bases.append(base)
            self.offsets.append(offset)
            base += w[3] * tiles
            offset += part * tiles
        self.extra_base, self.extra_offset = base, offset
        self.total, self.rows = base + extra * count, offset + extra

    def halves(self):
        if self.apart:
            return [(w[3] * t, LANES) for w, t in zip(self.weights, self.tiles)]
        return [(self.total, LANES)]

    def tile(self, refs, i, tile):
        rows = self.weights[i][3]
        if self.apart:
            return refs[i].at[tile * rows : (tile + 1) * rows, :]
        start = self.bases[i] + tile * rows
        return refs[0].at[start : start + rows, :]

    def products(self, half, lefts, rights):
        for i, (a, g, slot, _, _) in enumerate(self.weights):
            left = lefts[a][...]
            right = rights[g] if slot is None else rights[g].at[slot]
            step = 256 if self.cols[i] % 256 == 0 else self.cols[i]
            for start in range(0, self.cols[i], step):
                col = pl.multiple_of(half * self.cols[i] + start, LANES)
                yield i, start // LANES, dot_tn(left, right[:, pl.ds(col, step)])


def theirs_kernel(group, n_left, n_right, place_ref, *refs):
    lefts, rights = refs[:n_left], refs[n_left : n_left + n_right]
    rest = refs[n_left + n_right :]
    outs = rest[1:] if group.extra else rest
    for i, tile, value in group.products(1 - place_ref[0], lefts, rights):
        for j in range(value.shape[1] // LANES):
            group.tile(outs, i, tile + j)[...] = value[:, j * LANES : (j + 1) * LANES].astype(
                bf16
            )
    if group.extra:
        outs[-1][group.extra_base :, :] = rest[0][...].astype(bf16)


def mine_kernel(group, by_y, n_left, n_right, place_ref, *refs):
    lefts, rights = refs[:n_left], refs[n_left : n_left + n_right]
    rest = refs[n_left + n_right :]
    keep_ref, send_ref, scratch = rest[-3:]
    gots = rest[1:-3] if group.extra else rest[:-3]
    side = place_ref[3] if by_y else place_ref[1]

    def hand_out(size, cols, offset):
        half = size // 2 if by_y else size
        first = offset // 2 if by_y else offset
        for index in range(keep_ref.shape[0]):
            for ref, own in ((keep_ref, side), (send_ref, 1 - side)):
                row = pl.multiple_of((index * 2 + own) * half, 8)
                for j in range(cols // LANES):
                    ref[index, first + j * half : first + (j + 1) * half, :] = scratch[
                        pl.ds(row, half), j * LANES : (j + 1) * LANES
                    ].astype(bf16)

    for i, tile, value in group.products(place_ref[0], lefts, rights):
        rows, cols = value.shape
        for j in range(cols // LANES):
            got = group.tile(gots, i, tile + j)[...].astype(f32)
            cut = slice(j * LANES, (j + 1) * LANES)
            scratch[:rows, cut] = value[:, cut] + got
        part = group.parts[i]
        hand_out(part, cols, group.offsets[i] + tile * part)
    if group.extra:
        rows = group.extra * group.count
        got = gots[0][group.extra_base :, :].astype(f32)
        scratch[:rows, :LANES] = rest[0][...].astype(f32) + got
        hand_out(group.extra, LANES, group.extra_offset)


def mine_all_kernel(group, n_left, n_right, place_ref, *refs):
    lefts, rights = refs[:n_left], refs[n_left : n_left + n_right]
    gots, out_ref = refs[n_left + n_right : -1], refs[-1]
    for i, tile, value in group.products(place_ref[0], lefts, rights):
        part = group.parts[i]
        for j in range(value.shape[1] // LANES):
            got = group.tile(gots, i, tile + j)[...].astype(f32)
            total = value[:, j * LANES : (j + 1) * LANES] + got
            first = group.offsets[i] + (tile + j) * part
            for shard in range(group.count):
                out_ref[shard, first : first + part, :] = total[
                    shard * part : (shard + 1) * part, :
                ].astype(bf16)


def split_near_kernel(place_ref, keep_ref, got_ref, stay_ref, leave_ref):
    near = place_ref[1]
    for far in range(stay_ref.shape[0]):
        for ref, side in ((stay_ref, near), (leave_ref, 1 - near)):
            shard = 2 * far + side
            ref[far] = (keep_ref[shard].astype(f32) + got_ref[shard].astype(f32)).astype(bf16)


def sum_kernel(parts_ref, out_ref):
    total = parts_ref[0].astype(f32)
    for k in range(1, parts_ref.shape[0]):
        total = total + parts_ref[k].astype(f32)
    out_ref[...] = total.astype(bf16)


class Reduce:
    def __init__(self, at, order, group, by_y, whole, lefts, rights, extra=()):
        self.at, self.order, self.group = at, order, group
        self.by_y, self.whole = by_y, whole
        self.operands = (*lefts, *rights, *extra)
        self.counts = (len(lefts), len(rights))

    def theirs(self):
        group = self.group

        def call(*operands):
            return in_vmem(
                lambda *refs: theirs_kernel(group, *self.counts, *refs),
                [(shape, bf16) for shape in group.halves()],
                operands,
                (self.at.scalars,),
            )

        self.got = in_parts(self.at.over_core, self.order(call, *self.operands))

    def mine(self):
        group, at = self.group, self.at
        shape = (at.count, group.rows // 2) if self.by_y else (at.shifts, group.rows)
        shape += (LANES,)
        tall = max(w[3] for w in group.weights)
        wide = max(c if c % 256 else 256 for c in group.cols)

        def call(*operands):
            return in_vmem(
                lambda *refs: mine_kernel(group, self.by_y, *self.counts, *refs),
                [(shape, bf16), (shape, bf16)],
                operands,
                (at.scalars,),
                [pltpu.VMEM((tall, wide), f32)],
                limit=10,
            )

        if self.whole and not self.by_y:
            total = self.order(self.mine_all, *self.operands, *self.got)
            self.got = lax.psum_scatter(total, "fsdp", scatter_dimension=0, tiled=True)
            return
        self.keep, send = self.order(call, *self.operands, *self.got)
        self.got = at.over_y(send) if self.by_y else at.over_near(send)

    def mine_all(self, *operands):
        group = self.group
        return in_vmem(
            lambda *refs: mine_all_kernel(group, *self.counts, *refs),
            [((self.at.count, group.rows, LANES), bf16)],
            operands,
            (self.at.scalars,),
            limit=10,
        )[0]

    def split(self):
        if self.whole:
            total = self.order(join, self.keep, self.got)
            self.got = lax.psum_scatter(total, "fsdp", scatter_dimension=0, tiled=True)
            return
        shape = (self.at.shifts,) + self.keep.shape[1:]

        def call(*operands):
            return in_vmem(
                split_near_kernel,
                [(shape, bf16), (shape, bf16)],
                operands,
                (self.at.scalars,),
            )

        self.keep, send = self.order(call, self.keep, self.got)
        self.got = self.at.over_near(send)

    def deal(self):
        self.got = self.at.over_far(self.order(join, self.keep, self.got))

    def gather(self):
        def call(parts):
            return in_vmem(sum_kernel, [(parts.shape[1:], bf16)], (parts,))[0]

        if self.whole:
            self.total = after(self.got, *self.order.last)[0]
            self.order.wait(self.total)
        else:
            self.total = self.order(call, self.got)
        self.got = self.at.over_y(self.total)
        if self.by_y:
            self.other = self.at.over_core(self.total)

    def finish(self):
        if self.by_y:
            self.got = after(self.got, *self.order.last)
            self.order.wait(self.got)
            self.got_other = self.at.over_core(self.got)
        else:
            self.total = self.order(join, self.total, self.got)
            self.other = self.at.over_core(self.total)

    def flats(self):
        if self.by_y:
            return (self.total, self.other, self.got, self.got_other)
        return (self.total, self.other)


def unpack_kernel(reduces, plan, extra, place_ref, *refs):
    flats, at = [], 0
    for r in reduces:
        flats.append(refs[at : at + len(r.flats())])
        at += len(r.flats())
    outs = refs[at:]

    for out_ref, blocks in zip(outs, plan):
        for block, (g, i) in enumerate(blocks):
            group, ways = reduces[g].group, len(flats[g]) // 2
            cols, part = group.cols[i], group.parts[i] // ways
            for n, flat in enumerate(flats[g]):
                first = (place_ref[0] ^ (n % 2)) * cols
                row = pl.multiple_of((place_ref[3] ^ (n // 2)) * part, 8) if ways == 2 else 0
                for j in range(group.tiles[i]):
                    start = group.offsets[i] // ways + j * part
                    col = pl.multiple_of(first + j * LANES, LANES)
                    out_ref[block, pl.ds(row, part), pl.ds(col, LANES)] = flat[
                        start : start + part, :
                    ].astype(f32)

    if extra is not None:
        group = reduces[extra].group
        outs[-1][...] = flats[extra][0][group.extra_offset :, :].astype(f32)


def unpack(at, order, reduces, plan, extra=None):
    outs = []
    for blocks in plan:
        group, i = reduces[blocks[0][0]].group, blocks[0][1]
        outs.append(((len(blocks), group.parts[i], 2 * group.cols[i]), f32))
    if extra is not None:
        outs.append(((reduces[extra].group.extra, LANES), f32))

    def call(*operands):
        return in_vmem(
            lambda *refs: unpack_kernel(reduces, plan, extra, *refs),
            outs,
            operands,
            (at.scalars,),
        )

    return order(call, *[v for r in reduces for v in r.flats()])


def per_device(
    hidden_in,
    cotangent,
    attn_gain,
    query_weight,
    key_weight,
    value_weight,
    out_weight,
    ffn_gain,
    gate_weight,
    up_weight,
    down_weight,
):
    at = Places()
    order = Order()
    rows, d = hidden_in.shape[2:]
    ff = gate_weight.shape[2]
    p, q = query_weight.shape[1], down_weight.shape[1]
    assert hidden_in.shape[0] == 2 and at.seq == 4
    direct = p % 32 == 0 and q % 32 == 0
    at.scalars = jnp.stack([at.core, at.near, at.far, at.y]).astype(jnp.int32)

    low = jnp.minimum(at.s, 3 - at.s)
    role = low.astype(jnp.int32).reshape(1)
    first_is_own = at.s < 2
    own_start = jnp.where(first_is_own, 0, rows).astype(jnp.int32).reshape(1)
    y = at.y.astype(jnp.int32).reshape(1)

    def spread(value, *waits):
        own = pick(value[:, 0], at.y, 0)
        got = at.mirror(after(pick(value[:, 0], 1 - at.y, 0), *waits))
        return jnp.concatenate(
            [jnp.where(first_is_own, own, got), jnp.where(first_is_own, got, own)]
        )

    def tables_of(first):
        steps = jnp.arange(rows, dtype=jnp.int32)
        return rope_tables(
            jnp.concatenate([first * rows + steps, (3 - first) * rows + steps])
        )

    tables = tables_of(low)
    attn_shards = jnp.stack([query_weight, key_weight, value_weight, out_weight], 1)
    gu_shards = jnp.stack([gate_weight, up_weight], 1)
    gain_shards = jnp.concatenate([attn_gain, ffn_gain])


    act = spread(hidden_in)
    cot = spread(cotangent)
    if direct:
        ph, qh = p // 2, q // 2

        def half(value, axis):
            size = value.shape[axis] // 2
            return lax.dynamic_slice_in_dim(value, at.core * size, size, axis)

        attn_half, gu_half, down_half = half(attn_shards, 2), half(gu_shards, 2), half(down_weight, 1)
        gain_rows = jnp.zeros((16, d), bf16).at[0, : 4 * p].set(gain_shards.reshape(4 * p))
        a0 = Gather(at, order, attn_half[0, :2].reshape(2 * ph, d))
        b0 = Gather(
            at, order, jnp.concatenate([attn_half[0, 2:].reshape(2 * ph, d), gain_rows])
        )
        gu0 = Gather(at, order, pick(gu_half[0], at.y, 0), True)
        d0 = Gather(at, order, down_half[0])
        da1 = GatherWhole(
            at, order, jnp.concatenate([down_half[1], attn_half[1].reshape(4 * ph, d)])
        )
        gu1 = GatherWhole(at, order, gu_half[1].reshape(2 * ph, ff))
        a0_plan = [(0, i, i * ph, ph, False) for i in range(2)]
        b0_plan = [(0, 2 + i, i * ph, ph, False) for i in range(2)]
        gu_plan = [(0, (1, 0), 0, ph, False)]
        d0_plan = [(0, 0, 0, qh, False)]
        da1_plan = [(0, i, qh + i * ph, ph, False) for i in range(4)]
        da1_plan += [(1, 0, 0, qh, False)]
        gu1_plan = [(0, i, i * ph, ph, False) for i in range(2)]
        attn_shape, gu_shape, down_shape = (4, d, d), (2, d, ff), (1, ff, d)

        a0.far()
        b0.far()
        order.wait(act, cot)
        a0.near()
        a0.cores()
        b0.near()
        da1.far()
        gu1.far()
        gu0.far()
        b0.cores()
        (w_attn0,) = place(order, [attn_shape], (a0, a0_plan), (b0, b0_plan))
        w_out0 = w_attn0[3]
        index = ((jnp.arange(at.count) % 2) ^ at.near) * at.shifts
        index = index + jnp.arange(at.count) // 2
        gain_got = jnp.concatenate(
            [b0.here[:, 2 * ph, : 4 * p], b0.there[:, 2 * ph, : 4 * p]]
        )
        select = jax.nn.one_hot(index, at.count, dtype=f32)
        gains = jnp.dot(select, gain_got.astype(f32), precision=lax.Precision.HIGHEST)
        gains = gains.reshape(at.count, 4, p).transpose(1, 0, 2).reshape(4, d)
    else:

        def whole(value, axis):
            return lax.all_gather(value, "fsdp", axis=axis, tiled=True)

        attn_all, gu_all, down_all = whole(attn_shards, 2), whole(gu_shards, 2), whole(down_weight, 1)
        gains = whole(gain_shards, 1).astype(f32)
        w_attn0, w_out0 = attn_all[0], attn_all[0, 3]

    q0, kv0 = order(lambda *v: project_qkv(*v, tables), act, w_attn0)
    kv0_other = at.over_core(kv0)
    if direct:
        gu0.near()
        d0.far()
    o0, lse0 = order(lambda *v: attn_forward(role, *v), q0, kv0, kv0_other)
    sum0, act0 = order(lambda *v: project_out(0, *v), o0, w_out0, act, gains)
    if direct:
        gu0.middle()
        d0.near()
        gu0.cores()
        (w_gu0,) = place(order, [gu_shape], (gu0, gu_plan))
    else:
        w_gu0 = gu_all[0]
    hidden0, silu0, slope0 = order(ffn_in, act0, w_gu0)
    if direct:
        d0.cores()
        da1.near()
        w_down0 = place(order, [down_shape], (d0, d0_plan))[0][0]
    else:
        w_down0 = down_all[0]
    sum1, z, act1 = order(ffn_out_first, hidden0, w_down0, sum0, gains)
    if direct:
        da1.cores()
        w_attn1, w_down1 = place(order, [attn_shape, down_shape], (da1, da1_plan))
        w_out1, w_down1 = w_attn1[3], w_down1[0]
    else:
        w_attn1, w_out1, w_down1 = attn_all[1], attn_all[1, 3], down_all[1]
    q1, kv1 = order(lambda *v: project_qkv(*v, tables), act1, w_attn1)
    kv1_other = at.over_core(kv1)
    if direct:
        gu1.near()
    o1, lse1 = order(lambda *v: attn_forward(role, *v), q1, kv1, kv1_other)
    sum2, act2 = order(lambda *v: project_out(3, *v), o1, w_out1, z, gains)
    if direct:
        gu1.cores()
        (w_gu1,) = place(order, [gu_shape], (gu1, gu1_plan))
    else:
        w_gu1 = gu_all[1]
    hidden1, silu1, slope1 = order(ffn_in, act2, w_gu1)
    out_own, out_send = order(
        lambda *v: ffn_out_second(own_start, *v), hidden1, w_down1, sum2
    )


    ffn_group = [(0, 0, 0, d, ff), (0, 0, 1, d, ff), (1, 1, None, ff, d), (2, 2, None, d, d)]
    gu_group = [(0, 0, 0, d, ff), (0, 0, 1, d, ff)]
    rest_group = [(0, 0, None, ff, d), (1, 1, None, d, d)]
    qkv_group = [(0, 0, None, d, d), (0, 1, 0, d, d), (0, 1, 1, d, d)]

    def reduce(weights, by_y, whole, *rest):
        group = Group(weights, at.count, 16 * (len(rest) == 3), weights is gu_group)
        return Reduce(at, order, group, by_y, whole, *rest)

    dgu1, grad, low1, do1, dgain_f1 = order(
        lambda *v: ffn_back(False, *v), cot, silu1, slope1, w_down1, w_gu1, w_out1, sum2, gains
    )
    if direct:
        r1 = reduce(ffn_group, False, True, (act2, hidden1, o1), (dgu1, cot, low1))
        r1.theirs()
    dq1, dkv1, *dkv1_other = order(
        lambda *v: attn_backward(role, *v, tables),
        q1, kv1, kv1_other, lse1, o1, do1,
    )
    dkv1_got = in_parts(at.over_core, dkv1_other)
    if direct:
        r1.mine()
    dkv1 = order(join_parts, dkv1, *dkv1_got, *tables)
    if direct:
        r2 = reduce(qkv_group, False, False, (act1,), (dq1, dkv1))
        r2.theirs()
    grad, low_mid, dgain_mid = order(
        qkv_back_second, dq1, dkv1, w_attn1, grad, z, sum1, gains
    )
    if direct:
        r2.mine()
    out_got = at.mirror(after(out_send, *order.last))
    dgu0, grad, low0, do0, dgain_a0 = order(
        lambda *v: ffn_back(True, *v), grad, silu0, slope0, w_down0, w_gu0, w_out0, sum0, gains
    )
    layer_out = order(lambda *v: merge(y, *v), out_own, out_got)
    if direct:
        r3 = reduce(gu_group, True, False, (act0,), (dgu0,))
        s3 = reduce(rest_group, False, False, (hidden0, o0), (low_mid, low0))
        r3.theirs()
        s3.theirs()
        r3.mine()
        s3.mine()
        r2.deal()
    dq0, dkv0, *dkv0_other = order(
        lambda *v: attn_backward(role, *v, tables),
        q0, kv0, kv0_other, lse0, o0, do0,
    )
    dkv0_got = in_parts(at.over_core, dkv0_other)
    if direct:
        s3.deal()
        r3.split()
    dkv0 = order(join_parts, dkv0, *dkv0_got, *tables)
    dgains = jnp.concatenate([dgain_a0, dgain_mid, dgain_f1])
    if direct:
        extra = dgains.reshape(4, at.count, p).transpose(1, 0, 2).reshape(at.count, -1, LANES)
        extra = jnp.pad(extra, ((0, 0), (0, 16 - extra.shape[1]), (0, 0)))
        extra = extra.reshape(at.count * 16, LANES)
        r4 = reduce(qkv_group, False, False, (act,), (dq0, dkv0), (extra,))
        r4.theirs()
    in_own, in_send = order(
        lambda *v: qkv_back_first(own_start, *v), dq0, dkv0, w_attn0, grad
    )
    in_got = at.mirror(in_send)

    if direct:
        r3.deal()
        r4.mine()
        r2.gather()
        input_grad = order(lambda *v: merge(y, *v), in_own, in_got)
        r1.gather()
        r2.finish()
        s3.gather()
        r4.deal()
        r1.finish()
        r3.gather()
        s3.finish()
        r3.finish()
        r4.gather()
        grad_gate, grad_up, grad_down, grad_out = unpack(
            at, order, [r3, s3, r1],
            [[(0, 0), (2, 0)], [(0, 1), (2, 1)], [(1, 0), (2, 2)], [(1, 1), (2, 3)]],
        )
        r4.finish()
        *grad_qkv, gain_rows = unpack(
            at, order, [r4, r2], [[(0, i), (1, i)] for i in range(3)], 0
        )
        gain_grads = gain_rows.reshape(-1)[: 4 * p].reshape(4, p)
    else:
        input_grad = merge(y, in_own, in_got)

        def sums(*values):
            total = jnp.stack(values).astype(bf16)
            total = lax.psum_scatter(total, "fsdp", scatter_dimension=1, tiled=True)
            return lax.psum(total, "seq").astype(f32)

        grad_qkv = [
            sums(dot_tn(act, dq0), dot_tn(act1, dq1)),
            sums(dot_tn(act, dkv0[0]), dot_tn(act1, dkv1[0])),
            sums(dot_tn(act, dkv0[1]), dot_tn(act1, dkv1[1])),
        ]
        grad_gate = sums(dot_tn(act0, dgu0[0]), dot_tn(act2, dgu1[0]))
        grad_up = sums(dot_tn(act0, dgu0[1]), dot_tn(act2, dgu1[1]))
        grad_down = sums(dot_tn(hidden0, low_mid), dot_tn(hidden1, cot))
        grad_out = sums(dot_tn(o0, low0), dot_tn(o1, low1))
        gain_grads = lax.psum_scatter(dgains, "fsdp", scatter_dimension=1, tiled=True)
        gain_grads = lax.psum(gain_grads, "seq")
    return (
        layer_out,
        input_grad,
        gain_grads[:2],
        *grad_qkv,
        grad_out,
        gain_grads[2:],
        grad_gate,
        grad_up,
        grad_down,
    )


def solution(mesh):
    tokens = P(None, "fsdp", "seq", None)
    gain = P(None, "fsdp")
    weight = P(None, "fsdp", None)
    return jax.shard_map(
        per_device,
        mesh=mesh,
        in_specs=(tokens, tokens, gain) + (weight,) * 4 + (gain,) + (weight,) * 3,
        out_specs=(tokens, tokens, gain) + (weight,) * 4 + (gain,) + (weight,) * 3,
        check_vma=False,
    )
```

```python
import math

import jax
import jax.numpy as jnp
from jax import lax
from jax.experimental import pallas as pl
from jax.experimental.pallas import tpu as pltpu
from jax.sharding import PartitionSpec as P

HD = 64
LANES = 128
epsilon = 1e-05
masked_value = -1e30
QUERY_SCALE = HD**-0.5 * math.log2(math.e)
bf16 = jnp.bfloat16
f32 = jnp.float32
MIB = 1 << 20
CHUNK = 256
FREE = pl.CostEstimate(flops=1, bytes_accessed=1, transcendentals=0)
NT = (((1,), (1,)), ((), ()))
TN = (((0,), (0,)), ((), ()))


def rope_tables(positions):
    half_dim = HD // 2
    rates = jnp.exp(jnp.arange(half_dim, dtype=f32) * (-2.0 * math.log(10000.0) / HD))
    angles = positions.astype(f32)[:, None] * rates[None, :]
    repeat = LANES // half_dim
    return jnp.tile(jnp.cos(angles), (1, repeat)), jnp.tile(jnp.sin(angles), (1, repeat))


def turn(values, cosine, sine):
    lane = lax.broadcasted_iota(jnp.int32, values.shape, 1)
    first = (lane % HD) < HD // 2
    back = pltpu.roll(values, LANES - HD // 2, 1)
    ahead = pltpu.roll(values, HD // 2, 1)
    return values * cosine + jnp.where(first, -back, ahead) * sine


def in_vmem(kernel, outs, operands, scalars=(), scratch=(), limit=6):
    smem = [pl.BlockSpec(memory_space=pltpu.SMEM)] * len(scalars)
    vmem = pl.BlockSpec(memory_space=pltpu.VMEM)
    moved = sum(v.size * v.dtype.itemsize for v in operands)
    moved += sum(math.prod(shape) * jnp.dtype(dtype).itemsize for shape, dtype in outs)
    room = limit * MIB + moved
    return pl.pallas_call(
        kernel,
        in_specs=smem + [vmem] * len(operands),
        out_specs=[vmem] * len(outs),
        out_shape=[jax.ShapeDtypeStruct(shape, dtype) for shape, dtype in outs],
        scratch_shapes=list(scratch),
        compiler_params=pltpu.CompilerParams(vmem_limit_bytes=room),
        cost_estimate=FREE,
    )(*scalars, *operands)


def chunks(size, step=CHUNK):
    return [slice(i, min(i + step, size)) for i in range(0, size, step)]


def root(values):
    return lax.rsqrt(jnp.mean(values * values, -1, keepdims=True) + epsilon)


def norm_back(values, gain, grad):
    scale = root(values)
    unit = values * scale
    inner = grad * gain
    out = scale * (inner - unit * jnp.mean(inner * unit, -1, keepdims=True))
    return out, jnp.sum(grad * unit, 0, keepdims=True)


def dot(left, right):
    return jnp.dot(left, right, preferred_element_type=f32)


def dot_nt(left, right):
    return lax.dot_general(left, right, NT, preferred_element_type=f32)


def dot_tn(left, right):
    return lax.dot_general(left, right, TN, preferred_element_type=f32)


def qkv_kernel(act_ref, w_ref, cos_ref, sin_ref, q_ref, kv_ref):
    act = act_ref[...]
    for i in range(3):
        for cols in chunks(act.shape[1]):
            prod = dot(act, w_ref[i, :, cols])
            for at in range(cols.start, cols.stop, LANES):
                part = prod[:, at - cols.start : at - cols.start + LANES]
                if i < 2:
                    part = turn(part, cos_ref[...], sin_ref[...])
                if i == 0:
                    part = part * QUERY_SCALE
                part = part.astype(bf16)
                if i == 0:
                    q_ref[:, at : at + LANES] = part
                else:
                    kv_ref[i - 1, :, at : at + LANES] = part


def project_qkv(act, w_qkv, tables):
    rows, width = act.shape
    outs = [((rows, width), bf16), ((2, rows, width), bf16)]
    return in_vmem(qkv_kernel, outs, (act, w_qkv, *tables))


def out_kernel(which, o_ref, w_ref, resid_ref, gain_ref, sum_ref, act_ref):
    o = o_ref[...]
    for cols in chunks(o.shape[1]):
        sum_ref[:, cols] = resid_ref[:, cols].astype(f32) + dot(o, w_ref[:, cols])
    total = sum_ref[...]
    act_ref[...] = (total * root(total) * gain_ref[which : which + 1, :]).astype(bf16)


def project_out(which, o, w_out, resid, gains):
    shape = o.shape
    return in_vmem(
        lambda *refs: out_kernel(which, *refs),
        [(shape, f32), (shape, bf16)],
        (o, w_out, resid, gains),
    )


def ffn_in_kernel(act_ref, w_ref, hidden_ref, silu_ref, slope_ref):
    act = act_ref[...]
    for cols in chunks(hidden_ref.shape[1]):
        gate = dot(act, w_ref[0, :, cols])
        up = dot(act, w_ref[1, :, cols])
        sig = jax.nn.sigmoid(gate)
        silu = gate * sig
        hidden_ref[:, cols] = (silu * up).astype(bf16)
        silu_ref[:, cols] = silu.astype(bf16)
        slope_ref[:, cols] = (up * sig * (1.0 + gate * (1.0 - sig))).astype(bf16)


def ffn_in(act, w_gu):
    shape = (act.shape[0], w_gu.shape[2])
    return in_vmem(ffn_in_kernel, [(shape, bf16)] * 3, (act, w_gu))


def ffn_out_first_kernel(hid_ref, w_ref, sum_ref, gain_ref, next_ref, z_ref, act_ref):
    total = sum_ref[...]
    next_ref[...] = total * root(total) * gain_ref[0:1, :]
    hid = hid_ref[...]
    for cols in chunks(w_ref.shape[1]):
        next_ref[:, cols] += dot(hid, w_ref[:, cols])
    total = next_ref[...]
    z = total * root(total) * gain_ref[2:3, :]
    z_ref[...] = z
    act_ref[...] = (z * root(z) * gain_ref[1:2, :]).astype(bf16)


def ffn_out_first(hidden, w_down, total, gains):
    shape = total.shape
    return in_vmem(
        ffn_out_first_kernel,
        [(shape, f32), (shape, f32), (shape, bf16)],
        (hidden, w_down, total, gains),
    )


def split_rows(start_ref, value_ref, own_ref, send_ref):
    rows = own_ref.shape[0]
    own = pl.multiple_of(start_ref[0], rows)
    send = pl.multiple_of(rows - start_ref[0], rows)
    own_ref[...] = value_ref[pl.ds(own, rows), :]
    send_ref[...] = value_ref[pl.ds(send, rows), :].astype(bf16)


def ffn_out_second_kernel(start_ref, hid_ref, w_ref, sum_ref, own_ref, send_ref, total):
    hid = hid_ref[...]
    for cols in chunks(w_ref.shape[1]):
        total[:, cols] = sum_ref[:, cols] + dot(hid, w_ref[:, cols])
    split_rows(start_ref, total, own_ref, send_ref)


def ffn_out_second(start, hidden, w_down, total):
    rows, width = total.shape
    half = (rows // 2, width)
    return in_vmem(
        ffn_out_second_kernel,
        [(half, f32), (half, bf16)],
        (hidden, w_down, total),
        (start,),
        [pltpu.VMEM(total.shape, f32)],
    )


def ffn_back_kernel(
    post, grad_ref, silu_ref, slope_ref, wd_ref, wgu_ref, wo_ref, sum_ref, gain_ref,
    dgu_ref, total_ref, low_ref, do_ref, dgain_ref,
):
    grad_low = grad_ref[...].astype(bf16)
    for cols in chunks(wd_ref.shape[0]):
        hid = dot_nt(grad_low, wd_ref[cols, :])
        dgu_ref[0, :, cols] = (hid * slope_ref[:, cols].astype(f32)).astype(bf16)
        dgu_ref[1, :, cols] = (hid * silu_ref[:, cols].astype(f32)).astype(bf16)
    for cols in chunks(total_ref.shape[1]):
        back = dot_nt(dgu_ref[0], wgu_ref[0, cols, :])
        back += dot_nt(dgu_ref[1], wgu_ref[1, cols, :])
        total_ref[:, cols] = back
    if post:
        out, dgain = norm_back(
            sum_ref[...], gain_ref[0:1, :], grad_ref[...] + total_ref[...]
        )
    else:
        out, dgain = norm_back(sum_ref[...], gain_ref[3:4, :], total_ref[...])
        out = grad_ref[...].astype(f32) + out
    dgain_ref[...] = dgain
    total_ref[...] = out
    low_ref[...] = out.astype(bf16)
    low = low_ref[...]
    for cols in chunks(total_ref.shape[1]):
        do_ref[:, cols] = dot_nt(low, wo_ref[cols, :]).astype(bf16)


def ffn_back(post, grad, silu, slope, w_down, w_gu, w_out, total, gains):
    shape = total.shape
    outs = [
        ((2,) + silu.shape, bf16), (shape, f32), (shape, bf16), (shape, bf16),
        ((1, shape[1]), f32),
    ]
    return in_vmem(
        lambda *refs: ffn_back_kernel(post, *refs),
        outs,
        (grad, silu, slope, w_down, w_gu, w_out, total, gains),
    )


def join_kernel(a_ref, b_ref, out_ref):
    out_ref[...] = (a_ref[...].astype(f32) + b_ref[...].astype(f32)).astype(bf16)


def join(a, b):
    return in_vmem(join_kernel, [(a.shape, bf16)], (a, b))[0]


def join_parts_kernel(a_ref, dk_ref, dv_ref, cos_ref, sin_ref, out_ref):
    for at in range(0, a_ref.shape[2], LANES):
        cols = slice(at, at + LANES)
        total = a_ref[0, :, cols].astype(f32) + dk_ref[:, cols].astype(f32)
        out_ref[0, :, cols] = turn(total, cos_ref[...], -sin_ref[...]).astype(bf16)
    out_ref[1] = (a_ref[1].astype(f32) + dv_ref[...].astype(f32)).astype(bf16)


def join_parts(a, *rest):
    return in_vmem(join_parts_kernel, [(a.shape, bf16)], (a, *rest))[0]


def in_parts(send, values):
    return [send(v) for v in values]


def qkv_back_product(dq_ref, dkv_ref, w_ref, out_ref, base_ref):
    dq, dk, dv = dq_ref[...], dkv_ref[0], dkv_ref[1]
    for cols in chunks(out_ref.shape[1]):
        back = dot_nt(dq, w_ref[0, cols, :])
        back += dot_nt(dk, w_ref[1, cols, :])
        back += dot_nt(dv, w_ref[2, cols, :])
        if base_ref is not None:
            back += base_ref[:, cols]
        out_ref[:, cols] = back


def qkv_back_second_kernel(
    dq_ref, dkv_ref, w_ref, grad_ref, z_ref, sum_ref, gain_ref,
    out_ref, low_ref, dgain_ref,
):
    qkv_back_product(dq_ref, dkv_ref, w_ref, out_ref, None)
    back, dgain = norm_back(z_ref[...], gain_ref[1:2, :], out_ref[...])
    dgain_ref[0:1, :] = dgain
    out, dgain = norm_back(sum_ref[...], gain_ref[2:3, :], grad_ref[...] + back)
    dgain_ref[1:2, :] = dgain
    out_ref[...] = out
    low_ref[...] = out.astype(bf16)


def qkv_back_second(dq, dkv, w_qkv, grad, z, total, gains):
    shape = grad.shape
    return in_vmem(
        qkv_back_second_kernel,
        [(shape, f32), (shape, bf16), ((2, shape[1]), f32)],
        (dq, dkv, w_qkv, grad, z, total, gains),
    )


def qkv_back_first_kernel(
    start_ref, dq_ref, dkv_ref, w_ref, grad_ref, own_ref, send_ref, total
):
    qkv_back_product(dq_ref, dkv_ref, w_ref, total, grad_ref)
    split_rows(start_ref, total, own_ref, send_ref)


def qkv_back_first(start, dq, dkv, w_qkv, grad):
    rows, width = grad.shape
    half = (rows // 2, width)
    return in_vmem(
        qkv_back_first_kernel,
        [(half, f32), (half, bf16)],
        (dq, dkv, w_qkv, grad),
        (start,),
        [pltpu.VMEM(grad.shape, f32)],
    )


def merge_kernel(y_ref, own_ref, got_ref, out_ref):
    out_ref[y_ref[0], 0] = own_ref[...]
    out_ref[1 - y_ref[0], 0] = got_ref[...].astype(f32)


def merge(y, own, got):
    return in_vmem(merge_kernel, [((2, 1) + own.shape, f32)], (own, got), (y,))[0]


def key_tiles(role, block_index, own, other):
    if role == 0:
        table = [(own, 0), (other, 0), (other, 1), (own, 1)]
    else:
        table = [(other, 0), (own, 0), (own, 1), (other, 1)]
    return table[: block_index + 1]


def both_heads(values):
    lane = lax.broadcasted_iota(jnp.int32, values.shape, 1)
    zero = jnp.zeros_like(values)
    return jnp.concatenate(
        [jnp.where(lane < HD, values, zero), jnp.where(lane >= HD, values, zero)], 0
    )


def own_heads(values, rows):
    return jnp.concatenate([values[:HD, :rows], values[HD:, rows:]], 0)


def allowed_keys(rows):
    key = lax.broadcasted_iota(jnp.int32, (rows, rows), 0)
    query = lax.broadcasted_iota(jnp.int32, (rows, rows), 1)
    return jnp.concatenate([key <= query] * 2, 1)


def attn_fwd_kernel(role_ref, q_ref, ko_ref, vo_ref, kt_ref, vt_ref, o_ref, lse_ref):
    rows = q_ref.shape[0] // 2
    own, other = (0, ko_ref, vo_ref), (1, kt_ref, vt_ref)

    def one(role, j, turned):
        block_index = (role, 3 - role)[j]
        tiles = key_tiles(role, block_index, own, other)
        here = slice(j * rows, (j + 1) * rows)
        pair = both_heads(q_ref[here, :])
        allowed = allowed_keys(rows)
        scores = []
        top = None
        for t, ((_, k_ref, _), i) in enumerate(tiles):
            s = dot_nt(k_ref[0, i * rows : (i + 1) * rows, :], pair)
            if t == block_index:
                s = jnp.where(allowed, s, masked_value)
            scores.append(s)
            tile_top = jnp.max(s, 0, keepdims=True)
            top = tile_top if top is None else jnp.maximum(top, tile_top)
        total = None
        mixed = None
        for s, ((which, _, _), i) in zip(scores, tiles):
            p = jnp.exp2(s - top)
            part = jnp.sum(p, 0, keepdims=True)
            total = part if total is None else total + part
            m = dot(turned[(which, i)], p.astype(bf16))
            mixed = m if mixed is None else mixed + m
        mixed = mixed * (1.0 / total)
        sums = top + jnp.log2(total)
        for h in range(2):
            lse_ref[0, h : h + 1, here] = sums[:, h * rows : (h + 1) * rows]
        o_ref[here, :] = own_heads(mixed, rows).T.astype(bf16)

    for role in range(2):

        @pl.when(role_ref[0] == role)
        def _(role=role):
            turned = {}
            for which, _, v_ref in (own, other):
                for i in range(2):
                    turned[(which, i)] = v_ref[0, i * rows : (i + 1) * rows, :].T
            for j in range(2):
                one(role, j, turned)


def attn_forward(role, q, kv_own, kv_other):
    rows, width = q.shape
    pairs = width // LANES
    smem = pl.BlockSpec(memory_space=pltpu.SMEM)
    act = pl.BlockSpec((rows, LANES), lambda i: (0, i))

    def kv(which):
        return pl.BlockSpec((1, rows, LANES), lambda i: (which, 0, i))

    return pl.pallas_call(
        attn_fwd_kernel,
        grid=(pairs,),
        in_specs=[smem, act, kv(0), kv(1), kv(0), kv(1)],
        out_specs=[act, pl.BlockSpec((1, 2, rows), lambda i: (i, 0, 0))],
        out_shape=[
            jax.ShapeDtypeStruct((rows, width), bf16),
            jax.ShapeDtypeStruct((pairs, 2, rows), f32),
        ],
        compiler_params=pltpu.CompilerParams(vmem_limit_bytes=12 * MIB),
        cost_estimate=FREE,
    )(role, q, kv_own, kv_own, kv_other, kv_other)


def attn_bwd_kernel(
    role_ref, q_ref, ko_ref, vo_ref, kt_ref, vt_ref, lse_ref, o_ref, do_ref,
    cos_ref, sin_ref, dq_ref, down_ref, *rest
):
    *other_refs, acc_ref = rest
    rows = q_ref.shape[0] // 2
    own, other = (0, ko_ref, vo_ref), (1, kt_ref, vt_ref)

    def one(role, j, seen, turned):
        block_index = (role, 3 - role)[j]
        tiles = key_tiles(role, block_index, own, other)
        here = slice(j * rows, (j + 1) * rows)
        pair, grads = both_heads(q_ref[here, :]), both_heads(do_ref[here, :])
        allowed = allowed_keys(rows)
        both = (do_ref[here, :].astype(f32) * o_ref[here, :].astype(f32)).T
        delta = jnp.concatenate(
            [jnp.sum(both[h * HD : (h + 1) * HD, :], 0, keepdims=True) for h in range(2)], 1
        )
        lse = jnp.concatenate([lse_ref[0, h : h + 1, here] for h in range(2)], 1)
        total = None
        for t, ((which, k_ref, v_ref), i) in enumerate(tiles):
            there = slice(i * rows, (i + 1) * rows)
            s = dot_nt(k_ref[0, there, :], pair)
            p = jnp.exp2(s - lse)
            if t == block_index:
                p = jnp.where(allowed, p, 0.0)
            dp = dot_nt(v_ref[0, there, :], grads)
            ds = (p * (dp - delta)).astype(bf16)
            dv = dot(p.astype(bf16), grads)
            dk = dot(ds, pair)
            dq = dot(turned[(which, i)], ds)
            total = dq if total is None else total + dq
            key = (which, i)
            if key in seen:
                acc_ref[which, 0, there, :] += dk
                acc_ref[which, 1, there, :] += dv
            else:
                seen.add(key)
                acc_ref[which, 0, there, :] = dk
                acc_ref[which, 1, there, :] = dv
        grad = own_heads(total, rows).T * (HD**-0.5)
        dq_ref[here, :] = turn(grad, cos_ref[here, :], -sin_ref[here, :]).astype(bf16)

    for role in range(2):

        @pl.when(role_ref[0] == role)
        def _(role=role):
            seen, turned = set(), {}
            for which, k_ref, _ in (own, other):
                for i in range(2):
                    turned[(which, i)] = k_ref[0, i * rows : (i + 1) * rows, :].T
            for j in range(2):
                one(role, j, seen, turned)
            for which in range(2):
                for i in range(2):
                    if (which, i) not in seen:
                        zeros = jnp.zeros((2, rows, LANES), f32)
                        acc_ref[which, :, i * rows : (i + 1) * rows, :] = zeros

    down_ref[0] = (acc_ref[0, 0] * math.log(2.0)).astype(bf16)
    down_ref[1] = acc_ref[0, 1].astype(bf16)
    other_refs[0][...] = (acc_ref[1, 0] * math.log(2.0)).astype(bf16)
    other_refs[1][...] = acc_ref[1, 1].astype(bf16)


def attn_backward(role, q, kv_own, kv_other, lse, o, do, tables):
    rows, width = q.shape
    pairs = width // LANES
    smem = pl.BlockSpec(memory_space=pltpu.SMEM)
    act = pl.BlockSpec((rows, LANES), lambda i: (0, i))
    tab = pl.BlockSpec((rows, LANES), lambda i: (0, 0))
    two = pl.BlockSpec((2, rows, LANES), lambda i: (0, 0, i))

    def kv(which):
        return pl.BlockSpec((1, rows, LANES), lambda i: (which, 0, i))

    return pl.pallas_call(
        attn_bwd_kernel,
        grid=(pairs,),
        in_specs=[
            smem, act, kv(0), kv(1), kv(0), kv(1),
            pl.BlockSpec((1, 2, rows), lambda i: (i, 0, 0)), act, act, tab, tab,
        ],
        out_specs=[act, two, act, act],
        out_shape=[
            jax.ShapeDtypeStruct((rows, width), bf16),
            jax.ShapeDtypeStruct((2, rows, width), bf16),
        ]
        + [jax.ShapeDtypeStruct((rows, width), bf16)] * 2,
        scratch_shapes=[pltpu.VMEM((2, 2, rows, LANES), f32)],
        compiler_params=pltpu.CompilerParams(vmem_limit_bytes=12 * MIB),
        cost_estimate=FREE,
    )(role, q, kv_own, kv_own, kv_other, kv_other, lse, o, do, *tables)


class Places:
    def __init__(self):
        self.count = lax.axis_size("fsdp")
        self.seq = lax.axis_size("seq")
        self.f = lax.axis_index("fsdp")
        self.s = lax.axis_index("seq")
        self.far, self.near = self.f // 2, self.f % 2
        self.shifts = self.count // 2
        self.core = self.s % 2
        self.y = self.s // 2

    def over_far(self, value):
        groups = [list(range(i, self.count, 2)) for i in range(2)]
        return lax.all_to_all(value, "fsdp", 0, 0, axis_index_groups=groups, tiled=True)

    def over_near(self, value):
        return lax.ppermute(value, "fsdp", [(i, i ^ 1) for i in range(self.count)])

    def over_core(self, value):
        return lax.ppermute(value, "seq", [(i, i ^ 1) for i in range(self.seq)])

    def over_y(self, value):
        return lax.ppermute(value, "seq", [(i, i ^ 2) for i in range(self.seq)])

    def mirror(self, value):
        last = self.seq - 1
        return lax.ppermute(value, "seq", [(i, last - i) for i in range(self.seq)])


def after(value, *others):
    return lax.optimization_barrier((value,) + others)[0]


def pick(value, index, axis):
    return lax.dynamic_index_in_dim(value, index, axis, keepdims=False)


def place_kernel(plans, unit_ref, slot_ref, *refs):
    count = len(plans)
    pieces, outs = refs[:count], refs[count:]
    for a, (piece, plan) in enumerate(zip(pieces, plans)):
        for k in range(piece.shape[0]):
            unit = unit_ref[a * piece.shape[0] + k]
            for out_index, slot, start, size, by_rows in plan:
                number = unit * 2 + slot_ref[a] if by_rows else unit
                row = pl.multiple_of(number * size, 16)
                if isinstance(slot, tuple):
                    slot = slot_ref[a] * slot[0] + slot[1]
                outs[out_index][slot, pl.ds(row, size), :] = piece[k, start : start + size, :]


def place(order, out_shapes, *groups):
    plans, pieces, units, slots = [], [], [], []
    for gather, plan in groups:
        for value, unit, slot in gather.pieces():
            plans.append(plan)
            pieces.append(value)
            units.append(unit)
            slots.append(slot)
    units = jnp.concatenate(units).astype(jnp.int32)
    slots = jnp.stack(slots).astype(jnp.int32)

    def call(*values):
        return in_vmem(
            lambda *refs: place_kernel(plans, *refs),
            [(shape, bf16) for shape in out_shapes],
            values,
            (units, slots),
        )

    return order(call, *pieces)


class Order:
    def __init__(self):
        self.last = ()

    def wait(self, *values):
        self.last = self.last + values

    def __call__(self, function, *operands):
        if self.last:
            operands = (after(operands[0], *self.last),) + operands[1:]
        out = function(*operands)
        self.last = (out[0] if isinstance(out, (tuple, list)) else out,)
        return out


class Gather:
    def __init__(self, at, order, own, by_y=False):
        self.at, self.order, self.own, self.by_y = at, order, own, by_y

    def far(self):
        own = after(self.own, *self.order.last) if self.order.last else self.own
        self.here = self.at.over_far(jnp.broadcast_to(own[None], (self.at.shifts,) + own.shape))

    def arrived(self, value):
        value = after(value, *self.order.last)
        self.order.wait(value)
        return value

    def near(self):
        self.here = self.arrived(self.here)
        self.there = self.at.over_near(self.here)
        if self.by_y:
            self.here_y = self.at.over_y(self.here)
        self.here_core = self.at.over_core(self.here)

    def middle(self):
        self.there = self.arrived(self.there)
        self.there_y = self.at.over_y(self.there)
        self.there_core = self.at.over_core(self.there)
        self.here_y = self.arrived(self.here_y)
        self.here_y_core = self.at.over_core(self.here_y)

    def cores(self):
        if self.by_y:
            self.there_y = self.arrived(self.there_y)
            self.there_y_core = self.at.over_core(self.there_y)
        else:
            self.there = self.arrived(self.there)
            self.there_core = self.at.over_core(self.there)

    def pieces(self):
        at = self.at
        far = jnp.arange(at.shifts, dtype=jnp.int32)
        values = [(self.here, self.there, self.here_core, self.there_core)]
        if self.by_y:
            more = (self.here_y, self.there_y, self.here_y_core, self.there_y_core)
            values.append(more)
        for side, four in enumerate(values):
            for i, value in enumerate(four):
                near, core = at.near ^ (i % 2), at.core ^ (i // 2)
                yield value, (far * 2 + near) * 2 + core, at.y ^ side


class GatherWhole(Gather):
    def far(self):
        rows = self.own.shape[0]
        own = after(self.own, *self.order.last)
        here = lax.all_gather(own, "fsdp", axis=0, tiled=True)
        self.here = here.reshape(self.at.count, rows, here.shape[1])

    def near(self):
        self.here = self.arrived(self.here)
        if self.by_y:
            self.here_y = self.at.over_y(self.here)
        self.here_core = self.at.over_core(self.here)

    def cores(self):
        if self.by_y:
            self.here_y = self.arrived(self.here_y)
            self.here_y_core = self.at.over_core(self.here_y)
        else:
            self.here_core = self.arrived(self.here_core)

    def pieces(self):
        at = self.at
        shard = jnp.arange(at.count, dtype=jnp.int32)
        yield self.here, shard * 2 + at.core, at.y
        yield self.here_core, shard * 2 + 1 - at.core, at.y
        if not self.by_y:
            return
        yield self.here_y, shard * 2 + at.core, 1 - at.y
        yield self.here_y_core, shard * 2 + 1 - at.core, 1 - at.y


class Group:
    def __init__(self, weights, count, extra=0, apart=False):
        self.weights, self.count, self.extra, self.apart = weights, count, extra, apart
        self.cols = [n // 2 for *_, n in weights]
        self.tiles = [c // LANES for c in self.cols]
        self.parts = [w[3] // count for w in weights]
        self.bases, self.offsets = [], []
        base = offset = 0
        for w, tiles, part in zip(weights, self.tiles, self.parts):
            self.bases.append(base)
            self.offsets.append(offset)
            base += w[3] * tiles
            offset += part * tiles
        self.extra_base, self.extra_offset = base, offset
        self.rows = offset + extra

    def halves(self):
        extra = [(self.extra * self.count, LANES)] if self.extra else []
        if self.apart:
            return [(w[3] * t, LANES) for w, t in zip(self.weights, self.tiles)] + extra
        return [(self.extra_base, LANES)] + extra

    def tile(self, refs, i, tile):
        rows = self.weights[i][3]
        if self.apart:
            return refs[i].at[tile * rows : (tile + 1) * rows, :]
        start = self.bases[i] + tile * rows
        return refs[0].at[start : start + rows, :]

    def products(self, half, lefts, rights):
        for i, (a, g, slot, _, _) in enumerate(self.weights):
            left = lefts[a][...]
            right = rights[g] if slot is None else rights[g].at[slot]
            step = 256 if self.cols[i] % 256 == 0 else self.cols[i]
            for start in range(0, self.cols[i], step):
                col = pl.multiple_of(half * self.cols[i] + start, LANES)
                yield i, start // LANES, dot_tn(left, right[:, pl.ds(col, step)])


def theirs_kernel(group, n_left, n_right, place_ref, *refs):
    lefts, rights = refs[:n_left], refs[n_left : n_left + n_right]
    rest = refs[n_left + n_right :]
    outs = rest[1:] if group.extra else rest
    for i, tile, value in group.products(1 - place_ref[0], lefts, rights):
        for j in range(value.shape[1] // LANES):
            group.tile(outs, i, tile + j)[...] = value[:, j * LANES : (j + 1) * LANES].astype(
                bf16
            )
    if group.extra:
        outs[-1][...] = rest[0][...].astype(bf16)


def mine_kernel(group, by_y, n_left, n_right, place_ref, *refs):
    lefts, rights = refs[:n_left], refs[n_left : n_left + n_right]
    rest = refs[n_left + n_right :]
    keep_ref, send_ref, scratch = rest[-3:]
    gots = rest[1:-3] if group.extra else rest[:-3]
    side = place_ref[3] if by_y else place_ref[1]

    def hand_out(size, cols, offset):
        half = size // 2 if by_y else size
        first = offset // 2 if by_y else offset
        for index in range(keep_ref.shape[0]):
            for ref, own in ((keep_ref, side), (send_ref, 1 - side)):
                row = pl.multiple_of((index * 2 + own) * half, 8)
                for j in range(cols // LANES):
                    ref[index, first + j * half : first + (j + 1) * half, :] = scratch[
                        pl.ds(row, half), j * LANES : (j + 1) * LANES
                    ].astype(bf16)

    for i, tile, value in group.products(place_ref[0], lefts, rights):
        rows, cols = value.shape
        for j in range(cols // LANES):
            got = group.tile(gots, i, tile + j)[...].astype(f32)
            cut = slice(j * LANES, (j + 1) * LANES)
            scratch[:rows, cut] = value[:, cut] + got
        part = group.parts[i]
        hand_out(part, cols, group.offsets[i] + tile * part)
    if group.extra:
        rows = group.extra * group.count
        scratch[:rows, :LANES] = rest[0][...].astype(f32) + gots[-1][...].astype(f32)
        hand_out(group.extra, LANES, group.extra_offset)


def mine_all_kernel(group, n_left, n_right, place_ref, *refs):
    lefts, rights = refs[:n_left], refs[n_left : n_left + n_right]
    gots, out_ref = refs[n_left + n_right : -1], refs[-1]
    for i, tile, value in group.products(place_ref[0], lefts, rights):
        part = group.parts[i]
        for j in range(value.shape[1] // LANES):
            got = group.tile(gots, i, tile + j)[...].astype(f32)
            total = value[:, j * LANES : (j + 1) * LANES] + got
            first = group.offsets[i] + (tile + j) * part
            for shard in range(group.count):
                out_ref[shard, first : first + part, :] = total[
                    shard * part : (shard + 1) * part, :
                ].astype(bf16)


def split_near_kernel(place_ref, keep_ref, got_ref, stay_ref, leave_ref):
    near = place_ref[1]
    for far in range(stay_ref.shape[0]):
        for ref, side in ((stay_ref, near), (leave_ref, 1 - near)):
            shard = 2 * far + side
            ref[far] = (keep_ref[shard].astype(f32) + got_ref[shard].astype(f32)).astype(bf16)


def sum_kernel(parts_ref, out_ref):
    total = parts_ref[0].astype(f32)
    for k in range(1, parts_ref.shape[0]):
        total = total + parts_ref[k].astype(f32)
    out_ref[...] = total.astype(bf16)


class Reduce:
    def __init__(self, at, order, group, by_y, whole, lefts, rights, extra=()):
        self.at, self.order, self.group = at, order, group
        self.by_y, self.whole = by_y, whole
        self.operands = (*lefts, *rights, *extra)
        self.counts = (len(lefts), len(rights))

    def theirs(self):
        group = self.group

        def call(*operands):
            return in_vmem(
                lambda *refs: theirs_kernel(group, *self.counts, *refs),
                [(shape, bf16) for shape in group.halves()],
                operands,
                (self.at.scalars,),
            )

        self.got = in_parts(self.at.over_core, self.order(call, *self.operands))

    def mine(self):
        group, at = self.group, self.at
        shape = (at.count, group.rows // 2) if self.by_y else (at.shifts, group.rows)
        shape += (LANES,)
        tall = max(w[3] for w in group.weights)
        wide = max(c if c % 256 else 256 for c in group.cols)

        def call(*operands):
            return in_vmem(
                lambda *refs: mine_kernel(group, self.by_y, *self.counts, *refs),
                [(shape, bf16), (shape, bf16)],
                operands,
                (at.scalars,),
                [pltpu.VMEM((tall, wide), f32)],
                limit=10,
            )

        if self.whole and not self.by_y:
            total = self.order(self.mine_all, *self.operands, *self.got)
            self.got = lax.psum_scatter(total, "fsdp", scatter_dimension=0, tiled=True)
            return
        self.keep, send = self.order(call, *self.operands, *self.got)
        self.got = at.over_y(send) if self.by_y else at.over_near(send)

    def mine_all(self, *operands):
        group = self.group
        return in_vmem(
            lambda *refs: mine_all_kernel(group, *self.counts, *refs),
            [((self.at.count, group.rows, LANES), bf16)],
            operands,
            (self.at.scalars,),
            limit=10,
        )[0]

    def split(self):
        if self.whole:
            total = self.order(join, self.keep, self.got)
            self.got = lax.psum_scatter(total, "fsdp", scatter_dimension=0, tiled=True)
            return
        shape = (self.at.shifts,) + self.keep.shape[1:]

        def call(*operands):
            return in_vmem(
                split_near_kernel,
                [(shape, bf16), (shape, bf16)],
                operands,
                (self.at.scalars,),
            )

        self.keep, send = self.order(call, self.keep, self.got)
        self.got = self.at.over_near(send)

    def deal(self):
        self.got = self.at.over_far(self.order(join, self.keep, self.got))

    def gather(self):
        def call(parts):
            return in_vmem(sum_kernel, [(parts.shape[1:], bf16)], (parts,))[0]

        if self.whole:
            self.total = after(self.got, *self.order.last)[0]
            self.order.wait(self.total)
        else:
            self.total = self.order(call, self.got)
        self.got = self.at.over_y(self.total)
        if self.by_y:
            self.other = self.at.over_core(self.total)

    def finish(self):
        if self.by_y:
            self.got = after(self.got, *self.order.last)
            self.order.wait(self.got)
            self.got_other = self.at.over_core(self.got)
        else:
            self.total = self.order(join, self.total, self.got)
            self.other = self.at.over_core(self.total)

    def flats(self):
        if self.by_y:
            return (self.total, self.other, self.got, self.got_other)
        return (self.total, self.other)


def unpack_kernel(reduces, plan, extra, place_ref, *refs):
    flats, at = [], 0
    for r in reduces:
        flats.append(refs[at : at + len(r.flats())])
        at += len(r.flats())
    outs = refs[at:]

    for out_ref, blocks in zip(outs, plan):
        for block, (g, i) in enumerate(blocks):
            group, ways = reduces[g].group, len(flats[g]) // 2
            cols, part = group.cols[i], group.parts[i] // ways
            for n, flat in enumerate(flats[g]):
                first = (place_ref[0] ^ (n % 2)) * cols
                row = pl.multiple_of((place_ref[3] ^ (n // 2)) * part, 8) if ways == 2 else 0
                for j in range(group.tiles[i]):
                    start = group.offsets[i] // ways + j * part
                    col = pl.multiple_of(first + j * LANES, LANES)
                    out_ref[block, pl.ds(row, part), pl.ds(col, LANES)] = flat[
                        start : start + part, :
                    ].astype(f32)

    if extra is not None:
        group = reduces[extra].group
        outs[-1][...] = flats[extra][0][group.extra_offset :, :].astype(f32)


def unpack(at, order, reduces, plan, extra=None):
    outs = []
    for blocks in plan:
        group, i = reduces[blocks[0][0]].group, blocks[0][1]
        outs.append(((len(blocks), group.parts[i], 2 * group.cols[i]), f32))
    if extra is not None:
        outs.append(((reduces[extra].group.extra, LANES), f32))

    def call(*operands):
        return in_vmem(
            lambda *refs: unpack_kernel(reduces, plan, extra, *refs),
            outs,
            operands,
            (at.scalars,),
        )

    return order(call, *[v for r in reduces for v in r.flats()])


def per_device(
    hidden_in,
    cotangent,
    attn_gain,
    query_weight,
    key_weight,
    value_weight,
    out_weight,
    ffn_gain,
    gate_weight,
    up_weight,
    down_weight,
):
    at = Places()
    order = Order()
    rows, d = hidden_in.shape[2:]
    ff = gate_weight.shape[2]
    p, q = query_weight.shape[1], down_weight.shape[1]
    assert hidden_in.shape[0] == 2 and at.seq == 4
    direct = p % 32 == 0 and q % 32 == 0
    at.scalars = jnp.stack([at.core, at.near, at.far, at.y]).astype(jnp.int32)

    low = jnp.minimum(at.s, 3 - at.s)
    role = low.astype(jnp.int32).reshape(1)
    first_is_own = at.s < 2
    own_start = jnp.where(first_is_own, 0, rows).astype(jnp.int32).reshape(1)
    y = at.y.astype(jnp.int32).reshape(1)

    def spread(value, *waits):
        own = pick(value[:, 0], at.y, 0)
        got = at.mirror(after(pick(value[:, 0], 1 - at.y, 0), *waits))
        return jnp.concatenate(
            [jnp.where(first_is_own, own, got), jnp.where(first_is_own, got, own)]
        )

    def tables_of(first):
        steps = jnp.arange(rows, dtype=jnp.int32)
        return rope_tables(
            jnp.concatenate([first * rows + steps, (3 - first) * rows + steps])
        )

    tables = tables_of(low)
    attn_shards = jnp.stack([query_weight, key_weight, value_weight, out_weight], 1)
    gu_shards = jnp.stack([gate_weight, up_weight], 1)
    gain_shards = jnp.concatenate([attn_gain, ffn_gain])


    act = spread(hidden_in)
    cot = spread(cotangent)
    if direct:
        ph, qh = p // 2, q // 2

        def half(value, axis):
            size = value.shape[axis] // 2
            return lax.dynamic_slice_in_dim(value, at.core * size, size, axis)

        attn_half, gu_half, down_half = half(attn_shards, 2), half(gu_shards, 2), half(down_weight, 1)
        gain_rows = jnp.zeros((16, d), bf16).at[0, : 4 * p].set(gain_shards.reshape(4 * p))
        attn_part = pick(attn_half[0].reshape(2, 2 * ph, d), at.y, 0)
        a0 = Gather(at, order, jnp.concatenate([attn_part, gain_rows]), True)
        gu0 = Gather(at, order, pick(gu_half[0], at.y, 0), True)
        d0 = Gather(at, order, pick(down_half[0].reshape(2, qh // 2, d), at.y, 0), True)
        da1 = GatherWhole(
            at, order, jnp.concatenate([down_half[1], attn_half[1].reshape(4 * ph, d)])
        )
        gu1 = GatherWhole(at, order, gu_half[1].reshape(2 * ph, ff))
        a0_plan = [(0, (2, i), i * ph, ph, False) for i in range(2)]
        gu_plan = [(0, (1, 0), 0, ph, False)]
        d0_plan = [(0, 0, 0, qh // 2, True)]
        da1_plan = [(0, i, qh + i * ph, ph, False) for i in range(4)]
        da1_plan += [(1, 0, 0, qh, False)]
        gu1_plan = [(0, i, i * ph, ph, False) for i in range(2)]
        attn_shape, gu_shape, down_shape = (4, d, d), (2, d, ff), (1, ff, d)

        a0.far()
        order.wait(act, cot)
        a0.near()
        gu0.far()
        da1.far()
        gu1.far()
        a0.middle()
        a0.cores()
        gu0.near()
        (w_attn0,) = place(order, [attn_shape], (a0, a0_plan))
        w_out0 = w_attn0[3]
        index = ((jnp.arange(at.count) % 2) ^ at.near) * at.shifts
        index = index + jnp.arange(at.count) // 2
        gain_got = jnp.concatenate(
            [a0.here[:, 2 * ph, : 4 * p], a0.there[:, 2 * ph, : 4 * p]]
        )
        select = jax.nn.one_hot(index, at.count, dtype=f32)
        gains = jnp.dot(select, gain_got.astype(f32), precision=lax.Precision.HIGHEST)
        gains = gains.reshape(at.count, 4, p).transpose(1, 0, 2).reshape(4, d)
    else:

        def whole(value, axis):
            return lax.all_gather(value, "fsdp", axis=axis, tiled=True)

        attn_all, gu_all, down_all = whole(attn_shards, 2), whole(gu_shards, 2), whole(down_weight, 1)
        gains = whole(gain_shards, 1).astype(f32)
        w_attn0, w_out0 = attn_all[0], attn_all[0, 3]

    q0, kv0 = order(lambda *v: project_qkv(*v, tables), act, w_attn0)
    kv0_other = at.over_core(kv0)
    if direct:
        d0.far()
    o0, lse0 = order(lambda *v: attn_forward(role, *v), q0, kv0, kv0_other)
    if direct:
        d0.near()
    sum0, act0 = order(lambda *v: project_out(0, *v), o0, w_out0, act, gains)
    if direct:
        gu0.middle()
        gu0.cores()
        (w_gu0,) = place(order, [gu_shape], (gu0, gu_plan))
    else:
        w_gu0 = gu_all[0]
    hidden0, silu0, slope0 = order(ffn_in, act0, w_gu0)
    if direct:
        d0.middle()
        d0.cores()
        da1.near()
        w_down0 = place(order, [down_shape], (d0, d0_plan))[0][0]
    else:
        w_down0 = down_all[0]
    sum1, z, act1 = order(ffn_out_first, hidden0, w_down0, sum0, gains)
    if direct:
        gu1.near()
        da1.cores()
        w_attn1, w_down1 = place(order, [attn_shape, down_shape], (da1, da1_plan))
        w_out1, w_down1 = w_attn1[3], w_down1[0]
    else:
        w_attn1, w_out1, w_down1 = attn_all[1], attn_all[1, 3], down_all[1]
    q1, kv1 = order(lambda *v: project_qkv(*v, tables), act1, w_attn1)
    kv1_other = at.over_core(kv1)
    o1, lse1 = order(lambda *v: attn_forward(role, *v), q1, kv1, kv1_other)
    sum2, act2 = order(lambda *v: project_out(3, *v), o1, w_out1, z, gains)
    if direct:
        gu1.cores()
        (w_gu1,) = place(order, [gu_shape], (gu1, gu1_plan))
    else:
        w_gu1 = gu_all[1]
    hidden1, silu1, slope1 = order(ffn_in, act2, w_gu1)
    out_own, out_send = order(
        lambda *v: ffn_out_second(own_start, *v), hidden1, w_down1, sum2
    )


    ffn_group = [(0, 0, 0, d, ff), (0, 0, 1, d, ff), (1, 1, None, ff, d), (2, 2, None, d, d)]
    gu_group = [(0, 0, 0, d, ff), (0, 0, 1, d, ff)]
    rest_group = [(0, 0, None, ff, d), (1, 1, None, d, d)]
    qkv_group = [(0, 0, None, d, d), (0, 1, 0, d, d), (0, 1, 1, d, d)]

    def reduce(weights, by_y, whole, *rest):
        group = Group(weights, at.count, 16 * (len(rest) == 3), weights is not ffn_group)
        return Reduce(at, order, group, by_y, whole, *rest)

    dgu1, grad, low1, do1, dgain_f1 = order(
        lambda *v: ffn_back(False, *v), cot, silu1, slope1, w_down1, w_gu1, w_out1, sum2, gains
    )
    if direct:
        r1 = reduce(ffn_group, False, True, (act2, hidden1, o1), (dgu1, cot, low1))
        r1.theirs()
    dq1, dkv1, *dkv1_other = order(
        lambda *v: attn_backward(role, *v, tables),
        q1, kv1, kv1_other, lse1, o1, do1,
    )
    dkv1_got = in_parts(at.over_core, dkv1_other)
    if direct:
        r1.mine()
    dkv1 = order(join_parts, dkv1, *dkv1_got, *tables)
    if direct:
        r2 = reduce(qkv_group, False, False, (act1,), (dq1, dkv1))
        r2.theirs()
    grad, low_mid, dgain_mid = order(
        qkv_back_second, dq1, dkv1, w_attn1, grad, z, sum1, gains
    )
    if direct:
        r2.mine()
    out_got = at.mirror(after(out_send, *order.last))
    dgu0, grad, low0, do0, dgain_a0 = order(
        lambda *v: ffn_back(True, *v), grad, silu0, slope0, w_down0, w_gu0, w_out0, sum0, gains
    )
    layer_out = order(lambda *v: merge(y, *v), out_own, out_got)
    if direct:
        r3 = reduce(gu_group, True, False, (act0,), (dgu0,))
        s3 = reduce(rest_group, False, False, (hidden0, o0), (low_mid, low0))
        r3.theirs()
        s3.theirs()
        r3.mine()
        s3.mine()
        r2.deal()
    dq0, dkv0, *dkv0_other = order(
        lambda *v: attn_backward(role, *v, tables),
        q0, kv0, kv0_other, lse0, o0, do0,
    )
    dkv0_got = in_parts(at.over_core, dkv0_other)
    if direct:
        s3.deal()
        r3.split()
    dkv0 = order(join_parts, dkv0, *dkv0_got, *tables)
    dgains = jnp.concatenate([dgain_a0, dgain_mid, dgain_f1])
    if direct:
        extra = dgains.reshape(4, at.count, p).transpose(1, 0, 2).reshape(at.count, -1, LANES)
        extra = jnp.pad(extra, ((0, 0), (0, 16 - extra.shape[1]), (0, 0)))
        extra = extra.reshape(at.count * 16, LANES)
        r4 = reduce(qkv_group, False, False, (act,), (dq0, dkv0), (extra,))
        r4.theirs()
    in_own, in_send = order(
        lambda *v: qkv_back_first(own_start, *v), dq0, dkv0, w_attn0, grad
    )
    in_got = at.mirror(in_send)

    if direct:
        r4.mine()
        input_grad = order(lambda *v: merge(y, *v), in_own, in_got)
        r3.deal()
        r2.gather()
        r1.gather()
        r2.finish()
        r1.finish()
        s3.gather()
        r4.deal()
        s3.finish()
        r3.gather()
        r3.finish()
        grad_gate, grad_up, grad_down, grad_out = unpack(
            at, order, [r3, s3, r1],
            [[(0, 0), (2, 0)], [(0, 1), (2, 1)], [(1, 0), (2, 2)], [(1, 1), (2, 3)]],
        )
        r4.gather()
        r4.finish()
        *grad_qkv, gain_rows = unpack(
            at, order, [r4, r2], [[(0, i), (1, i)] for i in range(3)], 0
        )
        gain_grads = gain_rows.reshape(-1)[: 4 * p].reshape(4, p)
    else:
        input_grad = merge(y, in_own, in_got)

        def sums(*values):
            total = jnp.stack(values).astype(bf16)
            total = lax.psum_scatter(total, "fsdp", scatter_dimension=1, tiled=True)
            return lax.psum(total, "seq").astype(f32)

        grad_qkv = [
            sums(dot_tn(act, dq0), dot_tn(act1, dq1)),
            sums(dot_tn(act, dkv0[0]), dot_tn(act1, dkv1[0])),
            sums(dot_tn(act, dkv0[1]), dot_tn(act1, dkv1[1])),
        ]
        grad_gate = sums(dot_tn(act0, dgu0[0]), dot_tn(act2, dgu1[0]))
        grad_up = sums(dot_tn(act0, dgu0[1]), dot_tn(act2, dgu1[1]))
        grad_down = sums(dot_tn(hidden0, low_mid), dot_tn(hidden1, cot))
        grad_out = sums(dot_tn(o0, low0), dot_tn(o1, low1))
        gain_grads = lax.psum_scatter(dgains, "fsdp", scatter_dimension=1, tiled=True)
        gain_grads = lax.psum(gain_grads, "seq")
    return (
        layer_out,
        input_grad,
        gain_grads[:2],
        *grad_qkv,
        grad_out,
        gain_grads[2:],
        grad_gate,
        grad_up,
        grad_down,
    )


def solution(mesh):
    tokens = P(None, "fsdp", "seq", None)
    gain = P(None, "fsdp")
    weight = P(None, "fsdp", None)
    return jax.shard_map(
        per_device,
        mesh=mesh,
        in_specs=(tokens, tokens, gain) + (weight,) * 4 + (gain,) + (weight,) * 3,
        out_specs=(tokens, tokens, gain) + (weight,) * 4 + (gain,) + (weight,) * 3,
        check_vma=False,
    )
```

```python
import math

import jax
import jax.numpy as jnp
from jax import lax
from jax.experimental import pallas as pl
from jax.experimental.pallas import tpu as pltpu
from jax.sharding import PartitionSpec as P

HD = 64
LANES = 128
epsilon = 1e-05
masked_value = -1e30
QUERY_SCALE = HD**-0.5 * math.log2(math.e)
bf16 = jnp.bfloat16
f32 = jnp.float32
MIB = 1 << 20
CHUNK = 256
FREE = pl.CostEstimate(flops=1, bytes_accessed=1, transcendentals=0)
NT = (((1,), (1,)), ((), ()))
TN = (((0,), (0,)), ((), ()))


def rope_tables(positions):
    half_dim = HD // 2
    rates = jnp.exp(jnp.arange(half_dim, dtype=f32) * (-2.0 * math.log(10000.0) / HD))
    angles = positions.astype(f32)[:, None] * rates[None, :]
    repeat = LANES // half_dim
    return jnp.tile(jnp.cos(angles), (1, repeat)), jnp.tile(jnp.sin(angles), (1, repeat))


def turn(values, cosine, sine):
    lane = lax.broadcasted_iota(jnp.int32, values.shape, 1)
    first = (lane % HD) < HD // 2
    back = pltpu.roll(values, LANES - HD // 2, 1)
    ahead = pltpu.roll(values, HD // 2, 1)
    return values * cosine + jnp.where(first, -back, ahead) * sine


def in_vmem(kernel, outs, operands, scalars=(), scratch=(), limit=6):
    smem = [pl.BlockSpec(memory_space=pltpu.SMEM)] * len(scalars)
    vmem = pl.BlockSpec(memory_space=pltpu.VMEM)
    moved = sum(v.size * v.dtype.itemsize for v in operands)
    moved += sum(math.prod(shape) * jnp.dtype(dtype).itemsize for shape, dtype in outs)
    room = limit * MIB + moved
    return pl.pallas_call(
        kernel,
        in_specs=smem + [vmem] * len(operands),
        out_specs=[vmem] * len(outs),
        out_shape=[jax.ShapeDtypeStruct(shape, dtype) for shape, dtype in outs],
        scratch_shapes=list(scratch),
        compiler_params=pltpu.CompilerParams(vmem_limit_bytes=room),
        cost_estimate=FREE,
    )(*scalars, *operands)


def chunks(size, step=CHUNK):
    return [slice(i, min(i + step, size)) for i in range(0, size, step)]


def root(values):
    return lax.rsqrt(jnp.mean(values * values, -1, keepdims=True) + epsilon)


def norm_back(values, gain, grad):
    scale = root(values)
    unit = values * scale
    inner = grad * gain
    out = scale * (inner - unit * jnp.mean(inner * unit, -1, keepdims=True))
    return out, jnp.sum(grad * unit, 0, keepdims=True)


def dot(left, right):
    return jnp.dot(left, right, preferred_element_type=f32)


def dot_nt(left, right):
    return lax.dot_general(left, right, NT, preferred_element_type=f32)


def dot_tn(left, right):
    return lax.dot_general(left, right, TN, preferred_element_type=f32)


def qkv_kernel(act_ref, w_ref, cos_ref, sin_ref, q_ref, kv_ref):
    act = act_ref[...]
    for i in range(3):
        for cols in chunks(act.shape[1]):
            prod = dot(act, w_ref[i, :, cols])
            for at in range(cols.start, cols.stop, LANES):
                part = prod[:, at - cols.start : at - cols.start + LANES]
                if i < 2:
                    part = turn(part, cos_ref[...], sin_ref[...])
                if i == 0:
                    part = part * QUERY_SCALE
                part = part.astype(bf16)
                if i == 0:
                    q_ref[:, at : at + LANES] = part
                else:
                    kv_ref[i - 1, :, at : at + LANES] = part


def project_qkv(act, w_qkv, tables):
    rows, width = act.shape
    outs = [((rows, width), bf16), ((2, rows, width), bf16)]
    return in_vmem(qkv_kernel, outs, (act, w_qkv, *tables))


def out_kernel(which, o_ref, w_ref, resid_ref, gain_ref, sum_ref, act_ref):
    o = o_ref[...]
    for cols in chunks(o.shape[1]):
        sum_ref[:, cols] = resid_ref[:, cols].astype(f32) + dot(o, w_ref[:, cols])
    total = sum_ref[...]
    act_ref[...] = (total * root(total) * gain_ref[which : which + 1, :]).astype(bf16)


def project_out(which, o, w_out, resid, gains):
    shape = o.shape
    return in_vmem(
        lambda *refs: out_kernel(which, *refs),
        [(shape, f32), (shape, bf16)],
        (o, w_out, resid, gains),
    )


def ffn_in_kernel(act_ref, w_ref, hidden_ref, silu_ref, slope_ref):
    act = act_ref[...]
    for cols in chunks(hidden_ref.shape[1]):
        gate = dot(act, w_ref[0, :, cols])
        up = dot(act, w_ref[1, :, cols])
        sig = jax.nn.sigmoid(gate)
        silu = gate * sig
        hidden_ref[:, cols] = (silu * up).astype(bf16)
        silu_ref[:, cols] = silu.astype(bf16)
        slope_ref[:, cols] = (up * sig * (1.0 + gate * (1.0 - sig))).astype(bf16)


def ffn_in(act, w_gu):
    shape = (act.shape[0], w_gu.shape[2])
    return in_vmem(ffn_in_kernel, [(shape, bf16)] * 3, (act, w_gu))


def ffn_out_first_kernel(hid_ref, w_ref, sum_ref, gain_ref, next_ref, z_ref, act_ref):
    total = sum_ref[...]
    next_ref[...] = total * root(total) * gain_ref[0:1, :]
    hid = hid_ref[...]
    for cols in chunks(w_ref.shape[1]):
        next_ref[:, cols] += dot(hid, w_ref[:, cols])
    total = next_ref[...]
    z = total * root(total) * gain_ref[2:3, :]
    z_ref[...] = z
    act_ref[...] = (z * root(z) * gain_ref[1:2, :]).astype(bf16)


def ffn_out_first(hidden, w_down, total, gains):
    shape = total.shape
    return in_vmem(
        ffn_out_first_kernel,
        [(shape, f32), (shape, f32), (shape, bf16)],
        (hidden, w_down, total, gains),
    )


def split_rows(start_ref, value_ref, own_ref, send_ref):
    rows = own_ref.shape[0]
    own = pl.multiple_of(start_ref[0], rows)
    send = pl.multiple_of(rows - start_ref[0], rows)
    own_ref[...] = value_ref[pl.ds(own, rows), :]
    send_ref[...] = value_ref[pl.ds(send, rows), :].astype(bf16)


def ffn_out_second_kernel(start_ref, hid_ref, w_ref, sum_ref, own_ref, send_ref, total):
    hid = hid_ref[...]
    for cols in chunks(w_ref.shape[1]):
        total[:, cols] = sum_ref[:, cols] + dot(hid, w_ref[:, cols])
    split_rows(start_ref, total, own_ref, send_ref)


def ffn_out_second(start, hidden, w_down, total):
    rows, width = total.shape
    half = (rows // 2, width)
    return in_vmem(
        ffn_out_second_kernel,
        [(half, f32), (half, bf16)],
        (hidden, w_down, total),
        (start,),
        [pltpu.VMEM(total.shape, f32)],
    )


def ffn_back_kernel(
    post, grad_ref, silu_ref, slope_ref, wd_ref, wgu_ref, wo_ref, sum_ref, gain_ref,
    dgu_ref, total_ref, low_ref, do_ref, dgain_ref,
):
    grad_low = grad_ref[...].astype(bf16)
    for cols in chunks(wd_ref.shape[0]):
        hid = dot_nt(grad_low, wd_ref[cols, :])
        dgu_ref[0, :, cols] = (hid * slope_ref[:, cols].astype(f32)).astype(bf16)
        dgu_ref[1, :, cols] = (hid * silu_ref[:, cols].astype(f32)).astype(bf16)
    for cols in chunks(total_ref.shape[1]):
        back = dot_nt(dgu_ref[0], wgu_ref[0, cols, :])
        back += dot_nt(dgu_ref[1], wgu_ref[1, cols, :])
        total_ref[:, cols] = back
    if post:
        out, dgain = norm_back(
            sum_ref[...], gain_ref[0:1, :], grad_ref[...] + total_ref[...]
        )
    else:
        out, dgain = norm_back(sum_ref[...], gain_ref[3:4, :], total_ref[...])
        out = grad_ref[...].astype(f32) + out
    dgain_ref[...] = dgain
    total_ref[...] = out
    low_ref[...] = out.astype(bf16)
    low = low_ref[...]
    for cols in chunks(total_ref.shape[1]):
        do_ref[:, cols] = dot_nt(low, wo_ref[cols, :]).astype(bf16)


def ffn_back(post, grad, silu, slope, w_down, w_gu, w_out, total, gains):
    shape = total.shape
    outs = [
        ((2,) + silu.shape, bf16), (shape, f32), (shape, bf16), (shape, bf16),
        ((1, shape[1]), f32),
    ]
    return in_vmem(
        lambda *refs: ffn_back_kernel(post, *refs),
        outs,
        (grad, silu, slope, w_down, w_gu, w_out, total, gains),
    )


def join_kernel(a_ref, b_ref, out_ref):
    out_ref[...] = (a_ref[...].astype(f32) + b_ref[...].astype(f32)).astype(bf16)


def join(a, b):
    return in_vmem(join_kernel, [(a.shape, bf16)], (a, b))[0]


def join_parts_kernel(a_ref, dk_ref, dv_ref, cos_ref, sin_ref, out_ref):
    for at in range(0, a_ref.shape[2], LANES):
        cols = slice(at, at + LANES)
        total = a_ref[0, :, cols].astype(f32) + dk_ref[:, cols].astype(f32)
        out_ref[0, :, cols] = turn(total, cos_ref[...], -sin_ref[...]).astype(bf16)
    out_ref[1] = (a_ref[1].astype(f32) + dv_ref[...].astype(f32)).astype(bf16)


def join_parts(a, *rest):
    return in_vmem(join_parts_kernel, [(a.shape, bf16)], (a, *rest))[0]


def in_parts(send, values):
    return [send(v) for v in values]


def qkv_back_product(dq_ref, dkv_ref, w_ref, out_ref, base_ref):
    dq, dk, dv = dq_ref[...], dkv_ref[0], dkv_ref[1]
    for cols in chunks(out_ref.shape[1]):
        back = dot_nt(dq, w_ref[0, cols, :])
        back += dot_nt(dk, w_ref[1, cols, :])
        back += dot_nt(dv, w_ref[2, cols, :])
        if base_ref is not None:
            back += base_ref[:, cols]
        out_ref[:, cols] = back


def qkv_back_second_kernel(
    dq_ref, dkv_ref, w_ref, grad_ref, z_ref, sum_ref, gain_ref,
    out_ref, low_ref, dgain_ref,
):
    qkv_back_product(dq_ref, dkv_ref, w_ref, out_ref, None)
    back, dgain = norm_back(z_ref[...], gain_ref[1:2, :], out_ref[...])
    dgain_ref[0:1, :] = dgain
    out, dgain = norm_back(sum_ref[...], gain_ref[2:3, :], grad_ref[...] + back)
    dgain_ref[1:2, :] = dgain
    out_ref[...] = out
    low_ref[...] = out.astype(bf16)


def qkv_back_second(dq, dkv, w_qkv, grad, z, total, gains):
    shape = grad.shape
    return in_vmem(
        qkv_back_second_kernel,
        [(shape, f32), (shape, bf16), ((2, shape[1]), f32)],
        (dq, dkv, w_qkv, grad, z, total, gains),
    )


def qkv_back_first_kernel(
    start_ref, dq_ref, dkv_ref, w_ref, grad_ref, own_ref, send_ref, total
):
    qkv_back_product(dq_ref, dkv_ref, w_ref, total, grad_ref)
    split_rows(start_ref, total, own_ref, send_ref)


def qkv_back_first(start, dq, dkv, w_qkv, grad):
    rows, width = grad.shape
    half = (rows // 2, width)
    return in_vmem(
        qkv_back_first_kernel,
        [(half, f32), (half, bf16)],
        (dq, dkv, w_qkv, grad),
        (start,),
        [pltpu.VMEM(grad.shape, f32)],
    )


def merge_kernel(y_ref, own_ref, got_ref, out_ref):
    out_ref[y_ref[0], 0] = own_ref[...]
    out_ref[1 - y_ref[0], 0] = got_ref[...].astype(f32)


def merge(y, own, got):
    return in_vmem(merge_kernel, [((2, 1) + own.shape, f32)], (own, got), (y,))[0]


def key_tiles(role, block_index, own, other):
    if role == 0:
        table = [(own, 0), (other, 0), (other, 1), (own, 1)]
    else:
        table = [(other, 0), (own, 0), (own, 1), (other, 1)]
    return table[: block_index + 1]


def both_heads(values):
    lane = lax.broadcasted_iota(jnp.int32, values.shape, 1)
    zero = jnp.zeros_like(values)
    return jnp.concatenate(
        [jnp.where(lane < HD, values, zero), jnp.where(lane >= HD, values, zero)], 0
    )


def own_heads(values, rows):
    return jnp.concatenate([values[:HD, :rows], values[HD:, rows:]], 0)


def allowed_keys(rows):
    key = lax.broadcasted_iota(jnp.int32, (rows, rows), 0)
    query = lax.broadcasted_iota(jnp.int32, (rows, rows), 1)
    return jnp.concatenate([key <= query] * 2, 1)


def attn_fwd_kernel(role_ref, q_ref, ko_ref, vo_ref, kt_ref, vt_ref, o_ref, lse_ref):
    rows = q_ref.shape[0] // 2
    own, other = (0, ko_ref, vo_ref), (1, kt_ref, vt_ref)

    def one(role, j, turned):
        block_index = (role, 3 - role)[j]
        tiles = key_tiles(role, block_index, own, other)
        here = slice(j * rows, (j + 1) * rows)
        pair = both_heads(q_ref[here, :])
        allowed = allowed_keys(rows)
        scores = []
        top = None
        for t, ((_, k_ref, _), i) in enumerate(tiles):
            s = dot_nt(k_ref[0, i * rows : (i + 1) * rows, :], pair)
            if t == block_index:
                s = jnp.where(allowed, s, masked_value)
            scores.append(s)
            tile_top = jnp.max(s, 0, keepdims=True)
            top = tile_top if top is None else jnp.maximum(top, tile_top)
        total = None
        mixed = None
        for s, ((which, _, _), i) in zip(scores, tiles):
            p = jnp.exp2(s - top)
            part = jnp.sum(p, 0, keepdims=True)
            total = part if total is None else total + part
            m = dot(turned[(which, i)], p.astype(bf16))
            mixed = m if mixed is None else mixed + m
        mixed = mixed * (1.0 / total)
        sums = top + jnp.log2(total)
        for h in range(2):
            lse_ref[0, h : h + 1, here] = sums[:, h * rows : (h + 1) * rows]
        o_ref[here, :] = own_heads(mixed, rows).T.astype(bf16)

    for role in range(2):

        @pl.when(role_ref[0] == role)
        def _(role=role):
            turned = {}
            for which, _, v_ref in (own, other):
                for i in range(2):
                    turned[(which, i)] = v_ref[0, i * rows : (i + 1) * rows, :].T
            for j in range(2):
                one(role, j, turned)


def attn_forward(role, q, kv_own, kv_other):
    rows, width = q.shape
    pairs = width // LANES
    smem = pl.BlockSpec(memory_space=pltpu.SMEM)
    act = pl.BlockSpec((rows, LANES), lambda i: (0, i))

    def kv(which):
        return pl.BlockSpec((1, rows, LANES), lambda i: (which, 0, i))

    return pl.pallas_call(
        attn_fwd_kernel,
        grid=(pairs,),
        in_specs=[smem, act, kv(0), kv(1), kv(0), kv(1)],
        out_specs=[act, pl.BlockSpec((1, 2, rows), lambda i: (i, 0, 0))],
        out_shape=[
            jax.ShapeDtypeStruct((rows, width), bf16),
            jax.ShapeDtypeStruct((pairs, 2, rows), f32),
        ],
        compiler_params=pltpu.CompilerParams(vmem_limit_bytes=12 * MIB),
        cost_estimate=FREE,
    )(role, q, kv_own, kv_own, kv_other, kv_other)


def attn_bwd_kernel(
    role_ref, q_ref, ko_ref, vo_ref, kt_ref, vt_ref, lse_ref, o_ref, do_ref,
    cos_ref, sin_ref, dq_ref, down_ref, *rest
):
    *other_refs, acc_ref = rest
    rows = q_ref.shape[0] // 2
    own, other = (0, ko_ref, vo_ref), (1, kt_ref, vt_ref)

    def one(role, j, seen, turned):
        block_index = (role, 3 - role)[j]
        tiles = key_tiles(role, block_index, own, other)
        here = slice(j * rows, (j + 1) * rows)
        pair, grads = both_heads(q_ref[here, :]), both_heads(do_ref[here, :])
        allowed = allowed_keys(rows)
        both = (do_ref[here, :].astype(f32) * o_ref[here, :].astype(f32)).T
        delta = jnp.concatenate(
            [jnp.sum(both[h * HD : (h + 1) * HD, :], 0, keepdims=True) for h in range(2)], 1
        )
        lse = jnp.concatenate([lse_ref[0, h : h + 1, here] for h in range(2)], 1)
        total = None
        for t, ((which, k_ref, v_ref), i) in enumerate(tiles):
            there = slice(i * rows, (i + 1) * rows)
            s = dot_nt(k_ref[0, there, :], pair)
            p = jnp.exp2(s - lse)
            if t == block_index:
                p = jnp.where(allowed, p, 0.0)
            dp = dot_nt(v_ref[0, there, :], grads)
            ds = (p * (dp - delta)).astype(bf16)
            dv = dot(p.astype(bf16), grads)
            dk = dot(ds, pair)
            dq = dot(turned[(which, i)], ds)
            total = dq if total is None else total + dq
            key = (which, i)
            if key in seen:
                acc_ref[which, 0, there, :] += dk
                acc_ref[which, 1, there, :] += dv
            else:
                seen.add(key)
                acc_ref[which, 0, there, :] = dk
                acc_ref[which, 1, there, :] = dv
        grad = own_heads(total, rows).T * (HD**-0.5)
        dq_ref[here, :] = turn(grad, cos_ref[here, :], -sin_ref[here, :]).astype(bf16)

    for role in range(2):

        @pl.when(role_ref[0] == role)
        def _(role=role):
            seen, turned = set(), {}
            for which, k_ref, _ in (own, other):
                for i in range(2):
                    turned[(which, i)] = k_ref[0, i * rows : (i + 1) * rows, :].T
            for j in range(2):
                one(role, j, seen, turned)
            for which in range(2):
                for i in range(2):
                    if (which, i) not in seen:
                        zeros = jnp.zeros((2, rows, LANES), f32)
                        acc_ref[which, :, i * rows : (i + 1) * rows, :] = zeros

    down_ref[0] = (acc_ref[0, 0] * math.log(2.0)).astype(bf16)
    down_ref[1] = acc_ref[0, 1].astype(bf16)
    other_refs[0][...] = (acc_ref[1, 0] * math.log(2.0)).astype(bf16)
    other_refs[1][...] = acc_ref[1, 1].astype(bf16)


def attn_backward(role, q, kv_own, kv_other, lse, o, do, tables):
    rows, width = q.shape
    pairs = width // LANES
    smem = pl.BlockSpec(memory_space=pltpu.SMEM)
    act = pl.BlockSpec((rows, LANES), lambda i: (0, i))
    tab = pl.BlockSpec((rows, LANES), lambda i: (0, 0))
    two = pl.BlockSpec((2, rows, LANES), lambda i: (0, 0, i))

    def kv(which):
        return pl.BlockSpec((1, rows, LANES), lambda i: (which, 0, i))

    return pl.pallas_call(
        attn_bwd_kernel,
        grid=(pairs,),
        in_specs=[
            smem, act, kv(0), kv(1), kv(0), kv(1),
            pl.BlockSpec((1, 2, rows), lambda i: (i, 0, 0)), act, act, tab, tab,
        ],
        out_specs=[act, two, act, act],
        out_shape=[
            jax.ShapeDtypeStruct((rows, width), bf16),
            jax.ShapeDtypeStruct((2, rows, width), bf16),
        ]
        + [jax.ShapeDtypeStruct((rows, width), bf16)] * 2,
        scratch_shapes=[pltpu.VMEM((2, 2, rows, LANES), f32)],
        compiler_params=pltpu.CompilerParams(vmem_limit_bytes=12 * MIB),
        cost_estimate=FREE,
    )(role, q, kv_own, kv_own, kv_other, kv_other, lse, o, do, *tables)


class Places:
    def __init__(self):
        self.count = lax.axis_size("fsdp")
        self.seq = lax.axis_size("seq")
        self.f = lax.axis_index("fsdp")
        self.s = lax.axis_index("seq")
        self.far, self.near = self.f // 2, self.f % 2
        self.shifts = self.count // 2
        self.core = self.s % 2
        self.y = self.s // 2

    def over_far(self, value):
        groups = [list(range(i, self.count, 2)) for i in range(2)]
        return lax.all_to_all(value, "fsdp", 0, 0, axis_index_groups=groups, tiled=True)

    def over_near(self, value):
        return lax.ppermute(value, "fsdp", [(i, i ^ 1) for i in range(self.count)])

    def over_core(self, value):
        return lax.ppermute(value, "seq", [(i, i ^ 1) for i in range(self.seq)])

    def over_y(self, value):
        return lax.ppermute(value, "seq", [(i, i ^ 2) for i in range(self.seq)])

    def mirror(self, value):
        last = self.seq - 1
        return lax.ppermute(value, "seq", [(i, last - i) for i in range(self.seq)])


def after(value, *others):
    return lax.optimization_barrier((value,) + others)[0]


def pick(value, index, axis):
    return lax.dynamic_index_in_dim(value, index, axis, keepdims=False)


def place_kernel(plans, unit_ref, slot_ref, *refs):
    count = len(plans)
    pieces, outs = refs[:count], refs[count:]
    for a, (piece, plan) in enumerate(zip(pieces, plans)):
        for k in range(piece.shape[0]):
            unit = unit_ref[a * piece.shape[0] + k]
            for out_index, slot, start, size, by_rows in plan:
                number = unit * 2 + slot_ref[a] if by_rows else unit
                row = pl.multiple_of(number * size, 16)
                if isinstance(slot, tuple):
                    slot = slot_ref[a] * slot[0] + slot[1]
                outs[out_index][slot, pl.ds(row, size), :] = piece[k, start : start + size, :]


def place(order, out_shapes, *groups):
    plans, pieces, units, slots = [], [], [], []
    for gather, plan in groups:
        for value, unit, slot in gather.pieces():
            plans.append(plan)
            pieces.append(value)
            units.append(unit)
            slots.append(slot)
    units = jnp.concatenate(units).astype(jnp.int32)
    slots = jnp.stack(slots).astype(jnp.int32)

    def call(*values):
        return in_vmem(
            lambda *refs: place_kernel(plans, *refs),
            [(shape, bf16) for shape in out_shapes],
            values,
            (units, slots),
        )

    return order(call, *pieces)


class Order:
    def __init__(self):
        self.last = ()

    def wait(self, *values):
        self.last = self.last + values

    def __call__(self, function, *operands):
        if self.last:
            operands = (after(operands[0], *self.last),) + operands[1:]
        out = function(*operands)
        self.last = (out[0] if isinstance(out, (tuple, list)) else out,)
        return out


class Gather:
    def __init__(self, at, order, own, by_y=False):
        self.at, self.order, self.own, self.by_y = at, order, own, by_y

    def far(self):
        own = after(self.own, *self.order.last) if self.order.last else self.own
        self.here = self.at.over_far(jnp.broadcast_to(own[None], (self.at.shifts,) + own.shape))

    def arrived(self, value):
        value = after(value, *self.order.last)
        self.order.wait(value)
        return value

    def near(self):
        self.here = self.arrived(self.here)
        self.there = self.at.over_near(self.here)
        if self.by_y:
            self.here_y = self.at.over_y(self.here)
        self.here_core = self.at.over_core(self.here)

    def middle(self):
        self.there = self.arrived(self.there)
        self.there_y = self.at.over_y(self.there)
        self.there_core = self.at.over_core(self.there)
        self.here_y = self.arrived(self.here_y)
        self.here_y_core = self.at.over_core(self.here_y)

    def cores(self):
        if self.by_y:
            self.there_y = self.arrived(self.there_y)
            self.there_y_core = self.at.over_core(self.there_y)
        else:
            self.there = self.arrived(self.there)
            self.there_core = self.at.over_core(self.there)

    def pieces(self):
        at = self.at
        far = jnp.arange(at.shifts, dtype=jnp.int32)
        values = [(self.here, self.there, self.here_core, self.there_core)]
        if self.by_y:
            more = (self.here_y, self.there_y, self.here_y_core, self.there_y_core)
            values.append(more)
        for side, four in enumerate(values):
            for i, value in enumerate(four):
                near, core = at.near ^ (i % 2), at.core ^ (i // 2)
                yield value, (far * 2 + near) * 2 + core, at.y ^ side


class GatherWhole(Gather):
    def far(self):
        rows = self.own.shape[0]
        own = after(self.own, *self.order.last)
        here = lax.all_gather(own, "fsdp", axis=0, tiled=True)
        self.here = here.reshape(self.at.count, rows, here.shape[1])

    def near(self):
        self.here = self.arrived(self.here)
        if self.by_y:
            self.here_y = self.at.over_y(self.here)
        self.here_core = self.at.over_core(self.here)

    def cores(self):
        if self.by_y:
            self.here_y = self.arrived(self.here_y)
            self.here_y_core = self.at.over_core(self.here_y)
        else:
            self.here_core = self.arrived(self.here_core)

    def pieces(self):
        at = self.at
        shard = jnp.arange(at.count, dtype=jnp.int32)
        yield self.here, shard * 2 + at.core, at.y
        yield self.here_core, shard * 2 + 1 - at.core, at.y
        if not self.by_y:
            return
        yield self.here_y, shard * 2 + at.core, 1 - at.y
        yield self.here_y_core, shard * 2 + 1 - at.core, 1 - at.y


class Group:
    def __init__(self, weights, count, extra=0, apart=False):
        self.weights, self.count, self.extra, self.apart = weights, count, extra, apart
        self.cols = [n // 2 for *_, n in weights]
        self.tiles = [c // LANES for c in self.cols]
        self.parts = [w[3] // count for w in weights]
        self.bases, self.offsets = [], []
        base = offset = 0
        for w, tiles, part in zip(weights, self.tiles, self.parts):
            self.bases.append(base)
            self.offsets.append(offset)
            base += w[3] * tiles
            offset += part * tiles
        self.extra_base, self.extra_offset = base, offset
        self.rows = offset + extra

    def halves(self):
        extra = [(self.extra * self.count, LANES)] if self.extra else []
        if self.apart:
            return [(w[3] * t, LANES) for w, t in zip(self.weights, self.tiles)] + extra
        return [(self.extra_base, LANES)] + extra

    def tile(self, refs, i, tile):
        rows = self.weights[i][3]
        if self.apart:
            return refs[i].at[tile * rows : (tile + 1) * rows, :]
        start = self.bases[i] + tile * rows
        return refs[0].at[start : start + rows, :]

    def products(self, half, lefts, rights):
        for i, (a, g, slot, _, _) in enumerate(self.weights):
            left = lefts[a][...]
            right = rights[g] if slot is None else rights[g].at[slot]
            step = 256 if self.cols[i] % 256 == 0 else self.cols[i]
            for start in range(0, self.cols[i], step):
                col = pl.multiple_of(half * self.cols[i] + start, LANES)
                yield i, start // LANES, dot_tn(left, right[:, pl.ds(col, step)])


def theirs_kernel(group, n_left, n_right, place_ref, *refs):
    lefts, rights = refs[:n_left], refs[n_left : n_left + n_right]
    rest = refs[n_left + n_right :]
    outs = rest[1:] if group.extra else rest
    for i, tile, value in group.products(1 - place_ref[0], lefts, rights):
        for j in range(value.shape[1] // LANES):
            group.tile(outs, i, tile + j)[...] = value[:, j * LANES : (j + 1) * LANES].astype(
                bf16
            )
    if group.extra:
        outs[-1][...] = rest[0][...].astype(bf16)


def mine_kernel(group, by_y, n_left, n_right, place_ref, *refs):
    lefts, rights = refs[:n_left], refs[n_left : n_left + n_right]
    rest = refs[n_left + n_right :]
    keep_ref, send_ref, scratch = rest[-3:]
    gots = rest[1:-3] if group.extra else rest[:-3]
    side = place_ref[3] if by_y else place_ref[1]

    def hand_out(size, cols, offset):
        half = size // 2 if by_y else size
        first = offset // 2 if by_y else offset
        for index in range(keep_ref.shape[0]):
            for ref, own in ((keep_ref, side), (send_ref, 1 - side)):
                row = pl.multiple_of((index * 2 + own) * half, 8)
                for j in range(cols // LANES):
                    ref[index, first + j * half : first + (j + 1) * half, :] = scratch[
                        pl.ds(row, half), j * LANES : (j + 1) * LANES
                    ].astype(bf16)

    for i, tile, value in group.products(place_ref[0], lefts, rights):
        rows, cols = value.shape
        for j in range(cols // LANES):
            got = group.tile(gots, i, tile + j)[...].astype(f32)
            cut = slice(j * LANES, (j + 1) * LANES)
            scratch[:rows, cut] = value[:, cut] + got
        part = group.parts[i]
        hand_out(part, cols, group.offsets[i] + tile * part)
    if group.extra:
        rows = group.extra * group.count
        scratch[:rows, :LANES] = rest[0][...].astype(f32) + gots[-1][...].astype(f32)
        hand_out(group.extra, LANES, group.extra_offset)


def mine_all_kernel(group, n_left, n_right, place_ref, *refs):
    lefts, rights = refs[:n_left], refs[n_left : n_left + n_right]
    gots, out_ref = refs[n_left + n_right : -1], refs[-1]
    for i, tile, value in group.products(place_ref[0], lefts, rights):
        part = group.parts[i]
        for j in range(value.shape[1] // LANES):
            got = group.tile(gots, i, tile + j)[...].astype(f32)
            total = value[:, j * LANES : (j + 1) * LANES] + got
            first = group.offsets[i] + (tile + j) * part
            for shard in range(group.count):
                out_ref[shard, first : first + part, :] = total[
                    shard * part : (shard + 1) * part, :
                ].astype(bf16)


def split_near_kernel(place_ref, keep_ref, got_ref, stay_ref, leave_ref):
    near = place_ref[1]
    for far in range(stay_ref.shape[0]):
        for ref, side in ((stay_ref, near), (leave_ref, 1 - near)):
            shard = 2 * far + side
            ref[far] = (keep_ref[shard].astype(f32) + got_ref[shard].astype(f32)).astype(bf16)


def sum_kernel(parts_ref, out_ref):
    total = parts_ref[0].astype(f32)
    for k in range(1, parts_ref.shape[0]):
        total = total + parts_ref[k].astype(f32)
    out_ref[...] = total.astype(bf16)


class Reduce:
    def __init__(self, at, order, group, by_y, whole, lefts, rights, extra=()):
        self.at, self.order, self.group = at, order, group
        self.by_y, self.whole = by_y, whole
        self.operands = (*lefts, *rights, *extra)
        self.counts = (len(lefts), len(rights))

    def theirs(self):
        group = self.group

        def call(*operands):
            return in_vmem(
                lambda *refs: theirs_kernel(group, *self.counts, *refs),
                [(shape, bf16) for shape in group.halves()],
                operands,
                (self.at.scalars,),
            )

        self.got = in_parts(self.at.over_core, self.order(call, *self.operands))

    def mine(self):
        group, at = self.group, self.at
        shape = (at.count, group.rows // 2) if self.by_y else (at.shifts, group.rows)
        shape += (LANES,)
        tall = max(w[3] for w in group.weights)
        wide = max(c if c % 256 else 256 for c in group.cols)

        def call(*operands):
            return in_vmem(
                lambda *refs: mine_kernel(group, self.by_y, *self.counts, *refs),
                [(shape, bf16), (shape, bf16)],
                operands,
                (at.scalars,),
                [pltpu.VMEM((tall, wide), f32)],
                limit=10,
            )

        if self.whole and not self.by_y:
            total = self.order(self.mine_all, *self.operands, *self.got)
            self.got = lax.psum_scatter(total, "fsdp", scatter_dimension=0, tiled=True)
            return
        self.keep, send = self.order(call, *self.operands, *self.got)
        self.got = at.over_y(send) if self.by_y else at.over_near(send)

    def mine_all(self, *operands):
        group = self.group
        return in_vmem(
            lambda *refs: mine_all_kernel(group, *self.counts, *refs),
            [((self.at.count, group.rows, LANES), bf16)],
            operands,
            (self.at.scalars,),
            limit=10,
        )[0]

    def split(self):
        if self.whole:
            total = self.order(join, self.keep, self.got)
            self.got = lax.psum_scatter(total, "fsdp", scatter_dimension=0, tiled=True)
            return
        shape = (self.at.shifts,) + self.keep.shape[1:]

        def call(*operands):
            return in_vmem(
                split_near_kernel,
                [(shape, bf16), (shape, bf16)],
                operands,
                (self.at.scalars,),
            )

        self.keep, send = self.order(call, self.keep, self.got)
        self.got = self.at.over_near(send)

    def deal(self):
        self.got = self.at.over_far(self.order(join, self.keep, self.got))

    def gather(self):
        def call(parts):
            return in_vmem(sum_kernel, [(parts.shape[1:], bf16)], (parts,))[0]

        if self.whole:
            self.total = after(self.got, *self.order.last)[0]
            self.order.wait(self.total)
        else:
            self.total = self.order(call, self.got)
        self.got = self.at.over_y(self.total)
        if self.by_y:
            self.other = self.at.over_core(self.total)

    def finish(self):
        if self.by_y:
            self.got = after(self.got, *self.order.last)
            self.order.wait(self.got)
            self.got_other = self.at.over_core(self.got)
        else:
            self.total = self.order(join, self.total, self.got)
            self.other = self.at.over_core(self.total)

    def flats(self):
        if self.by_y:
            return (self.total, self.other, self.got, self.got_other)
        return (self.total, self.other)


def unpack_kernel(reduces, plan, extra, place_ref, *refs):
    flats, at = [], 0
    for r in reduces:
        flats.append(refs[at : at + len(r.flats())])
        at += len(r.flats())
    outs = refs[at:]

    for out_ref, blocks in zip(outs, plan):
        for block, (g, i) in enumerate(blocks):
            group, ways = reduces[g].group, len(flats[g]) // 2
            cols, part = group.cols[i], group.parts[i] // ways
            for n, flat in enumerate(flats[g]):
                first = (place_ref[0] ^ (n % 2)) * cols
                row = pl.multiple_of((place_ref[3] ^ (n // 2)) * part, 8) if ways == 2 else 0
                for j in range(group.tiles[i]):
                    start = group.offsets[i] // ways + j * part
                    col = pl.multiple_of(first + j * LANES, LANES)
                    out_ref[block, pl.ds(row, part), pl.ds(col, LANES)] = flat[
                        start : start + part, :
                    ].astype(f32)

    if extra is not None:
        group = reduces[extra].group
        outs[-1][...] = flats[extra][0][group.extra_offset :, :].astype(f32)


def unpack(at, order, reduces, plan, extra=None):
    outs = []
    for blocks in plan:
        group, i = reduces[blocks[0][0]].group, blocks[0][1]
        outs.append(((len(blocks), group.parts[i], 2 * group.cols[i]), f32))
    if extra is not None:
        outs.append(((reduces[extra].group.extra, LANES), f32))

    def call(*operands):
        return in_vmem(
            lambda *refs: unpack_kernel(reduces, plan, extra, *refs),
            outs,
            operands,
            (at.scalars,),
        )

    return order(call, *[v for r in reduces for v in r.flats()])


def per_device(
    hidden_in,
    cotangent,
    attn_gain,
    query_weight,
    key_weight,
    value_weight,
    out_weight,
    ffn_gain,
    gate_weight,
    up_weight,
    down_weight,
):
    at = Places()
    order = Order()
    rows, d = hidden_in.shape[2:]
    ff = gate_weight.shape[2]
    p, q = query_weight.shape[1], down_weight.shape[1]
    assert hidden_in.shape[0] == 2 and at.seq == 4
    direct = p % 32 == 0 and q % 32 == 0
    at.scalars = jnp.stack([at.core, at.near, at.far, at.y]).astype(jnp.int32)

    low = jnp.minimum(at.s, 3 - at.s)
    role = low.astype(jnp.int32).reshape(1)
    first_is_own = at.s < 2
    own_start = jnp.where(first_is_own, 0, rows).astype(jnp.int32).reshape(1)
    y = at.y.astype(jnp.int32).reshape(1)

    def spread(value, *waits):
        own = pick(value[:, 0], at.y, 0)
        got = at.mirror(after(pick(value[:, 0], 1 - at.y, 0), *waits))
        return jnp.concatenate(
            [jnp.where(first_is_own, own, got), jnp.where(first_is_own, got, own)]
        )

    def tables_of(first):
        steps = jnp.arange(rows, dtype=jnp.int32)
        return rope_tables(
            jnp.concatenate([first * rows + steps, (3 - first) * rows + steps])
        )

    tables = tables_of(low)
    attn_shards = jnp.stack([query_weight, key_weight, value_weight, out_weight], 1)
    gu_shards = jnp.stack([gate_weight, up_weight], 1)
    gain_shards = jnp.concatenate([attn_gain, ffn_gain])


    act = spread(hidden_in)
    cot = spread(cotangent)
    if direct:
        ph, qh = p // 2, q // 2

        def half(value, axis):
            size = value.shape[axis] // 2
            return lax.dynamic_slice_in_dim(value, at.core * size, size, axis)

        attn_half, gu_half, down_half = half(attn_shards, 2), half(gu_shards, 2), half(down_weight, 1)
        gain_rows = jnp.zeros((16, d), bf16).at[0, : 4 * p].set(gain_shards.reshape(4 * p))
        attn_part = pick(attn_half[0].reshape(2, 2 * ph, d), at.y, 0)
        a0 = Gather(at, order, jnp.concatenate([attn_part, gain_rows]), True)
        gu0 = Gather(at, order, pick(gu_half[0], at.y, 0), True)
        d0 = Gather(at, order, pick(down_half[0].reshape(2, qh // 2, d), at.y, 0), True)
        da1 = GatherWhole(
            at, order, jnp.concatenate([down_half[1], attn_half[1].reshape(4 * ph, d)])
        )
        gu1 = GatherWhole(at, order, gu_half[1].reshape(2 * ph, ff))
        a0_plan = [(0, (2, i), i * ph, ph, False) for i in range(2)]
        gu_plan = [(0, (1, 0), 0, ph, False)]
        d0_plan = [(0, 0, 0, qh // 2, True)]
        da1_plan = [(0, i, qh + i * ph, ph, False) for i in range(4)]
        da1_plan += [(1, 0, 0, qh, False)]
        gu1_plan = [(0, i, i * ph, ph, False) for i in range(2)]
        attn_shape, gu_shape, down_shape = (4, d, d), (2, d, ff), (1, ff, d)

        a0.far()
        order.wait(act, cot)
        a0.near()
        gu0.far()
        a0.middle()
        a0.cores()
        gu0.near()
        da1.far()
        gu1.far()
        (w_attn0,) = place(order, [attn_shape], (a0, a0_plan))
        w_out0 = w_attn0[3]
        index = ((jnp.arange(at.count) % 2) ^ at.near) * at.shifts
        index = index + jnp.arange(at.count) // 2
        gain_got = jnp.concatenate(
            [a0.here[:, 2 * ph, : 4 * p], a0.there[:, 2 * ph, : 4 * p]]
        )
        select = jax.nn.one_hot(index, at.count, dtype=f32)
        gains = jnp.dot(select, gain_got.astype(f32), precision=lax.Precision.HIGHEST)
        gains = gains.reshape(at.count, 4, p).transpose(1, 0, 2).reshape(4, d)
    else:

        def whole(value, axis):
            return lax.all_gather(value, "fsdp", axis=axis, tiled=True)

        attn_all, gu_all, down_all = whole(attn_shards, 2), whole(gu_shards, 2), whole(down_weight, 1)
        gains = whole(gain_shards, 1).astype(f32)
        w_attn0, w_out0 = attn_all[0], attn_all[0, 3]

    q0, kv0 = order(lambda *v: project_qkv(*v, tables), act, w_attn0)
    kv0_other = at.over_core(kv0)
    if direct:
        d0.far()
    o0, lse0 = order(lambda *v: attn_forward(role, *v), q0, kv0, kv0_other)
    if direct:
        d0.near()
    sum0, act0 = order(lambda *v: project_out(0, *v), o0, w_out0, act, gains)
    if direct:
        gu0.middle()
        gu0.cores()
        (w_gu0,) = place(order, [gu_shape], (gu0, gu_plan))
    else:
        w_gu0 = gu_all[0]
    hidden0, silu0, slope0 = order(ffn_in, act0, w_gu0)
    if direct:
        d0.middle()
        d0.cores()
        da1.near()
        w_down0 = place(order, [down_shape], (d0, d0_plan))[0][0]
    else:
        w_down0 = down_all[0]
    sum1, z, act1 = order(ffn_out_first, hidden0, w_down0, sum0, gains)
    if direct:
        da1.cores()
        w_attn1, w_down1 = place(order, [attn_shape, down_shape], (da1, da1_plan))
        w_out1, w_down1 = w_attn1[3], w_down1[0]
    else:
        w_attn1, w_out1, w_down1 = attn_all[1], attn_all[1, 3], down_all[1]
    q1, kv1 = order(lambda *v: project_qkv(*v, tables), act1, w_attn1)
    kv1_other = at.over_core(kv1)
    o1, lse1 = order(lambda *v: attn_forward(role, *v), q1, kv1, kv1_other)
    sum2, act2 = order(lambda *v: project_out(3, *v), o1, w_out1, z, gains)
    if direct:
        gu1.near()
        gu1.cores()
        (w_gu1,) = place(order, [gu_shape], (gu1, gu1_plan))
    else:
        w_gu1 = gu_all[1]
    hidden1, silu1, slope1 = order(ffn_in, act2, w_gu1)
    out_own, out_send = order(
        lambda *v: ffn_out_second(own_start, *v), hidden1, w_down1, sum2
    )


    ffn_group = [(0, 0, 0, d, ff), (0, 0, 1, d, ff), (1, 1, None, ff, d), (2, 2, None, d, d)]
    gu_group = [(0, 0, 0, d, ff), (0, 0, 1, d, ff)]
    rest_group = [(0, 0, None, ff, d), (1, 1, None, d, d)]
    qkv_group = [(0, 0, None, d, d), (0, 1, 0, d, d), (0, 1, 1, d, d)]

    def reduce(weights, by_y, whole, *rest):
        group = Group(weights, at.count, 16 * (len(rest) == 3), weights is not ffn_group)
        return Reduce(at, order, group, by_y, whole, *rest)

    dgu1, grad, low1, do1, dgain_f1 = order(
        lambda *v: ffn_back(False, *v), cot, silu1, slope1, w_down1, w_gu1, w_out1, sum2, gains
    )
    if direct:
        r1 = reduce(ffn_group, False, True, (act2, hidden1, o1), (dgu1, cot, low1))
        r1.theirs()
    dq1, dkv1, *dkv1_other = order(
        lambda *v: attn_backward(role, *v, tables),
        q1, kv1, kv1_other, lse1, o1, do1,
    )
    dkv1_got = in_parts(at.over_core, dkv1_other)
    if direct:
        r1.mine()
    dkv1 = order(join_parts, dkv1, *dkv1_got, *tables)
    if direct:
        r2 = reduce(qkv_group, False, False, (act1,), (dq1, dkv1))
        r2.theirs()
    grad, low_mid, dgain_mid = order(
        qkv_back_second, dq1, dkv1, w_attn1, grad, z, sum1, gains
    )
    if direct:
        r2.mine()
    out_got = at.mirror(after(out_send, *order.last))
    dgu0, grad, low0, do0, dgain_a0 = order(
        lambda *v: ffn_back(True, *v), grad, silu0, slope0, w_down0, w_gu0, w_out0, sum0, gains
    )
    layer_out = order(lambda *v: merge(y, *v), out_own, out_got)
    if direct:
        r3 = reduce(gu_group, True, False, (act0,), (dgu0,))
        s3 = reduce(rest_group, False, False, (hidden0, o0), (low_mid, low0))
        r3.theirs()
        s3.theirs()
        r3.mine()
        s3.mine()
    dq0, dkv0, *dkv0_other = order(
        lambda *v: attn_backward(role, *v, tables),
        q0, kv0, kv0_other, lse0, o0, do0,
    )
    dkv0_got = in_parts(at.over_core, dkv0_other)
    if direct:
        r2.deal()
        r3.split()
    dkv0 = order(join_parts, dkv0, *dkv0_got, *tables)
    dgains = jnp.concatenate([dgain_a0, dgain_mid, dgain_f1])
    if direct:
        extra = dgains.reshape(4, at.count, p).transpose(1, 0, 2).reshape(at.count, -1, LANES)
        extra = jnp.pad(extra, ((0, 0), (0, 16 - extra.shape[1]), (0, 0)))
        extra = extra.reshape(at.count * 16, LANES)
        r4 = reduce(qkv_group, False, False, (act,), (dq0, dkv0), (extra,))
        r4.theirs()
        s3.deal()
    in_own, in_send = order(
        lambda *v: qkv_back_first(own_start, *v), dq0, dkv0, w_attn0, grad
    )
    in_got = at.mirror(in_send)

    if direct:
        r4.mine()
        input_grad = order(lambda *v: merge(y, *v), in_own, in_got)
        r3.deal()
        r2.gather()
        r1.gather()
        r2.finish()
        r1.finish()
        s3.gather()
        r4.deal()
        s3.finish()
        r3.gather()
        r3.finish()
        grad_gate, grad_up, grad_down, grad_out = unpack(
            at, order, [r3, s3, r1],
            [[(0, 0), (2, 0)], [(0, 1), (2, 1)], [(1, 0), (2, 2)], [(1, 1), (2, 3)]],
        )
        r4.gather()
        r4.finish()
        *grad_qkv, gain_rows = unpack(
            at, order, [r4, r2], [[(0, i), (1, i)] for i in range(3)], 0
        )
        gain_grads = gain_rows.reshape(-1)[: 4 * p].reshape(4, p)
    else:
        input_grad = merge(y, in_own, in_got)

        def sums(*values):
            total = jnp.stack(values).astype(bf16)
            total = lax.psum_scatter(total, "fsdp", scatter_dimension=1, tiled=True)
            return lax.psum(total, "seq").astype(f32)

        grad_qkv = [
            sums(dot_tn(act, dq0), dot_tn(act1, dq1)),
            sums(dot_tn(act, dkv0[0]), dot_tn(act1, dkv1[0])),
            sums(dot_tn(act, dkv0[1]), dot_tn(act1, dkv1[1])),
        ]
        grad_gate = sums(dot_tn(act0, dgu0[0]), dot_tn(act2, dgu1[0]))
        grad_up = sums(dot_tn(act0, dgu0[1]), dot_tn(act2, dgu1[1]))
        grad_down = sums(dot_tn(hidden0, low_mid), dot_tn(hidden1, cot))
        grad_out = sums(dot_tn(o0, low0), dot_tn(o1, low1))
        gain_grads = lax.psum_scatter(dgains, "fsdp", scatter_dimension=1, tiled=True)
        gain_grads = lax.psum(gain_grads, "seq")
    return (
        layer_out,
        input_grad,
        gain_grads[:2],
        *grad_qkv,
        grad_out,
        gain_grads[2:],
        grad_gate,
        grad_up,
        grad_down,
    )


def solution(mesh):
    tokens = P(None, "fsdp", "seq", None)
    gain = P(None, "fsdp")
    weight = P(None, "fsdp", None)
    return jax.shard_map(
        per_device,
        mesh=mesh,
        in_specs=(tokens, tokens, gain) + (weight,) * 4 + (gain,) + (weight,) * 3,
        out_specs=(tokens, tokens, gain) + (weight,) * 4 + (gain,) + (weight,) * 3,
        check_vma=False,
    )
```

```python
import math

import jax
import jax.numpy as jnp
from jax import lax
from jax.experimental import pallas as pl
from jax.experimental.pallas import tpu as pltpu
from jax.sharding import PartitionSpec as P

HD = 64
LANES = 128
epsilon = 1e-05
masked_value = -1e30
QUERY_SCALE = HD**-0.5 * math.log2(math.e)
bf16 = jnp.bfloat16
f32 = jnp.float32
MIB = 1 << 20
CHUNK = 256
FREE = pl.CostEstimate(flops=1, bytes_accessed=1, transcendentals=0)
NT = (((1,), (1,)), ((), ()))
TN = (((0,), (0,)), ((), ()))


def rope_tables(positions):
    half_dim = HD // 2
    rates = jnp.exp(jnp.arange(half_dim, dtype=f32) * (-2.0 * math.log(10000.0) / HD))
    angles = positions.astype(f32)[:, None] * rates[None, :]
    repeat = LANES // half_dim
    return jnp.tile(jnp.cos(angles), (1, repeat)), jnp.tile(jnp.sin(angles), (1, repeat))


def turn(values, cosine, sine):
    lane = lax.broadcasted_iota(jnp.int32, values.shape, 1)
    first = (lane % HD) < HD // 2
    back = pltpu.roll(values, LANES - HD // 2, 1)
    ahead = pltpu.roll(values, HD // 2, 1)
    return values * cosine + jnp.where(first, -back, ahead) * sine


def in_vmem(kernel, outs, operands, scalars=(), scratch=(), limit=6):
    smem = [pl.BlockSpec(memory_space=pltpu.SMEM)] * len(scalars)
    vmem = pl.BlockSpec(memory_space=pltpu.VMEM)
    moved = sum(v.size * v.dtype.itemsize for v in operands)
    moved += sum(math.prod(shape) * jnp.dtype(dtype).itemsize for shape, dtype in outs)
    room = limit * MIB + moved
    return pl.pallas_call(
        kernel,
        in_specs=smem + [vmem] * len(operands),
        out_specs=[vmem] * len(outs),
        out_shape=[jax.ShapeDtypeStruct(shape, dtype) for shape, dtype in outs],
        scratch_shapes=list(scratch),
        compiler_params=pltpu.CompilerParams(vmem_limit_bytes=room),
        cost_estimate=FREE,
    )(*scalars, *operands)


def chunks(size, step=CHUNK):
    return [slice(i, min(i + step, size)) for i in range(0, size, step)]


def root(values):
    return lax.rsqrt(jnp.mean(values * values, -1, keepdims=True) + epsilon)


def norm_back(values, gain, grad):
    scale = root(values)
    unit = values * scale
    inner = grad * gain
    out = scale * (inner - unit * jnp.mean(inner * unit, -1, keepdims=True))
    return out, jnp.sum(grad * unit, 0, keepdims=True)


def dot(left, right):
    return jnp.dot(left, right, preferred_element_type=f32)


def dot_nt(left, right):
    return lax.dot_general(left, right, NT, preferred_element_type=f32)


def dot_tn(left, right):
    return lax.dot_general(left, right, TN, preferred_element_type=f32)


def qkv_kernel(act_ref, w_ref, cos_ref, sin_ref, *outs):
    act = act_ref[...]
    for i in range(3):
        for cols in chunks(act.shape[1]):
            prod = dot(act, w_ref[i, :, cols])
            for at in range(cols.start, cols.stop, LANES):
                part = prod[:, at - cols.start : at - cols.start + LANES]
                if i < 2:
                    part = turn(part, cos_ref[...], sin_ref[...])
                if i == 0:
                    part = part * QUERY_SCALE
                outs[i][:, at : at + LANES] = part.astype(bf16)


def project_qkv(act, w_qkv, tables):
    rows, width = act.shape
    outs = [((rows, width), bf16)] * 3
    return in_vmem(qkv_kernel, outs, (act, w_qkv, *tables))


def out_kernel(which, o_ref, w_ref, resid_ref, gain_ref, sum_ref, act_ref):
    o = o_ref[...]
    for cols in chunks(o.shape[1]):
        sum_ref[:, cols] = resid_ref[:, cols].astype(f32) + dot(o, w_ref[:, cols])
    total = sum_ref[...]
    act_ref[...] = (total * root(total) * gain_ref[which : which + 1, :]).astype(bf16)


def project_out(which, o, w_out, resid, gains):
    shape = o.shape
    return in_vmem(
        lambda *refs: out_kernel(which, *refs),
        [(shape, f32), (shape, bf16)],
        (o, w_out, resid, gains),
    )


def ffn_in_kernel(act_ref, w_ref, hidden_ref, silu_ref, slope_ref):
    act = act_ref[...]
    for cols in chunks(hidden_ref.shape[1]):
        gate = dot(act, w_ref[0, :, cols])
        up = dot(act, w_ref[1, :, cols])
        sig = jax.nn.sigmoid(gate)
        silu = gate * sig
        hidden_ref[:, cols] = (silu * up).astype(bf16)
        silu_ref[:, cols] = silu.astype(bf16)
        slope_ref[:, cols] = (up * sig * (1.0 + gate * (1.0 - sig))).astype(bf16)


def ffn_in(act, w_gu):
    shape = (act.shape[0], w_gu.shape[2])
    return in_vmem(ffn_in_kernel, [(shape, bf16)] * 3, (act, w_gu))


def ffn_out_first_kernel(hid_ref, w_ref, sum_ref, gain_ref, next_ref, z_ref, act_ref):
    total = sum_ref[...]
    next_ref[...] = total * root(total) * gain_ref[0:1, :]
    hid = hid_ref[...]
    for cols in chunks(w_ref.shape[1]):
        next_ref[:, cols] += dot(hid, w_ref[:, cols])
    total = next_ref[...]
    z = total * root(total) * gain_ref[2:3, :]
    z_ref[...] = z
    act_ref[...] = (z * root(z) * gain_ref[1:2, :]).astype(bf16)


def ffn_out_first(hidden, w_down, total, gains):
    shape = total.shape
    return in_vmem(
        ffn_out_first_kernel,
        [(shape, f32), (shape, f32), (shape, bf16)],
        (hidden, w_down, total, gains),
    )


def split_rows(start_ref, value_ref, own_ref, send_ref):
    rows = own_ref.shape[0]
    own = pl.multiple_of(start_ref[0], rows)
    send = pl.multiple_of(rows - start_ref[0], rows)
    own_ref[...] = value_ref[pl.ds(own, rows), :]
    send_ref[...] = value_ref[pl.ds(send, rows), :].astype(bf16)


def ffn_out_second_kernel(start_ref, hid_ref, w_ref, sum_ref, own_ref, send_ref, total):
    hid = hid_ref[...]
    for cols in chunks(w_ref.shape[1]):
        total[:, cols] = sum_ref[:, cols] + dot(hid, w_ref[:, cols])
    split_rows(start_ref, total, own_ref, send_ref)


def ffn_out_second(start, hidden, w_down, total):
    rows, width = total.shape
    half = (rows // 2, width)
    return in_vmem(
        ffn_out_second_kernel,
        [(half, f32), (half, bf16)],
        (hidden, w_down, total),
        (start,),
        [pltpu.VMEM(total.shape, f32)],
    )


def ffn_back_kernel(
    post, grad_ref, silu_ref, slope_ref, wd_ref, wgu_ref, wo_ref, sum_ref, gain_ref,
    dgu_ref, total_ref, low_ref, do_ref, dgain_ref,
):
    grad_low = grad_ref[...].astype(bf16)
    for cols in chunks(wd_ref.shape[0]):
        hid = dot_nt(grad_low, wd_ref[cols, :])
        dgu_ref[0, :, cols] = (hid * slope_ref[:, cols].astype(f32)).astype(bf16)
        dgu_ref[1, :, cols] = (hid * silu_ref[:, cols].astype(f32)).astype(bf16)
    for cols in chunks(total_ref.shape[1]):
        back = dot_nt(dgu_ref[0], wgu_ref[0, cols, :])
        back += dot_nt(dgu_ref[1], wgu_ref[1, cols, :])
        total_ref[:, cols] = back
    if post:
        out, dgain = norm_back(
            sum_ref[...], gain_ref[0:1, :], grad_ref[...] + total_ref[...]
        )
    else:
        out, dgain = norm_back(sum_ref[...], gain_ref[3:4, :], total_ref[...])
        out = grad_ref[...].astype(f32) + out
    dgain_ref[...] = dgain
    total_ref[...] = out
    low_ref[...] = out.astype(bf16)
    low = low_ref[...]
    for cols in chunks(total_ref.shape[1]):
        do_ref[:, cols] = dot_nt(low, wo_ref[cols, :]).astype(bf16)


def ffn_back(post, grad, silu, slope, w_down, w_gu, w_out, total, gains):
    shape = total.shape
    outs = [
        ((2,) + silu.shape, bf16), (shape, f32), (shape, bf16), (shape, bf16),
        ((1, shape[1]), f32),
    ]
    return in_vmem(
        lambda *refs: ffn_back_kernel(post, *refs),
        outs,
        (grad, silu, slope, w_down, w_gu, w_out, total, gains),
    )


def join_kernel(a_ref, b_ref, out_ref):
    out_ref[...] = (a_ref[...].astype(f32) + b_ref[...].astype(f32)).astype(bf16)


def join(a, b):
    return in_vmem(join_kernel, [(a.shape, bf16)], (a, b))[0]


def join_parts_kernel(a_ref, dk_ref, dv_ref, cos_ref, sin_ref, out_ref):
    for at in range(0, a_ref.shape[2], LANES):
        cols = slice(at, at + LANES)
        total = a_ref[0, :, cols].astype(f32) + dk_ref[:, cols].astype(f32)
        out_ref[0, :, cols] = turn(total, cos_ref[...], -sin_ref[...]).astype(bf16)
    out_ref[1] = (a_ref[1].astype(f32) + dv_ref[...].astype(f32)).astype(bf16)


def join_parts(a, *rest):
    return in_vmem(join_parts_kernel, [(a.shape, bf16)], (a, *rest))[0]


def in_parts(send, values):
    return [send(v) for v in values]


def qkv_back_product(dq_ref, dkv_ref, w_ref, out_ref, base_ref):
    dq, dk, dv = dq_ref[...], dkv_ref[0], dkv_ref[1]
    for cols in chunks(out_ref.shape[1]):
        back = dot_nt(dq, w_ref[0, cols, :])
        back += dot_nt(dk, w_ref[1, cols, :])
        back += dot_nt(dv, w_ref[2, cols, :])
        if base_ref is not None:
            back += base_ref[:, cols]
        out_ref[:, cols] = back


def qkv_back_second_kernel(
    dq_ref, dkv_ref, w_ref, grad_ref, z_ref, sum_ref, gain_ref,
    out_ref, low_ref, dgain_ref,
):
    qkv_back_product(dq_ref, dkv_ref, w_ref, out_ref, None)
    back, dgain = norm_back(z_ref[...], gain_ref[1:2, :], out_ref[...])
    dgain_ref[0:1, :] = dgain
    out, dgain = norm_back(sum_ref[...], gain_ref[2:3, :], grad_ref[...] + back)
    dgain_ref[1:2, :] = dgain
    out_ref[...] = out
    low_ref[...] = out.astype(bf16)


def qkv_back_second(dq, dkv, w_qkv, grad, z, total, gains):
    shape = grad.shape
    return in_vmem(
        qkv_back_second_kernel,
        [(shape, f32), (shape, bf16), ((2, shape[1]), f32)],
        (dq, dkv, w_qkv, grad, z, total, gains),
    )


def qkv_back_first_kernel(
    start_ref, dq_ref, dkv_ref, w_ref, grad_ref, own_ref, send_ref, total
):
    qkv_back_product(dq_ref, dkv_ref, w_ref, total, grad_ref)
    split_rows(start_ref, total, own_ref, send_ref)


def qkv_back_first(start, dq, dkv, w_qkv, grad):
    rows, width = grad.shape
    half = (rows // 2, width)
    return in_vmem(
        qkv_back_first_kernel,
        [(half, f32), (half, bf16)],
        (dq, dkv, w_qkv, grad),
        (start,),
        [pltpu.VMEM(grad.shape, f32)],
    )


def merge_kernel(y_ref, own_ref, got_ref, out_ref):
    out_ref[y_ref[0], 0] = own_ref[...]
    out_ref[1 - y_ref[0], 0] = got_ref[...].astype(f32)


def merge(y, own, got):
    return in_vmem(merge_kernel, [((2, 1) + own.shape, f32)], (own, got), (y,))[0]


def key_tiles(role, block_index, own, other):
    if role == 0:
        table = [(own, 0), (other, 0), (other, 1), (own, 1)]
    else:
        table = [(other, 0), (own, 0), (own, 1), (other, 1)]
    return table[: block_index + 1]


def both_heads(values):
    lane = lax.broadcasted_iota(jnp.int32, values.shape, 1)
    zero = jnp.zeros_like(values)
    return jnp.concatenate(
        [jnp.where(lane < HD, values, zero), jnp.where(lane >= HD, values, zero)], 0
    )


def own_heads(values, rows):
    return jnp.concatenate([values[:HD, :rows], values[HD:, rows:]], 0)


def allowed_keys(rows):
    key = lax.broadcasted_iota(jnp.int32, (rows, rows), 0)
    query = lax.broadcasted_iota(jnp.int32, (rows, rows), 1)
    return jnp.concatenate([key <= query] * 2, 1)


def attn_fwd_kernel(role_ref, q_ref, ko_ref, vo_ref, kt_ref, vt_ref, o_ref, lse_ref):
    rows = q_ref.shape[0] // 2
    own, other = (0, ko_ref, vo_ref), (1, kt_ref, vt_ref)

    def one(role, j, turned):
        block_index = (role, 3 - role)[j]
        tiles = key_tiles(role, block_index, own, other)
        here = slice(j * rows, (j + 1) * rows)
        pair = both_heads(q_ref[here, :])
        allowed = allowed_keys(rows)
        scores = []
        top = None
        for t, ((_, k_ref, _), i) in enumerate(tiles):
            s = dot_nt(k_ref[i * rows : (i + 1) * rows, :], pair)
            if t == block_index:
                s = jnp.where(allowed, s, masked_value)
            scores.append(s)
            tile_top = jnp.max(s, 0, keepdims=True)
            top = tile_top if top is None else jnp.maximum(top, tile_top)
        total = None
        mixed = None
        for s, ((which, _, _), i) in zip(scores, tiles):
            p = jnp.exp2(s - top)
            part = jnp.sum(p, 0, keepdims=True)
            total = part if total is None else total + part
            m = dot(turned[(which, i)], p.astype(bf16))
            mixed = m if mixed is None else mixed + m
        mixed = mixed * (1.0 / total)
        sums = top + jnp.log2(total)
        for h in range(2):
            lse_ref[0, h : h + 1, here] = sums[:, h * rows : (h + 1) * rows]
        o_ref[here, :] = own_heads(mixed, rows).T.astype(bf16)

    for role in range(2):

        @pl.when(role_ref[0] == role)
        def _(role=role):
            turned = {}
            for which, _, v_ref in (own, other):
                for i in range(2):
                    turned[(which, i)] = v_ref[i * rows : (i + 1) * rows, :].T
            for j in range(2):
                one(role, j, turned)


def attn_forward(role, q, *kv):
    rows, width = q.shape
    pairs = width // LANES
    smem = pl.BlockSpec(memory_space=pltpu.SMEM)
    act = pl.BlockSpec((rows, LANES), lambda i: (0, i))

    return pl.pallas_call(
        attn_fwd_kernel,
        grid=(pairs,),
        in_specs=[smem] + [act] * 5,
        out_specs=[act, pl.BlockSpec((1, 2, rows), lambda i: (i, 0, 0))],
        out_shape=[
            jax.ShapeDtypeStruct((rows, width), bf16),
            jax.ShapeDtypeStruct((pairs, 2, rows), f32),
        ],
        compiler_params=pltpu.CompilerParams(vmem_limit_bytes=12 * MIB),
        cost_estimate=FREE,
    )(role, q, *kv)


def attn_bwd_kernel(
    role_ref, q_ref, ko_ref, vo_ref, kt_ref, vt_ref, lse_ref, o_ref, do_ref,
    cos_ref, sin_ref, dq_ref, down_ref, *rest
):
    *other_refs, acc_ref = rest
    rows = q_ref.shape[0] // 2
    own, other = (0, ko_ref, vo_ref), (1, kt_ref, vt_ref)

    def one(role, j, seen, turned):
        block_index = (role, 3 - role)[j]
        tiles = key_tiles(role, block_index, own, other)
        here = slice(j * rows, (j + 1) * rows)
        pair, grads = both_heads(q_ref[here, :]), both_heads(do_ref[here, :])
        allowed = allowed_keys(rows)
        both = (do_ref[here, :].astype(f32) * o_ref[here, :].astype(f32)).T
        delta = jnp.concatenate(
            [jnp.sum(both[h * HD : (h + 1) * HD, :], 0, keepdims=True) for h in range(2)], 1
        )
        lse = jnp.concatenate([lse_ref[0, h : h + 1, here] for h in range(2)], 1)
        total = None
        for t, ((which, k_ref, v_ref), i) in enumerate(tiles):
            there = slice(i * rows, (i + 1) * rows)
            s = dot_nt(k_ref[there, :], pair)
            p = jnp.exp2(s - lse)
            if t == block_index:
                p = jnp.where(allowed, p, 0.0)
            dp = dot_nt(v_ref[there, :], grads)
            ds = (p * (dp - delta)).astype(bf16)
            dv = dot(p.astype(bf16), grads)
            dk = dot(ds, pair)
            dq = dot(turned[(which, i)], ds)
            total = dq if total is None else total + dq
            key = (which, i)
            if key in seen:
                acc_ref[which, 0, there, :] += dk
                acc_ref[which, 1, there, :] += dv
            else:
                seen.add(key)
                acc_ref[which, 0, there, :] = dk
                acc_ref[which, 1, there, :] = dv
        grad = own_heads(total, rows).T * (HD**-0.5)
        dq_ref[here, :] = turn(grad, cos_ref[here, :], -sin_ref[here, :]).astype(bf16)

    for role in range(2):

        @pl.when(role_ref[0] == role)
        def _(role=role):
            seen, turned = set(), {}
            for which, k_ref, _ in (own, other):
                for i in range(2):
                    turned[(which, i)] = k_ref[i * rows : (i + 1) * rows, :].T
            for j in range(2):
                one(role, j, seen, turned)
            for which in range(2):
                for i in range(2):
                    if (which, i) not in seen:
                        zeros = jnp.zeros((2, rows, LANES), f32)
                        acc_ref[which, :, i * rows : (i + 1) * rows, :] = zeros

    down_ref[0] = (acc_ref[0, 0] * math.log(2.0)).astype(bf16)
    down_ref[1] = acc_ref[0, 1].astype(bf16)
    other_refs[0][...] = (acc_ref[1, 0] * math.log(2.0)).astype(bf16)
    other_refs[1][...] = acc_ref[1, 1].astype(bf16)


def attn_backward(role, q, k_own, v_own, k_other, v_other, lse, o, do, tables):
    rows, width = q.shape
    pairs = width // LANES
    smem = pl.BlockSpec(memory_space=pltpu.SMEM)
    act = pl.BlockSpec((rows, LANES), lambda i: (0, i))
    tab = pl.BlockSpec((rows, LANES), lambda i: (0, 0))
    two = pl.BlockSpec((2, rows, LANES), lambda i: (0, 0, i))

    return pl.pallas_call(
        attn_bwd_kernel,
        grid=(pairs,),
        in_specs=[
            smem, act, act, act, act, act,
            pl.BlockSpec((1, 2, rows), lambda i: (i, 0, 0)), act, act, tab, tab,
        ],
        out_specs=[act, two, act, act],
        out_shape=[
            jax.ShapeDtypeStruct((rows, width), bf16),
            jax.ShapeDtypeStruct((2, rows, width), bf16),
        ]
        + [jax.ShapeDtypeStruct((rows, width), bf16)] * 2,
        scratch_shapes=[pltpu.VMEM((2, 2, rows, LANES), f32)],
        compiler_params=pltpu.CompilerParams(vmem_limit_bytes=12 * MIB),
        cost_estimate=FREE,
    )(role, q, k_own, v_own, k_other, v_other, lse, o, do, *tables)


class Places:
    def __init__(self):
        self.count = lax.axis_size("fsdp")
        self.seq = lax.axis_size("seq")
        self.f = lax.axis_index("fsdp")
        self.s = lax.axis_index("seq")
        self.far, self.near = self.f // 2, self.f % 2
        self.shifts = self.count // 2
        self.core = self.s % 2
        self.y = self.s // 2

    def over_far(self, value):
        groups = [list(range(i, self.count, 2)) for i in range(2)]
        return lax.all_to_all(value, "fsdp", 0, 0, axis_index_groups=groups, tiled=True)

    def over_near(self, value):
        return lax.ppermute(value, "fsdp", [(i, i ^ 1) for i in range(self.count)])

    def over_core(self, value):
        return lax.ppermute(value, "seq", [(i, i ^ 1) for i in range(self.seq)])

    def over_y(self, value):
        return lax.ppermute(value, "seq", [(i, i ^ 2) for i in range(self.seq)])

    def mirror(self, value):
        last = self.seq - 1
        return lax.ppermute(value, "seq", [(i, last - i) for i in range(self.seq)])


def after(value, *others):
    return lax.optimization_barrier((value,) + others)[0]


def pick(value, index, axis):
    return lax.dynamic_index_in_dim(value, index, axis, keepdims=False)


def place_kernel(plans, unit_ref, slot_ref, *refs):
    count = len(plans)
    pieces, outs = refs[:count], refs[count:]
    for a, (piece, plan) in enumerate(zip(pieces, plans)):
        for k in range(piece.shape[0]):
            unit = unit_ref[a * piece.shape[0] + k]
            for out_index, slot, start, size, by_rows in plan:
                number = unit * 2 + slot_ref[a] if by_rows else unit
                row = pl.multiple_of(number * size, 16)
                if isinstance(slot, tuple):
                    slot = slot_ref[a] * slot[0] + slot[1]
                outs[out_index][slot, pl.ds(row, size), :] = piece[k, start : start + size, :]


def place(order, out_shapes, *groups):
    plans, pieces, units, slots = [], [], [], []
    for gather, plan in groups:
        for value, unit, slot in gather.pieces():
            plans.append(plan)
            pieces.append(value)
            units.append(unit)
            slots.append(slot)
    units = jnp.concatenate(units).astype(jnp.int32)
    slots = jnp.stack(slots).astype(jnp.int32)

    def call(*values):
        return in_vmem(
            lambda *refs: place_kernel(plans, *refs),
            [(shape, bf16) for shape in out_shapes],
            values,
            (units, slots),
        )

    return order(call, *pieces)


class Order:
    def __init__(self):
        self.last = ()

    def wait(self, *values):
        self.last = self.last + values

    def __call__(self, function, *operands):
        if self.last:
            operands = (after(operands[0], *self.last),) + operands[1:]
        out = function(*operands)
        self.last = (out[0] if isinstance(out, (tuple, list)) else out,)
        return out


class Gather:
    def __init__(self, at, order, own, by_y=False):
        self.at, self.order, self.own, self.by_y = at, order, own, by_y

    def far(self):
        own = after(self.own, *self.order.last) if self.order.last else self.own
        self.here = self.at.over_far(jnp.broadcast_to(own[None], (self.at.shifts,) + own.shape))

    def arrived(self, value):
        value = after(value, *self.order.last)
        self.order.wait(value)
        return value

    def near(self):
        self.here = self.arrived(self.here)
        self.there = self.at.over_near(self.here)
        if self.by_y:
            self.here_y = self.at.over_y(self.here)
        self.here_core = self.at.over_core(self.here)

    def middle(self):
        self.there = self.arrived(self.there)
        self.there_y = self.at.over_y(self.there)
        self.there_core = self.at.over_core(self.there)
        self.here_y = self.arrived(self.here_y)
        self.here_y_core = self.at.over_core(self.here_y)

    def cores(self):
        if self.by_y:
            self.there_y = self.arrived(self.there_y)
            self.there_y_core = self.at.over_core(self.there_y)
        else:
            self.there = self.arrived(self.there)
            self.there_core = self.at.over_core(self.there)

    def pieces(self):
        at = self.at
        far = jnp.arange(at.shifts, dtype=jnp.int32)
        values = [(self.here, self.there, self.here_core, self.there_core)]
        if self.by_y:
            more = (self.here_y, self.there_y, self.here_y_core, self.there_y_core)
            values.append(more)
        for side, four in enumerate(values):
            for i, value in enumerate(four):
                near, core = at.near ^ (i % 2), at.core ^ (i // 2)
                yield value, (far * 2 + near) * 2 + core, at.y ^ side


class GatherWhole(Gather):
    def far(self):
        rows = self.own.shape[0]
        own = after(self.own, *self.order.last)
        here = lax.all_gather(own, "fsdp", axis=0, tiled=True)
        self.here = here.reshape(self.at.count, rows, here.shape[1])

    def near(self):
        self.here = self.arrived(self.here)
        if self.by_y:
            self.here_y = self.at.over_y(self.here)
        self.here_core = self.at.over_core(self.here)

    def cores(self):
        if self.by_y:
            self.here_y = self.arrived(self.here_y)
            self.here_y_core = self.at.over_core(self.here_y)
        else:
            self.here_core = self.arrived(self.here_core)

    def pieces(self):
        at = self.at
        shard = jnp.arange(at.count, dtype=jnp.int32)
        yield self.here, shard * 2 + at.core, at.y
        yield self.here_core, shard * 2 + 1 - at.core, at.y
        if not self.by_y:
            return
        yield self.here_y, shard * 2 + at.core, 1 - at.y
        yield self.here_y_core, shard * 2 + 1 - at.core, 1 - at.y


class Group:
    def __init__(self, weights, count, extra=0, apart=False):
        self.weights, self.count, self.extra, self.apart = weights, count, extra, apart
        self.cols = [n // 2 for *_, n in weights]
        self.tiles = [c // LANES for c in self.cols]
        self.parts = [w[3] // count for w in weights]
        self.bases, self.offsets = [], []
        base = offset = 0
        for w, tiles, part in zip(weights, self.tiles, self.parts):
            self.bases.append(base)
            self.offsets.append(offset)
            base += w[3] * tiles
            offset += part * tiles
        self.extra_base, self.extra_offset = base, offset
        self.rows = offset + extra

    def halves(self):
        extra = [(self.extra * self.count, LANES)] if self.extra else []
        if self.apart:
            return [(w[3] * t, LANES) for w, t in zip(self.weights, self.tiles)] + extra
        return [(self.extra_base, LANES)] + extra

    def tile(self, refs, i, tile):
        rows = self.weights[i][3]
        if self.apart:
            return refs[i].at[tile * rows : (tile + 1) * rows, :]
        start = self.bases[i] + tile * rows
        return refs[0].at[start : start + rows, :]

    def products(self, half, lefts, rights):
        for i, (a, g, slot, _, _) in enumerate(self.weights):
            left = lefts[a][...]
            right = rights[g] if slot is None else rights[g].at[slot]
            step = 256 if self.cols[i] % 256 == 0 else self.cols[i]
            for start in range(0, self.cols[i], step):
                col = pl.multiple_of(half * self.cols[i] + start, LANES)
                yield i, start // LANES, dot_tn(left, right[:, pl.ds(col, step)])


def theirs_kernel(group, n_left, n_right, place_ref, *refs):
    lefts, rights = refs[:n_left], refs[n_left : n_left + n_right]
    rest = refs[n_left + n_right :]
    outs = rest[1:] if group.extra else rest
    for i, tile, value in group.products(1 - place_ref[0], lefts, rights):
        for j in range(value.shape[1] // LANES):
            group.tile(outs, i, tile + j)[...] = value[:, j * LANES : (j + 1) * LANES].astype(
                bf16
            )
    if group.extra:
        outs[-1][...] = rest[0][...].astype(bf16)


def mine_kernel(group, by_y, n_left, n_right, place_ref, *refs):
    lefts, rights = refs[:n_left], refs[n_left : n_left + n_right]
    rest = refs[n_left + n_right :]
    keep_ref, send_ref, scratch = rest[-3:]
    gots = rest[1:-3] if group.extra else rest[:-3]
    side = place_ref[3] if by_y else place_ref[1]

    def hand_out(size, cols, offset):
        half = size // 2 if by_y else size
        first = offset // 2 if by_y else offset
        for index in range(keep_ref.shape[0]):
            for ref, own in ((keep_ref, side), (send_ref, 1 - side)):
                row = pl.multiple_of((index * 2 + own) * half, 8)
                for j in range(cols // LANES):
                    ref[index, first + j * half : first + (j + 1) * half, :] = scratch[
                        pl.ds(row, half), j * LANES : (j + 1) * LANES
                    ].astype(bf16)

    for i, tile, value in group.products(place_ref[0], lefts, rights):
        rows, cols = value.shape
        for j in range(cols // LANES):
            got = group.tile(gots, i, tile + j)[...].astype(f32)
            cut = slice(j * LANES, (j + 1) * LANES)
            scratch[:rows, cut] = value[:, cut] + got
        part = group.parts[i]
        hand_out(part, cols, group.offsets[i] + tile * part)
    if group.extra:
        rows = group.extra * group.count
        scratch[:rows, :LANES] = rest[0][...].astype(f32) + gots[-1][...].astype(f32)
        hand_out(group.extra, LANES, group.extra_offset)


def mine_all_kernel(group, n_left, n_right, place_ref, *refs):
    lefts, rights = refs[:n_left], refs[n_left : n_left + n_right]
    gots, out_ref = refs[n_left + n_right : -1], refs[-1]
    for i, tile, value in group.products(place_ref[0], lefts, rights):
        part = group.parts[i]
        for j in range(value.shape[1] // LANES):
            got = group.tile(gots, i, tile + j)[...].astype(f32)
            total = value[:, j * LANES : (j + 1) * LANES] + got
            first = group.offsets[i] + (tile + j) * part
            for shard in range(group.count):
                out_ref[shard, first : first + part, :] = total[
                    shard * part : (shard + 1) * part, :
                ].astype(bf16)


def split_near_kernel(place_ref, keep_ref, got_ref, stay_ref, leave_ref):
    near = place_ref[1]
    for far in range(stay_ref.shape[0]):
        for ref, side in ((stay_ref, near), (leave_ref, 1 - near)):
            shard = 2 * far + side
            ref[far] = (keep_ref[shard].astype(f32) + got_ref[shard].astype(f32)).astype(bf16)


def sum_kernel(parts_ref, out_ref):
    total = parts_ref[0].astype(f32)
    for k in range(1, parts_ref.shape[0]):
        total = total + parts_ref[k].astype(f32)
    out_ref[...] = total.astype(bf16)


class Reduce:
    def __init__(self, at, order, group, by_y, whole, lefts, rights, extra=()):
        self.at, self.order, self.group = at, order, group
        self.by_y, self.whole = by_y, whole
        self.operands = (*lefts, *rights, *extra)
        self.counts = (len(lefts), len(rights))

    def theirs(self):
        group = self.group

        def call(*operands):
            return in_vmem(
                lambda *refs: theirs_kernel(group, *self.counts, *refs),
                [(shape, bf16) for shape in group.halves()],
                operands,
                (self.at.scalars,),
            )

        self.got = in_parts(self.at.over_core, self.order(call, *self.operands))

    def mine(self):
        group, at = self.group, self.at
        shape = (at.count, group.rows // 2) if self.by_y else (at.shifts, group.rows)
        shape += (LANES,)
        tall = max(w[3] for w in group.weights)
        wide = max(c if c % 256 else 256 for c in group.cols)

        def call(*operands):
            return in_vmem(
                lambda *refs: mine_kernel(group, self.by_y, *self.counts, *refs),
                [(shape, bf16), (shape, bf16)],
                operands,
                (at.scalars,),
                [pltpu.VMEM((tall, wide), f32)],
                limit=10,
            )

        if self.whole and not self.by_y:
            total = self.order(self.mine_all, *self.operands, *self.got)
            self.got = lax.psum_scatter(total, "fsdp", scatter_dimension=0, tiled=True)
            return
        self.keep, send = self.order(call, *self.operands, *self.got)
        self.got = at.over_y(send) if self.by_y else at.over_near(send)

    def mine_all(self, *operands):
        group = self.group
        return in_vmem(
            lambda *refs: mine_all_kernel(group, *self.counts, *refs),
            [((self.at.count, group.rows, LANES), bf16)],
            operands,
            (self.at.scalars,),
            limit=10,
        )[0]

    def split(self):
        if self.whole:
            total = self.order(join, self.keep, self.got)
            self.got = lax.psum_scatter(total, "fsdp", scatter_dimension=0, tiled=True)
            return
        shape = (self.at.shifts,) + self.keep.shape[1:]

        def call(*operands):
            return in_vmem(
                split_near_kernel,
                [(shape, bf16), (shape, bf16)],
                operands,
                (self.at.scalars,),
            )

        self.keep, send = self.order(call, self.keep, self.got)
        self.got = self.at.over_near(send)

    def deal(self):
        self.got = self.at.over_far(self.order(join, self.keep, self.got))

    def gather(self):
        def call(parts):
            return in_vmem(sum_kernel, [(parts.shape[1:], bf16)], (parts,))[0]

        if self.whole:
            self.total = after(self.got, *self.order.last)[0]
            self.order.wait(self.total)
        else:
            self.total = self.order(call, self.got)
        self.got = self.at.over_y(self.total)
        if self.by_y:
            self.other = self.at.over_core(self.total)

    def finish(self):
        if self.by_y:
            self.got = after(self.got, *self.order.last)
            self.order.wait(self.got)
            self.got_other = self.at.over_core(self.got)
        else:
            self.total = self.order(join, self.total, self.got)
            self.other = self.at.over_core(self.total)

    def flats(self):
        if self.by_y:
            return (self.total, self.other, self.got, self.got_other)
        return (self.total, self.other)


def unpack_kernel(reduces, plan, extra, place_ref, *refs):
    flats, at = [], 0
    for r in reduces:
        flats.append(refs[at : at + len(r.flats())])
        at += len(r.flats())
    outs = refs[at:]

    for out_ref, blocks in zip(outs, plan):
        for block, (g, i) in enumerate(blocks):
            group, ways = reduces[g].group, len(flats[g]) // 2
            cols, part = group.cols[i], group.parts[i] // ways
            for n, flat in enumerate(flats[g]):
                first = (place_ref[0] ^ (n % 2)) * cols
                row = pl.multiple_of((place_ref[3] ^ (n // 2)) * part, 8) if ways == 2 else 0
                for j in range(group.tiles[i]):
                    start = group.offsets[i] // ways + j * part
                    col = pl.multiple_of(first + j * LANES, LANES)
                    out_ref[block, pl.ds(row, part), pl.ds(col, LANES)] = flat[
                        start : start + part, :
                    ].astype(f32)

    if extra is not None:
        group = reduces[extra].group
        outs[-1][...] = flats[extra][0][group.extra_offset :, :].astype(f32)


def unpack(at, order, reduces, plan, extra=None):
    outs = []
    for blocks in plan:
        group, i = reduces[blocks[0][0]].group, blocks[0][1]
        outs.append(((len(blocks), group.parts[i], 2 * group.cols[i]), f32))
    if extra is not None:
        outs.append(((reduces[extra].group.extra, LANES), f32))

    def call(*operands):
        return in_vmem(
            lambda *refs: unpack_kernel(reduces, plan, extra, *refs),
            outs,
            operands,
            (at.scalars,),
        )

    return order(call, *[v for r in reduces for v in r.flats()])


def per_device(
    hidden_in,
    cotangent,
    attn_gain,
    query_weight,
    key_weight,
    value_weight,
    out_weight,
    ffn_gain,
    gate_weight,
    up_weight,
    down_weight,
):
    at = Places()
    order = Order()
    rows, d = hidden_in.shape[2:]
    ff = gate_weight.shape[2]
    p, q = query_weight.shape[1], down_weight.shape[1]
    assert hidden_in.shape[0] == 2 and at.seq == 4
    direct = p % 32 == 0 and q % 32 == 0
    at.scalars = jnp.stack([at.core, at.near, at.far, at.y]).astype(jnp.int32)

    low = jnp.minimum(at.s, 3 - at.s)
    role = low.astype(jnp.int32).reshape(1)
    first_is_own = at.s < 2
    own_start = jnp.where(first_is_own, 0, rows).astype(jnp.int32).reshape(1)
    y = at.y.astype(jnp.int32).reshape(1)

    def spread(value, *waits):
        own = pick(value[:, 0], at.y, 0)
        got = at.mirror(after(pick(value[:, 0], 1 - at.y, 0), *waits))
        return jnp.concatenate(
            [jnp.where(first_is_own, own, got), jnp.where(first_is_own, got, own)]
        )

    def tables_of(first):
        steps = jnp.arange(rows, dtype=jnp.int32)
        return rope_tables(
            jnp.concatenate([first * rows + steps, (3 - first) * rows + steps])
        )

    tables = tables_of(low)
    attn_shards = jnp.stack([query_weight, key_weight, value_weight, out_weight], 1)
    gu_shards = jnp.stack([gate_weight, up_weight], 1)
    gain_shards = jnp.concatenate([attn_gain, ffn_gain])


    act = spread(hidden_in)
    cot = spread(cotangent)
    if direct:
        ph, qh = p // 2, q // 2

        def half(value, axis):
            size = value.shape[axis] // 2
            return lax.dynamic_slice_in_dim(value, at.core * size, size, axis)

        attn_half, gu_half, down_half = half(attn_shards, 2), half(gu_shards, 2), half(down_weight, 1)
        gain_rows = jnp.zeros((16, d), bf16).at[0, : 4 * p].set(gain_shards.reshape(4 * p))
        attn_part = pick(attn_half[0].reshape(2, 2 * ph, d), at.y, 0)
        a0 = Gather(at, order, jnp.concatenate([attn_part, gain_rows]), True)
        gu0 = Gather(at, order, pick(gu_half[0], at.y, 0), True)
        d0 = Gather(at, order, pick(down_half[0].reshape(2, qh // 2, d), at.y, 0), True)
        a1 = GatherWhole(at, order, attn_half[1].reshape(4 * ph, d))
        d1 = Gather(at, order, pick(down_half[1].reshape(2, qh // 2, d), at.y, 0), True)
        gu1 = GatherWhole(at, order, gu_half[1].reshape(2 * ph, ff))
        a0_plan = [(0, (2, i), i * ph, ph, False) for i in range(2)]
        gu_plan = [(0, (1, 0), 0, ph, False)]
        d0_plan = [(0, 0, 0, qh // 2, True)]
        a1_plan = [(0, i, i * ph, ph, False) for i in range(4)]
        gu1_plan = [(0, i, i * ph, ph, False) for i in range(2)]
        attn_shape, gu_shape, down_shape = (4, d, d), (2, d, ff), (1, ff, d)

        a0.far()
        order.wait(act, cot)
        a0.near()
        gu0.far()
        a0.middle()
        a0.cores()
        gu0.near()
        a1.far()
        gu1.far()
        (w_attn0,) = place(order, [attn_shape], (a0, a0_plan))
        w_out0 = w_attn0[3]
        index = ((jnp.arange(at.count) % 2) ^ at.near) * at.shifts
        index = index + jnp.arange(at.count) // 2
        gain_got = jnp.concatenate(
            [a0.here[:, 2 * ph, : 4 * p], a0.there[:, 2 * ph, : 4 * p]]
        )
        select = jax.nn.one_hot(index, at.count, dtype=f32)
        gains = jnp.dot(select, gain_got.astype(f32), precision=lax.Precision.HIGHEST)
        gains = gains.reshape(at.count, 4, p).transpose(1, 0, 2).reshape(4, d)
    else:

        def whole(value, axis):
            return lax.all_gather(value, "fsdp", axis=axis, tiled=True)

        attn_all, gu_all, down_all = whole(attn_shards, 2), whole(gu_shards, 2), whole(down_weight, 1)
        gains = whole(gain_shards, 1).astype(f32)
        w_attn0, w_out0 = attn_all[0], attn_all[0, 3]

    q0, *kv0 = order(lambda *v: project_qkv(*v, tables), act, w_attn0)
    kv0_other = in_parts(at.over_core, kv0)
    if direct:
        d0.far()
    o0, lse0 = order(lambda *v: attn_forward(role, *v), q0, *kv0, *kv0_other)
    if direct:
        d0.near()
    sum0, act0 = order(lambda *v: project_out(0, *v), o0, w_out0, act, gains)
    if direct:
        gu0.middle()
        gu0.cores()
        (w_gu0,) = place(order, [gu_shape], (gu0, gu_plan))
    else:
        w_gu0 = gu_all[0]
    hidden0, silu0, slope0 = order(ffn_in, act0, w_gu0)
    if direct:
        d0.middle()
        d1.far()
        d0.cores()
        a1.near()
        w_down0 = place(order, [down_shape], (d0, d0_plan))[0][0]
    else:
        w_down0 = down_all[0]
    sum1, z, act1 = order(ffn_out_first, hidden0, w_down0, sum0, gains)
    if direct:
        a1.cores()
        (w_attn1,) = place(order, [attn_shape], (a1, a1_plan))
        w_out1 = w_attn1[3]
        d1.near()
    else:
        w_attn1, w_out1, w_down1 = attn_all[1], attn_all[1, 3], down_all[1]
    q1, *kv1 = order(lambda *v: project_qkv(*v, tables), act1, w_attn1)
    kv1_other = in_parts(at.over_core, kv1)
    o1, lse1 = order(lambda *v: attn_forward(role, *v), q1, *kv1, *kv1_other)
    sum2, act2 = order(lambda *v: project_out(3, *v), o1, w_out1, z, gains)
    if direct:
        d1.middle()
        gu1.near()
        gu1.cores()
        (w_gu1,) = place(order, [gu_shape], (gu1, gu1_plan))
    else:
        w_gu1 = gu_all[1]
    hidden1, silu1, slope1 = order(ffn_in, act2, w_gu1)
    if direct:
        d1.cores()
        w_down1 = place(order, [down_shape], (d1, d0_plan))[0][0]
    out_own, out_send = order(
        lambda *v: ffn_out_second(own_start, *v), hidden1, w_down1, sum2
    )


    ffn_group = [(0, 0, 0, d, ff), (0, 0, 1, d, ff), (1, 1, None, ff, d), (2, 2, None, d, d)]
    gu_group = [(0, 0, 0, d, ff), (0, 0, 1, d, ff)]
    rest_group = [(0, 0, None, ff, d), (1, 1, None, d, d)]
    qkv_group = [(0, 0, None, d, d), (0, 1, 0, d, d), (0, 1, 1, d, d)]

    def reduce(weights, by_y, whole, *rest):
        group = Group(weights, at.count, 16 * (len(rest) == 3), weights is not ffn_group)
        return Reduce(at, order, group, by_y, whole, *rest)

    dgu1, grad, low1, do1, dgain_f1 = order(
        lambda *v: ffn_back(False, *v), cot, silu1, slope1, w_down1, w_gu1, w_out1, sum2, gains
    )
    if direct:
        r1 = reduce(ffn_group, False, True, (act2, hidden1, o1), (dgu1, cot, low1))
        r1.theirs()
    dq1, dkv1, *dkv1_other = order(
        lambda *v: attn_backward(role, *v, tables),
        q1, *kv1, *kv1_other, lse1, o1, do1,
    )
    dkv1_got = in_parts(at.over_core, dkv1_other)
    if direct:
        r1.mine()
    dkv1 = order(join_parts, dkv1, *dkv1_got, *tables)
    if direct:
        r2 = reduce(qkv_group, False, False, (act1,), (dq1, dkv1))
        r2.theirs()
    grad, low_mid, dgain_mid = order(
        qkv_back_second, dq1, dkv1, w_attn1, grad, z, sum1, gains
    )
    if direct:
        r2.mine()
    out_got = at.mirror(after(out_send, *order.last))
    dgu0, grad, low0, do0, dgain_a0 = order(
        lambda *v: ffn_back(True, *v), grad, silu0, slope0, w_down0, w_gu0, w_out0, sum0, gains
    )
    layer_out = order(lambda *v: merge(y, *v), out_own, out_got)
    if direct:
        r3 = reduce(gu_group, True, False, (act0,), (dgu0,))
        s3 = reduce(rest_group, False, False, (hidden0, o0), (low_mid, low0))
        r3.theirs()
        s3.theirs()
        r3.mine()
        s3.mine()
    dq0, dkv0, *dkv0_other = order(
        lambda *v: attn_backward(role, *v, tables),
        q0, *kv0, *kv0_other, lse0, o0, do0,
    )
    dkv0_got = in_parts(at.over_core, dkv0_other)
    if direct:
        r2.deal()
        r3.split()
    dkv0 = order(join_parts, dkv0, *dkv0_got, *tables)
    dgains = jnp.concatenate([dgain_a0, dgain_mid, dgain_f1])
    if direct:
        extra = dgains.reshape(4, at.count, p).transpose(1, 0, 2).reshape(at.count, -1, LANES)
        extra = jnp.pad(extra, ((0, 0), (0, 16 - extra.shape[1]), (0, 0)))
        extra = extra.reshape(at.count * 16, LANES)
        r4 = reduce(qkv_group, False, False, (act,), (dq0, dkv0), (extra,))
        r4.theirs()
        s3.deal()
    in_own, in_send = order(
        lambda *v: qkv_back_first(own_start, *v), dq0, dkv0, w_attn0, grad
    )
    in_got = at.mirror(in_send)

    if direct:
        r4.mine()
        input_grad = order(lambda *v: merge(y, *v), in_own, in_got)
        r3.deal()
        r2.gather()
        r1.gather()
        r2.finish()
        r1.finish()
        s3.gather()
        r4.deal()
        s3.finish()
        r3.gather()
        r3.finish()
        grad_gate, grad_up, grad_down, grad_out = unpack(
            at, order, [r3, s3, r1],
            [[(0, 0), (2, 0)], [(0, 1), (2, 1)], [(1, 0), (2, 2)], [(1, 1), (2, 3)]],
        )
        r4.gather()
        r4.finish()
        *grad_qkv, gain_rows = unpack(
            at, order, [r4, r2], [[(0, i), (1, i)] for i in range(3)], 0
        )
        gain_grads = gain_rows.reshape(-1)[: 4 * p].reshape(4, p)
    else:
        input_grad = merge(y, in_own, in_got)

        def sums(*values):
            total = jnp.stack(values).astype(bf16)
            total = lax.psum_scatter(total, "fsdp", scatter_dimension=1, tiled=True)
            return lax.psum(total, "seq").astype(f32)

        grad_qkv = [
            sums(dot_tn(act, dq0), dot_tn(act1, dq1)),
            sums(dot_tn(act, dkv0[0]), dot_tn(act1, dkv1[0])),
            sums(dot_tn(act, dkv0[1]), dot_tn(act1, dkv1[1])),
        ]
        grad_gate = sums(dot_tn(act0, dgu0[0]), dot_tn(act2, dgu1[0]))
        grad_up = sums(dot_tn(act0, dgu0[1]), dot_tn(act2, dgu1[1]))
        grad_down = sums(dot_tn(hidden0, low_mid), dot_tn(hidden1, cot))
        grad_out = sums(dot_tn(o0, low0), dot_tn(o1, low1))
        gain_grads = lax.psum_scatter(dgains, "fsdp", scatter_dimension=1, tiled=True)
        gain_grads = lax.psum(gain_grads, "seq")
    return (
        layer_out,
        input_grad,
        gain_grads[:2],
        *grad_qkv,
        grad_out,
        gain_grads[2:],
        grad_gate,
        grad_up,
        grad_down,
    )


def solution(mesh):
    tokens = P(None, "fsdp", "seq", None)
    gain = P(None, "fsdp")
    weight = P(None, "fsdp", None)
    return jax.shard_map(
        per_device,
        mesh=mesh,
        in_specs=(tokens, tokens, gain) + (weight,) * 4 + (gain,) + (weight,) * 3,
        out_specs=(tokens, tokens, gain) + (weight,) * 4 + (gain,) + (weight,) * 3,
        check_vma=False,
    )
```

```python
import math

import jax
import jax.numpy as jnp
from jax import lax
from jax.experimental import pallas as pl
from jax.experimental.pallas import tpu as pltpu
from jax.sharding import PartitionSpec as P

HD = 64
LANES = 128
epsilon = 1e-05
masked_value = -1e30
QUERY_SCALE = HD**-0.5 * math.log2(math.e)
bf16 = jnp.bfloat16
f32 = jnp.float32
MIB = 1 << 20
CHUNK = 256
FREE = pl.CostEstimate(flops=1, bytes_accessed=1, transcendentals=0)
NT = (((1,), (1,)), ((), ()))
TN = (((0,), (0,)), ((), ()))


def rope_tables(positions):
    half_dim = HD // 2
    rates = jnp.exp(jnp.arange(half_dim, dtype=f32) * (-2.0 * math.log(10000.0) / HD))
    angles = positions.astype(f32)[:, None] * rates[None, :]
    repeat = LANES // half_dim
    return jnp.tile(jnp.cos(angles), (1, repeat)), jnp.tile(jnp.sin(angles), (1, repeat))


def turn(values, cosine, sine):
    lane = lax.broadcasted_iota(jnp.int32, values.shape, 1)
    first = (lane % HD) < HD // 2
    back = pltpu.roll(values, LANES - HD // 2, 1)
    ahead = pltpu.roll(values, HD // 2, 1)
    return values * cosine + jnp.where(first, -back, ahead) * sine


def in_vmem(kernel, outs, operands, scalars=(), scratch=(), limit=6):
    smem = [pl.BlockSpec(memory_space=pltpu.SMEM)] * len(scalars)
    vmem = pl.BlockSpec(memory_space=pltpu.VMEM)
    moved = sum(v.size * v.dtype.itemsize for v in operands)
    moved += sum(math.prod(shape) * jnp.dtype(dtype).itemsize for shape, dtype in outs)
    room = limit * MIB + moved
    return pl.pallas_call(
        kernel,
        in_specs=smem + [vmem] * len(operands),
        out_specs=[vmem] * len(outs),
        out_shape=[jax.ShapeDtypeStruct(shape, dtype) for shape, dtype in outs],
        scratch_shapes=list(scratch),
        compiler_params=pltpu.CompilerParams(vmem_limit_bytes=room),
        cost_estimate=FREE,
    )(*scalars, *operands)


def chunks(size, step=CHUNK):
    return [slice(i, min(i + step, size)) for i in range(0, size, step)]


def root(values):
    return lax.rsqrt(jnp.mean(values * values, -1, keepdims=True) + epsilon)


def norm_back(values, gain, grad):
    scale = root(values)
    unit = values * scale
    inner = grad * gain
    out = scale * (inner - unit * jnp.mean(inner * unit, -1, keepdims=True))
    return out, jnp.sum(grad * unit, 0, keepdims=True)


def dot(left, right):
    return jnp.dot(left, right, preferred_element_type=f32)


def dot_nt(left, right):
    return lax.dot_general(left, right, NT, preferred_element_type=f32)


def dot_tn(left, right):
    return lax.dot_general(left, right, TN, preferred_element_type=f32)


def qkv_kernel(act_ref, w_ref, cos_ref, sin_ref, *outs):
    act = act_ref[...]
    for i in range(3):
        for cols in chunks(act.shape[1]):
            prod = dot(act, w_ref[i, :, cols])
            for at in range(cols.start, cols.stop, LANES):
                part = prod[:, at - cols.start : at - cols.start + LANES]
                if i < 2:
                    part = turn(part, cos_ref[...], sin_ref[...])
                if i == 0:
                    part = part * QUERY_SCALE
                outs[i][:, at : at + LANES] = part.astype(bf16)


def project_qkv(act, w_qkv, tables):
    rows, width = act.shape
    outs = [((rows, width), bf16)] * 3
    return in_vmem(qkv_kernel, outs, (act, w_qkv, *tables))


def out_kernel(which, o_ref, w_ref, resid_ref, gain_ref, sum_ref, act_ref):
    o = o_ref[...]
    for cols in chunks(o.shape[1]):
        sum_ref[:, cols] = resid_ref[:, cols].astype(f32) + dot(o, w_ref[:, cols])
    total = sum_ref[...]
    act_ref[...] = (total * root(total) * gain_ref[which : which + 1, :]).astype(bf16)


def project_out(which, o, w_out, resid, gains):
    shape = o.shape
    return in_vmem(
        lambda *refs: out_kernel(which, *refs),
        [(shape, f32), (shape, bf16)],
        (o, w_out, resid, gains),
    )


def ffn_in_kernel(act_ref, w_ref, hidden_ref, silu_ref, slope_ref):
    act = act_ref[...]
    for cols in chunks(hidden_ref.shape[1]):
        gate = dot(act, w_ref[0, :, cols])
        up = dot(act, w_ref[1, :, cols])
        sig = jax.nn.sigmoid(gate)
        silu = gate * sig
        hidden_ref[:, cols] = (silu * up).astype(bf16)
        silu_ref[:, cols] = silu.astype(bf16)
        slope_ref[:, cols] = (up * sig * (1.0 + gate * (1.0 - sig))).astype(bf16)


def ffn_in(act, w_gu):
    shape = (act.shape[0], w_gu.shape[2])
    return in_vmem(ffn_in_kernel, [(shape, bf16)] * 3, (act, w_gu))


def ffn_out_first_kernel(hid_ref, w_ref, sum_ref, gain_ref, next_ref, z_ref, act_ref):
    total = sum_ref[...]
    next_ref[...] = total * root(total) * gain_ref[0:1, :]
    hid = hid_ref[...]
    for cols in chunks(w_ref.shape[1]):
        next_ref[:, cols] += dot(hid, w_ref[:, cols])
    total = next_ref[...]
    z = total * root(total) * gain_ref[2:3, :]
    z_ref[...] = z
    act_ref[...] = (z * root(z) * gain_ref[1:2, :]).astype(bf16)


def ffn_out_first(hidden, w_down, total, gains):
    shape = total.shape
    return in_vmem(
        ffn_out_first_kernel,
        [(shape, f32), (shape, f32), (shape, bf16)],
        (hidden, w_down, total, gains),
    )


def split_rows(start_ref, value_ref, own_ref, send_ref):
    rows = own_ref.shape[0]
    own = pl.multiple_of(start_ref[0], rows)
    send = pl.multiple_of(rows - start_ref[0], rows)
    own_ref[...] = value_ref[pl.ds(own, rows), :]
    send_ref[...] = value_ref[pl.ds(send, rows), :].astype(bf16)


def ffn_out_second_kernel(start_ref, hid_ref, w_ref, sum_ref, own_ref, send_ref, total):
    hid = hid_ref[...]
    for cols in chunks(w_ref.shape[1]):
        total[:, cols] = sum_ref[:, cols] + dot(hid, w_ref[:, cols])
    split_rows(start_ref, total, own_ref, send_ref)


def ffn_out_second(start, hidden, w_down, total):
    rows, width = total.shape
    half = (rows // 2, width)
    return in_vmem(
        ffn_out_second_kernel,
        [(half, f32), (half, bf16)],
        (hidden, w_down, total),
        (start,),
        [pltpu.VMEM(total.shape, f32)],
    )


def ffn_back_kernel(
    post, grad_ref, silu_ref, slope_ref, wd_ref, wgu_ref, wo_ref, sum_ref, gain_ref,
    dgu_ref, total_ref, low_ref, do_ref, dgain_ref,
):
    grad_low = grad_ref[...].astype(bf16)
    for cols in chunks(wd_ref.shape[0]):
        hid = dot_nt(grad_low, wd_ref[cols, :])
        dgu_ref[0, :, cols] = (hid * slope_ref[:, cols].astype(f32)).astype(bf16)
        dgu_ref[1, :, cols] = (hid * silu_ref[:, cols].astype(f32)).astype(bf16)
    for cols in chunks(total_ref.shape[1]):
        back = dot_nt(dgu_ref[0], wgu_ref[0, cols, :])
        back += dot_nt(dgu_ref[1], wgu_ref[1, cols, :])
        total_ref[:, cols] = back
    if post:
        out, dgain = norm_back(
            sum_ref[...], gain_ref[0:1, :], grad_ref[...] + total_ref[...]
        )
    else:
        out, dgain = norm_back(sum_ref[...], gain_ref[3:4, :], total_ref[...])
        out = grad_ref[...].astype(f32) + out
    dgain_ref[...] = dgain
    total_ref[...] = out
    low_ref[...] = out.astype(bf16)
    low = low_ref[...]
    for cols in chunks(total_ref.shape[1]):
        do_ref[:, cols] = dot_nt(low, wo_ref[cols, :]).astype(bf16)


def ffn_back(post, grad, silu, slope, w_down, w_gu, w_out, total, gains):
    shape = total.shape
    outs = [
        ((2,) + silu.shape, bf16), (shape, f32), (shape, bf16), (shape, bf16),
        ((1, shape[1]), f32),
    ]
    return in_vmem(
        lambda *refs: ffn_back_kernel(post, *refs),
        outs,
        (grad, silu, slope, w_down, w_gu, w_out, total, gains),
    )


def join_kernel(a_ref, b_ref, out_ref):
    out_ref[...] = (a_ref[...].astype(f32) + b_ref[...].astype(f32)).astype(bf16)


def join(a, b):
    return in_vmem(join_kernel, [(a.shape, bf16)], (a, b))[0]


def join_parts_kernel(a_ref, dk_ref, dv_ref, cos_ref, sin_ref, out_ref):
    for at in range(0, a_ref.shape[2], LANES):
        cols = slice(at, at + LANES)
        total = a_ref[0, :, cols].astype(f32) + dk_ref[:, cols].astype(f32)
        out_ref[0, :, cols] = turn(total, cos_ref[...], -sin_ref[...]).astype(bf16)
    out_ref[1] = (a_ref[1].astype(f32) + dv_ref[...].astype(f32)).astype(bf16)


def join_parts(a, *rest):
    return in_vmem(join_parts_kernel, [(a.shape, bf16)], (a, *rest))[0]


def in_parts(send, values):
    return [send(v) for v in values]


def qkv_back_product(dq_ref, dkv_ref, w_ref, out_ref, base_ref):
    dq, dk, dv = dq_ref[...], dkv_ref[0], dkv_ref[1]
    for cols in chunks(out_ref.shape[1]):
        back = dot_nt(dq, w_ref[0, cols, :])
        back += dot_nt(dk, w_ref[1, cols, :])
        back += dot_nt(dv, w_ref[2, cols, :])
        if base_ref is not None:
            back += base_ref[:, cols]
        out_ref[:, cols] = back


def qkv_back_second_kernel(
    dq_ref, dkv_ref, w_ref, grad_ref, z_ref, sum_ref, gain_ref,
    out_ref, low_ref, dgain_ref,
):
    qkv_back_product(dq_ref, dkv_ref, w_ref, out_ref, None)
    back, dgain = norm_back(z_ref[...], gain_ref[1:2, :], out_ref[...])
    dgain_ref[0:1, :] = dgain
    out, dgain = norm_back(sum_ref[...], gain_ref[2:3, :], grad_ref[...] + back)
    dgain_ref[1:2, :] = dgain
    out_ref[...] = out
    low_ref[...] = out.astype(bf16)


def qkv_back_second(dq, dkv, w_qkv, grad, z, total, gains):
    shape = grad.shape
    return in_vmem(
        qkv_back_second_kernel,
        [(shape, f32), (shape, bf16), ((2, shape[1]), f32)],
        (dq, dkv, w_qkv, grad, z, total, gains),
    )


def qkv_back_first_kernel(
    start_ref, dq_ref, dkv_ref, w_ref, grad_ref, own_ref, send_ref, total
):
    qkv_back_product(dq_ref, dkv_ref, w_ref, total, grad_ref)
    split_rows(start_ref, total, own_ref, send_ref)


def qkv_back_first(start, dq, dkv, w_qkv, grad):
    rows, width = grad.shape
    half = (rows // 2, width)
    return in_vmem(
        qkv_back_first_kernel,
        [(half, f32), (half, bf16)],
        (dq, dkv, w_qkv, grad),
        (start,),
        [pltpu.VMEM(grad.shape, f32)],
    )


def merge_kernel(y_ref, own_ref, got_ref, out_ref):
    out_ref[y_ref[0], 0] = own_ref[...]
    out_ref[1 - y_ref[0], 0] = got_ref[...].astype(f32)


def merge(y, own, got):
    return in_vmem(merge_kernel, [((2, 1) + own.shape, f32)], (own, got), (y,))[0]


def key_tiles(role, block_index, own, other):
    if role == 0:
        table = [(own, 0), (other, 0), (other, 1), (own, 1)]
    else:
        table = [(other, 0), (own, 0), (own, 1), (other, 1)]
    return table[: block_index + 1]


def both_heads(values):
    lane = lax.broadcasted_iota(jnp.int32, values.shape, 1)
    zero = jnp.zeros_like(values)
    return jnp.concatenate(
        [jnp.where(lane < HD, values, zero), jnp.where(lane >= HD, values, zero)], 0
    )


def own_heads(values, rows):
    return jnp.concatenate([values[:HD, :rows], values[HD:, rows:]], 0)


def allowed_keys(rows):
    key = lax.broadcasted_iota(jnp.int32, (rows, rows), 0)
    query = lax.broadcasted_iota(jnp.int32, (rows, rows), 1)
    return jnp.concatenate([key <= query] * 2, 1)


def attn_fwd_kernel(role_ref, q_ref, ko_ref, vo_ref, kt_ref, vt_ref, o_ref, lse_ref):
    rows = q_ref.shape[0] // 2
    own, other = (0, ko_ref, vo_ref), (1, kt_ref, vt_ref)

    def one(role, j, turned):
        block_index = (role, 3 - role)[j]
        tiles = key_tiles(role, block_index, own, other)
        here = slice(j * rows, (j + 1) * rows)
        pair = both_heads(q_ref[here, :])
        allowed = allowed_keys(rows)
        scores = []
        top = None
        for t, ((_, k_ref, _), i) in enumerate(tiles):
            s = dot_nt(k_ref[i * rows : (i + 1) * rows, :], pair)
            if t == block_index:
                s = jnp.where(allowed, s, masked_value)
            scores.append(s)
            tile_top = jnp.max(s, 0, keepdims=True)
            top = tile_top if top is None else jnp.maximum(top, tile_top)
        total = None
        mixed = None
        for s, ((which, _, _), i) in zip(scores, tiles):
            p = jnp.exp2(s - top)
            part = jnp.sum(p, 0, keepdims=True)
            total = part if total is None else total + part
            m = dot(turned[(which, i)], p.astype(bf16))
            mixed = m if mixed is None else mixed + m
        mixed = mixed * (1.0 / total)
        sums = top + jnp.log2(total)
        for h in range(2):
            lse_ref[0, h : h + 1, here] = sums[:, h * rows : (h + 1) * rows]
        o_ref[here, :] = own_heads(mixed, rows).T.astype(bf16)

    for role in range(2):

        @pl.when(role_ref[0] == role)
        def _(role=role):
            turned = {}
            for which, _, v_ref in (own, other):
                for i in range(2):
                    turned[(which, i)] = v_ref[i * rows : (i + 1) * rows, :].T
            for j in range(2):
                one(role, j, turned)


def attn_forward(role, q, *kv):
    rows, width = q.shape
    pairs = width // LANES
    smem = pl.BlockSpec(memory_space=pltpu.SMEM)
    act = pl.BlockSpec((rows, LANES), lambda i: (0, i))

    return pl.pallas_call(
        attn_fwd_kernel,
        grid=(pairs,),
        in_specs=[smem] + [act] * 5,
        out_specs=[act, pl.BlockSpec((1, 2, rows), lambda i: (i, 0, 0))],
        out_shape=[
            jax.ShapeDtypeStruct((rows, width), bf16),
            jax.ShapeDtypeStruct((pairs, 2, rows), f32),
        ],
        compiler_params=pltpu.CompilerParams(vmem_limit_bytes=12 * MIB),
        cost_estimate=FREE,
    )(role, q, *kv)


def attn_bwd_kernel(
    role_ref, q_ref, ko_ref, vo_ref, kt_ref, vt_ref, lse_ref, o_ref, do_ref,
    cos_ref, sin_ref, dq_ref, down_ref, *rest
):
    *other_refs, acc_ref = rest
    rows = q_ref.shape[0] // 2
    own, other = (0, ko_ref, vo_ref), (1, kt_ref, vt_ref)

    def one(role, j, seen, turned):
        block_index = (role, 3 - role)[j]
        tiles = key_tiles(role, block_index, own, other)
        here = slice(j * rows, (j + 1) * rows)
        pair, grads = both_heads(q_ref[here, :]), both_heads(do_ref[here, :])
        allowed = allowed_keys(rows)
        both = (do_ref[here, :].astype(f32) * o_ref[here, :].astype(f32)).T
        delta = jnp.concatenate(
            [jnp.sum(both[h * HD : (h + 1) * HD, :], 0, keepdims=True) for h in range(2)], 1
        )
        lse = jnp.concatenate([lse_ref[0, h : h + 1, here] for h in range(2)], 1)
        total = None
        for t, ((which, k_ref, v_ref), i) in enumerate(tiles):
            there = slice(i * rows, (i + 1) * rows)
            s = dot_nt(k_ref[there, :], pair)
            p = jnp.exp2(s - lse)
            if t == block_index:
                p = jnp.where(allowed, p, 0.0)
            dp = dot_nt(v_ref[there, :], grads)
            ds = (p * (dp - delta)).astype(bf16)
            dv = dot(p.astype(bf16), grads)
            dk = dot(ds, pair)
            dq = dot(turned[(which, i)], ds)
            total = dq if total is None else total + dq
            key = (which, i)
            if key in seen:
                acc_ref[which, 0, there, :] += dk
                acc_ref[which, 1, there, :] += dv
            else:
                seen.add(key)
                acc_ref[which, 0, there, :] = dk
                acc_ref[which, 1, there, :] = dv
        grad = own_heads(total, rows).T * (HD**-0.5)
        dq_ref[here, :] = turn(grad, cos_ref[here, :], -sin_ref[here, :]).astype(bf16)

    for role in range(2):

        @pl.when(role_ref[0] == role)
        def _(role=role):
            seen, turned = set(), {}
            for which, k_ref, _ in (own, other):
                for i in range(2):
                    turned[(which, i)] = k_ref[i * rows : (i + 1) * rows, :].T
            for j in range(2):
                one(role, j, seen, turned)
            for which in range(2):
                for i in range(2):
                    if (which, i) not in seen:
                        zeros = jnp.zeros((2, rows, LANES), f32)
                        acc_ref[which, :, i * rows : (i + 1) * rows, :] = zeros

    down_ref[0] = (acc_ref[0, 0] * math.log(2.0)).astype(bf16)
    down_ref[1] = acc_ref[0, 1].astype(bf16)
    other_refs[0][...] = (acc_ref[1, 0] * math.log(2.0)).astype(bf16)
    other_refs[1][...] = acc_ref[1, 1].astype(bf16)


def attn_backward(role, q, k_own, v_own, k_other, v_other, lse, o, do, tables):
    rows, width = q.shape
    pairs = width // LANES
    smem = pl.BlockSpec(memory_space=pltpu.SMEM)
    act = pl.BlockSpec((rows, LANES), lambda i: (0, i))
    tab = pl.BlockSpec((rows, LANES), lambda i: (0, 0))
    two = pl.BlockSpec((2, rows, LANES), lambda i: (0, 0, i))

    return pl.pallas_call(
        attn_bwd_kernel,
        grid=(pairs,),
        in_specs=[
            smem, act, act, act, act, act,
            pl.BlockSpec((1, 2, rows), lambda i: (i, 0, 0)), act, act, tab, tab,
        ],
        out_specs=[act, two, act, act],
        out_shape=[
            jax.ShapeDtypeStruct((rows, width), bf16),
            jax.ShapeDtypeStruct((2, rows, width), bf16),
        ]
        + [jax.ShapeDtypeStruct((rows, width), bf16)] * 2,
        scratch_shapes=[pltpu.VMEM((2, 2, rows, LANES), f32)],
        compiler_params=pltpu.CompilerParams(vmem_limit_bytes=12 * MIB),
        cost_estimate=FREE,
    )(role, q, k_own, v_own, k_other, v_other, lse, o, do, *tables)


class Places:
    def __init__(self):
        self.count = lax.axis_size("fsdp")
        self.seq = lax.axis_size("seq")
        self.f = lax.axis_index("fsdp")
        self.s = lax.axis_index("seq")
        self.far, self.near = self.f // 2, self.f % 2
        self.shifts = self.count // 2
        self.core = self.s % 2
        self.y = self.s // 2

    def over_far(self, value):
        groups = [list(range(i, self.count, 2)) for i in range(2)]
        return lax.all_to_all(value, "fsdp", 0, 0, axis_index_groups=groups, tiled=True)

    def over_near(self, value):
        return lax.ppermute(value, "fsdp", [(i, i ^ 1) for i in range(self.count)])

    def over_core(self, value):
        return lax.ppermute(value, "seq", [(i, i ^ 1) for i in range(self.seq)])

    def over_y(self, value):
        return lax.ppermute(value, "seq", [(i, i ^ 2) for i in range(self.seq)])

    def mirror(self, value):
        last = self.seq - 1
        return lax.ppermute(value, "seq", [(i, last - i) for i in range(self.seq)])


def after(value, *others):
    return lax.optimization_barrier((value,) + others)[0]


def pick(value, index, axis):
    return lax.dynamic_index_in_dim(value, index, axis, keepdims=False)


def place_kernel(plans, unit_ref, slot_ref, *refs):
    count = len(plans)
    pieces, outs = refs[:count], refs[count:]
    for a, (piece, plan) in enumerate(zip(pieces, plans)):
        for k in range(piece.shape[0]):
            unit = unit_ref[a * piece.shape[0] + k]
            for out_index, slot, start, size, by_rows in plan:
                number = unit * 2 + slot_ref[a] if by_rows else unit
                row = pl.multiple_of(number * size, 16)
                if isinstance(slot, tuple):
                    slot = slot_ref[a] * slot[0] + slot[1]
                outs[out_index][slot, pl.ds(row, size), :] = piece[k, start : start + size, :]


def place(order, out_shapes, *groups):
    plans, pieces, units, slots = [], [], [], []
    for gather, plan in groups:
        for value, unit, slot in gather.pieces():
            plans.append(plan)
            pieces.append(value)
            units.append(unit)
            slots.append(slot)
    units = jnp.concatenate(units).astype(jnp.int32)
    slots = jnp.stack(slots).astype(jnp.int32)

    def call(*values):
        return in_vmem(
            lambda *refs: place_kernel(plans, *refs),
            [(shape, bf16) for shape in out_shapes],
            values,
            (units, slots),
        )

    return order(call, *pieces)


class Order:
    def __init__(self):
        self.last = ()

    def wait(self, *values):
        self.last = self.last + values

    def __call__(self, function, *operands):
        if self.last:
            operands = (after(operands[0], *self.last),) + operands[1:]
        out = function(*operands)
        self.last = (out[0] if isinstance(out, (tuple, list)) else out,)
        return out


class Gather:
    def __init__(self, at, order, own, by_y=False):
        self.at, self.order, self.own, self.by_y = at, order, own, by_y

    def far(self):
        own = after(self.own, *self.order.last) if self.order.last else self.own
        self.here = self.at.over_far(jnp.broadcast_to(own[None], (self.at.shifts,) + own.shape))

    def arrived(self, value):
        value = after(value, *self.order.last)
        self.order.wait(value)
        return value

    def near(self):
        self.here = self.arrived(self.here)
        self.there = self.at.over_near(self.here)
        if self.by_y:
            self.here_y = self.at.over_y(self.here)
        self.here_core = self.at.over_core(self.here)

    def middle(self):
        self.there = self.arrived(self.there)
        self.there_y = self.at.over_y(self.there)
        self.there_core = self.at.over_core(self.there)
        self.here_y = self.arrived(self.here_y)
        self.here_y_core = self.at.over_core(self.here_y)

    def cores(self):
        if self.by_y:
            self.there_y = self.arrived(self.there_y)
            self.there_y_core = self.at.over_core(self.there_y)
        else:
            self.there = self.arrived(self.there)
            self.there_core = self.at.over_core(self.there)

    def pieces(self):
        at = self.at
        far = jnp.arange(at.shifts, dtype=jnp.int32)
        values = [(self.here, self.there, self.here_core, self.there_core)]
        if self.by_y:
            more = (self.here_y, self.there_y, self.here_y_core, self.there_y_core)
            values.append(more)
        for side, four in enumerate(values):
            for i, value in enumerate(four):
                near, core = at.near ^ (i % 2), at.core ^ (i // 2)
                yield value, (far * 2 + near) * 2 + core, at.y ^ side


class GatherWhole(Gather):
    def far(self):
        rows = self.own.shape[0]
        own = after(self.own, *self.order.last)
        here = lax.all_gather(own, "fsdp", axis=0, tiled=True)
        self.here = here.reshape(self.at.count, rows, here.shape[1])

    def near(self):
        self.here = self.arrived(self.here)
        if self.by_y:
            self.here_y = self.at.over_y(self.here)
        self.here_core = self.at.over_core(self.here)

    def cores(self):
        if self.by_y:
            self.here_y = self.arrived(self.here_y)
            self.here_y_core = self.at.over_core(self.here_y)
        else:
            self.here_core = self.arrived(self.here_core)

    def pieces(self):
        at = self.at
        shard = jnp.arange(at.count, dtype=jnp.int32)
        yield self.here, shard * 2 + at.core, at.y
        yield self.here_core, shard * 2 + 1 - at.core, at.y
        if not self.by_y:
            return
        yield self.here_y, shard * 2 + at.core, 1 - at.y
        yield self.here_y_core, shard * 2 + 1 - at.core, 1 - at.y


class Group:
    def __init__(self, weights, count, extra=0, apart=False):
        self.weights, self.count, self.extra, self.apart = weights, count, extra, apart
        self.cols = [n // 2 for *_, n in weights]
        self.tiles = [c // LANES for c in self.cols]
        self.parts = [w[3] // count for w in weights]
        self.bases, self.offsets = [], []
        base = offset = 0
        for w, tiles, part in zip(weights, self.tiles, self.parts):
            self.bases.append(base)
            self.offsets.append(offset)
            base += w[3] * tiles
            offset += part * tiles
        self.extra_base, self.extra_offset = base, offset
        self.rows = offset + extra

    def halves(self):
        extra = [(self.extra * self.count, LANES)] if self.extra else []
        if self.apart:
            return [(w[3] * t, LANES) for w, t in zip(self.weights, self.tiles)] + extra
        return [(self.extra_base, LANES)] + extra

    def tile(self, refs, i, tile):
        rows = self.weights[i][3]
        if self.apart:
            return refs[i].at[tile * rows : (tile + 1) * rows, :]
        start = self.bases[i] + tile * rows
        return refs[0].at[start : start + rows, :]

    def products(self, half, lefts, rights):
        for i, (a, g, slot, _, _) in enumerate(self.weights):
            left = lefts[a][...]
            right = rights[g] if slot is None else rights[g].at[slot]
            step = 256 if self.cols[i] % 256 == 0 else self.cols[i]
            for start in range(0, self.cols[i], step):
                col = pl.multiple_of(half * self.cols[i] + start, LANES)
                yield i, start // LANES, dot_tn(left, right[:, pl.ds(col, step)])


def theirs_kernel(group, n_left, n_right, place_ref, *refs):
    lefts, rights = refs[:n_left], refs[n_left : n_left + n_right]
    rest = refs[n_left + n_right :]
    outs = rest[1:] if group.extra else rest
    for i, tile, value in group.products(1 - place_ref[0], lefts, rights):
        for j in range(value.shape[1] // LANES):
            group.tile(outs, i, tile + j)[...] = value[:, j * LANES : (j + 1) * LANES].astype(
                bf16
            )
    if group.extra:
        outs[-1][...] = rest[0][...].astype(bf16)


def mine_kernel(group, by_y, n_left, n_right, place_ref, *refs):
    lefts, rights = refs[:n_left], refs[n_left : n_left + n_right]
    rest = refs[n_left + n_right :]
    keep_ref, send_ref, scratch = rest[-3:]
    gots = rest[1:-3] if group.extra else rest[:-3]
    side = place_ref[3] if by_y else place_ref[1]

    def hand_out(size, cols, offset):
        half = size // 2 if by_y else size
        first = offset // 2 if by_y else offset
        for index in range(keep_ref.shape[0]):
            for ref, own in ((keep_ref, side), (send_ref, 1 - side)):
                row = pl.multiple_of((index * 2 + own) * half, 8)
                for j in range(cols // LANES):
                    ref[index, first + j * half : first + (j + 1) * half, :] = scratch[
                        pl.ds(row, half), j * LANES : (j + 1) * LANES
                    ].astype(bf16)

    for i, tile, value in group.products(place_ref[0], lefts, rights):
        rows, cols = value.shape
        for j in range(cols // LANES):
            got = group.tile(gots, i, tile + j)[...].astype(f32)
            cut = slice(j * LANES, (j + 1) * LANES)
            scratch[:rows, cut] = value[:, cut] + got
        part = group.parts[i]
        hand_out(part, cols, group.offsets[i] + tile * part)
    if group.extra:
        rows = group.extra * group.count
        scratch[:rows, :LANES] = rest[0][...].astype(f32) + gots[-1][...].astype(f32)
        hand_out(group.extra, LANES, group.extra_offset)


def mine_all_kernel(group, n_left, n_right, place_ref, *refs):
    lefts, rights = refs[:n_left], refs[n_left : n_left + n_right]
    gots, out_ref = refs[n_left + n_right : -1], refs[-1]
    for i, tile, value in group.products(place_ref[0], lefts, rights):
        part = group.parts[i]
        for j in range(value.shape[1] // LANES):
            got = group.tile(gots, i, tile + j)[...].astype(f32)
            total = value[:, j * LANES : (j + 1) * LANES] + got
            first = group.offsets[i] + (tile + j) * part
            for shard in range(group.count):
                out_ref[shard, first : first + part, :] = total[
                    shard * part : (shard + 1) * part, :
                ].astype(bf16)


def split_near_kernel(place_ref, keep_ref, got_ref, stay_ref, leave_ref):
    near = place_ref[1]
    for far in range(stay_ref.shape[0]):
        for ref, side in ((stay_ref, near), (leave_ref, 1 - near)):
            shard = 2 * far + side
            ref[far] = (keep_ref[shard].astype(f32) + got_ref[shard].astype(f32)).astype(bf16)


def sum_kernel(parts_ref, out_ref):
    total = parts_ref[0].astype(f32)
    for k in range(1, parts_ref.shape[0]):
        total = total + parts_ref[k].astype(f32)
    out_ref[...] = total.astype(bf16)


class Reduce:
    def __init__(self, at, order, group, by_y, whole, lefts, rights, extra=()):
        self.at, self.order, self.group = at, order, group
        self.by_y, self.whole = by_y, whole
        self.operands = (*lefts, *rights, *extra)
        self.counts = (len(lefts), len(rights))

    def theirs(self):
        group = self.group

        def call(*operands):
            return in_vmem(
                lambda *refs: theirs_kernel(group, *self.counts, *refs),
                [(shape, bf16) for shape in group.halves()],
                operands,
                (self.at.scalars,),
            )

        self.got = in_parts(self.at.over_core, self.order(call, *self.operands))

    def mine(self):
        group, at = self.group, self.at
        shape = (at.count, group.rows // 2) if self.by_y else (at.shifts, group.rows)
        shape += (LANES,)
        tall = max(w[3] for w in group.weights)
        wide = max(c if c % 256 else 256 for c in group.cols)

        def call(*operands):
            return in_vmem(
                lambda *refs: mine_kernel(group, self.by_y, *self.counts, *refs),
                [(shape, bf16), (shape, bf16)],
                operands,
                (at.scalars,),
                [pltpu.VMEM((tall, wide), f32)],
                limit=10,
            )

        if self.whole and not self.by_y:
            total = self.order(self.mine_all, *self.operands, *self.got)
            self.got = lax.psum_scatter(total, "fsdp", scatter_dimension=0, tiled=True)
            return
        self.keep, send = self.order(call, *self.operands, *self.got)
        self.got = at.over_y(send) if self.by_y else at.over_near(send)

    def mine_all(self, *operands):
        group = self.group
        return in_vmem(
            lambda *refs: mine_all_kernel(group, *self.counts, *refs),
            [((self.at.count, group.rows, LANES), bf16)],
            operands,
            (self.at.scalars,),
            limit=10,
        )[0]

    def split(self):
        if self.whole:
            total = self.order(join, self.keep, self.got)
            self.got = lax.psum_scatter(total, "fsdp", scatter_dimension=0, tiled=True)
            return
        shape = (self.at.shifts,) + self.keep.shape[1:]

        def call(*operands):
            return in_vmem(
                split_near_kernel,
                [(shape, bf16), (shape, bf16)],
                operands,
                (self.at.scalars,),
            )

        self.keep, send = self.order(call, self.keep, self.got)
        self.got = self.at.over_near(send)

    def deal(self):
        self.got = self.at.over_far(self.order(join, self.keep, self.got))

    def gather(self):
        def call(parts):
            return in_vmem(sum_kernel, [(parts.shape[1:], bf16)], (parts,))[0]

        if self.whole:
            self.total = after(self.got, *self.order.last)[0]
            self.order.wait(self.total)
        else:
            self.total = self.order(call, self.got)
        self.got = self.at.over_y(self.total)
        if self.by_y:
            self.other = self.at.over_core(self.total)

    def finish(self):
        if self.by_y:
            self.got = after(self.got, *self.order.last)
            self.order.wait(self.got)
            self.got_other = self.at.over_core(self.got)
        else:
            self.total = self.order(join, self.total, self.got)
            self.other = self.at.over_core(self.total)

    def flats(self):
        if self.by_y:
            return (self.total, self.other, self.got, self.got_other)
        return (self.total, self.other)


def unpack_kernel(reduces, plan, extra, place_ref, *refs):
    flats, at = [], 0
    for r in reduces:
        flats.append(refs[at : at + len(r.flats())])
        at += len(r.flats())
    outs = refs[at:]

    for out_ref, blocks in zip(outs, plan):
        for block, (g, i) in enumerate(blocks):
            group, ways = reduces[g].group, len(flats[g]) // 2
            cols, part = group.cols[i], group.parts[i] // ways
            for n, flat in enumerate(flats[g]):
                first = (place_ref[0] ^ (n % 2)) * cols
                row = pl.multiple_of((place_ref[3] ^ (n // 2)) * part, 8) if ways == 2 else 0
                for j in range(group.tiles[i]):
                    start = group.offsets[i] // ways + j * part
                    col = pl.multiple_of(first + j * LANES, LANES)
                    out_ref[block, pl.ds(row, part), pl.ds(col, LANES)] = flat[
                        start : start + part, :
                    ].astype(f32)

    if extra is not None:
        group = reduces[extra].group
        outs[-1][...] = flats[extra][0][group.extra_offset :, :].astype(f32)


def unpack(at, order, reduces, plan, extra=None):
    outs = []
    for blocks in plan:
        group, i = reduces[blocks[0][0]].group, blocks[0][1]
        outs.append(((len(blocks), group.parts[i], 2 * group.cols[i]), f32))
    if extra is not None:
        outs.append(((reduces[extra].group.extra, LANES), f32))

    def call(*operands):
        return in_vmem(
            lambda *refs: unpack_kernel(reduces, plan, extra, *refs),
            outs,
            operands,
            (at.scalars,),
        )

    return order(call, *[v for r in reduces for v in r.flats()])


def per_device(
    hidden_in,
    cotangent,
    attn_gain,
    query_weight,
    key_weight,
    value_weight,
    out_weight,
    ffn_gain,
    gate_weight,
    up_weight,
    down_weight,
):
    at = Places()
    order = Order()
    rows, d = hidden_in.shape[2:]
    ff = gate_weight.shape[2]
    p, q = query_weight.shape[1], down_weight.shape[1]
    assert hidden_in.shape[0] == 2 and at.seq == 4
    direct = p % 32 == 0 and q % 32 == 0
    at.scalars = jnp.stack([at.core, at.near, at.far, at.y]).astype(jnp.int32)

    low = jnp.minimum(at.s, 3 - at.s)
    role = low.astype(jnp.int32).reshape(1)
    first_is_own = at.s < 2
    own_start = jnp.where(first_is_own, 0, rows).astype(jnp.int32).reshape(1)
    y = at.y.astype(jnp.int32).reshape(1)

    def spread(value, *waits):
        own = pick(value[:, 0], at.y, 0)
        got = at.mirror(after(pick(value[:, 0], 1 - at.y, 0), *waits))
        return jnp.concatenate(
            [jnp.where(first_is_own, own, got), jnp.where(first_is_own, got, own)]
        )

    def tables_of(first):
        steps = jnp.arange(rows, dtype=jnp.int32)
        return rope_tables(
            jnp.concatenate([first * rows + steps, (3 - first) * rows + steps])
        )

    tables = tables_of(low)
    attn_shards = jnp.stack([query_weight, key_weight, value_weight, out_weight], 1)
    gu_shards = jnp.stack([gate_weight, up_weight], 1)
    gain_shards = jnp.concatenate([attn_gain, ffn_gain])


    act = spread(hidden_in)
    cot = spread(cotangent)
    if direct:
        ph, qh = p // 2, q // 2

        def half(value, axis):
            size = value.shape[axis] // 2
            return lax.dynamic_slice_in_dim(value, at.core * size, size, axis)

        attn_half, gu_half, down_half = half(attn_shards, 2), half(gu_shards, 2), half(down_weight, 1)
        gain_rows = jnp.zeros((16, d), bf16).at[0, : 4 * p].set(gain_shards.reshape(4 * p))
        attn_part = pick(attn_half[0].reshape(2, 2 * ph, d), at.y, 0)
        a0 = Gather(at, order, jnp.concatenate([attn_part, gain_rows]), True)
        gu0 = Gather(at, order, pick(gu_half[0], at.y, 0), True)
        d0 = Gather(at, order, pick(down_half[0].reshape(2, qh // 2, d), at.y, 0), True)
        a1 = GatherWhole(at, order, attn_half[1].reshape(4 * ph, d))
        d1 = Gather(at, order, pick(down_half[1].reshape(2, qh // 2, d), at.y, 0), True)
        gu1 = GatherWhole(at, order, gu_half[1].reshape(2 * ph, ff))
        a0_plan = [(0, (2, i), i * ph, ph, False) for i in range(2)]
        gu_plan = [(0, (1, 0), 0, ph, False)]
        d0_plan = [(0, 0, 0, qh // 2, True)]
        a1_plan = [(0, i, i * ph, ph, False) for i in range(4)]
        gu1_plan = [(0, i, i * ph, ph, False) for i in range(2)]
        attn_shape, gu_shape, down_shape = (4, d, d), (2, d, ff), (1, ff, d)

        a0.far()
        order.wait(act, cot)
        a0.near()
        gu0.far()
        a0.middle()
        a0.cores()
        gu0.near()
        a1.far()
        gu1.far()
        (w_attn0,) = place(order, [attn_shape], (a0, a0_plan))
        w_out0 = w_attn0[3]
        index = ((jnp.arange(at.count) % 2) ^ at.near) * at.shifts
        index = index + jnp.arange(at.count) // 2
        gain_got = jnp.concatenate(
            [a0.here[:, 2 * ph, : 4 * p], a0.there[:, 2 * ph, : 4 * p]]
        )
        select = jax.nn.one_hot(index, at.count, dtype=f32)
        gains = jnp.dot(select, gain_got.astype(f32), precision=lax.Precision.HIGHEST)
        gains = gains.reshape(at.count, 4, p).transpose(1, 0, 2).reshape(4, d)
    else:

        def whole(value, axis):
            return lax.all_gather(value, "fsdp", axis=axis, tiled=True)

        attn_all, gu_all, down_all = whole(attn_shards, 2), whole(gu_shards, 2), whole(down_weight, 1)
        gains = whole(gain_shards, 1).astype(f32)
        w_attn0, w_out0 = attn_all[0], attn_all[0, 3]

    q0, *kv0 = order(lambda *v: project_qkv(*v, tables), act, w_attn0)
    kv0_other = in_parts(at.over_core, kv0)
    if direct:
        d0.far()
    o0, lse0 = order(lambda *v: attn_forward(role, *v), q0, *kv0, *kv0_other)
    if direct:
        d0.near()
    sum0, act0 = order(lambda *v: project_out(0, *v), o0, w_out0, act, gains)
    if direct:
        gu0.middle()
        gu0.cores()
        (w_gu0,) = place(order, [gu_shape], (gu0, gu_plan))
    else:
        w_gu0 = gu_all[0]
    hidden0, silu0, slope0 = order(ffn_in, act0, w_gu0)
    if direct:
        d0.middle()
        d1.far()
        d0.cores()
        a1.near()
        w_down0 = place(order, [down_shape], (d0, d0_plan))[0][0]
    else:
        w_down0 = down_all[0]
    sum1, z, act1 = order(ffn_out_first, hidden0, w_down0, sum0, gains)
    if direct:
        a1.cores()
        (w_attn1,) = place(order, [attn_shape], (a1, a1_plan))
        w_out1 = w_attn1[3]
    else:
        w_attn1, w_out1, w_down1 = attn_all[1], attn_all[1, 3], down_all[1]
    q1, *kv1 = order(lambda *v: project_qkv(*v, tables), act1, w_attn1)
    kv1_other = in_parts(at.over_core, kv1)
    if direct:
        d1.near()
    o1, lse1 = order(lambda *v: attn_forward(role, *v), q1, *kv1, *kv1_other)
    sum2, act2 = order(lambda *v: project_out(3, *v), o1, w_out1, z, gains)
    if direct:
        d1.middle()
        gu1.near()
        gu1.cores()
        (w_gu1,) = place(order, [gu_shape], (gu1, gu1_plan))
    else:
        w_gu1 = gu_all[1]
    hidden1, silu1, slope1 = order(ffn_in, act2, w_gu1)
    if direct:
        d1.cores()
        w_down1 = place(order, [down_shape], (d1, d0_plan))[0][0]
    out_own, out_send = order(
        lambda *v: ffn_out_second(own_start, *v), hidden1, w_down1, sum2
    )


    ffn_group = [(0, 0, 0, d, ff), (0, 0, 1, d, ff), (1, 1, None, ff, d), (2, 2, None, d, d)]
    gu_group = [(0, 0, 0, d, ff), (0, 0, 1, d, ff)]
    rest_group = [(0, 0, None, ff, d), (1, 1, None, d, d)]
    qkv_group = [(0, 0, None, d, d), (0, 1, 0, d, d), (0, 1, 1, d, d)]

    def reduce(weights, by_y, whole, *rest):
        group = Group(weights, at.count, 16 * (len(rest) == 3), weights is not ffn_group)
        return Reduce(at, order, group, by_y, whole, *rest)

    dgu1, grad, low1, do1, dgain_f1 = order(
        lambda *v: ffn_back(False, *v), cot, silu1, slope1, w_down1, w_gu1, w_out1, sum2, gains
    )
    if direct:
        r1 = reduce(ffn_group, False, True, (act2, hidden1, o1), (dgu1, cot, low1))
        r1.theirs()
    dq1, dkv1, *dkv1_other = order(
        lambda *v: attn_backward(role, *v, tables),
        q1, *kv1, *kv1_other, lse1, o1, do1,
    )
    dkv1_got = in_parts(at.over_core, dkv1_other)
    if direct:
        r1.mine()
    dkv1 = order(join_parts, dkv1, *dkv1_got, *tables)
    if direct:
        r2 = reduce(qkv_group, False, False, (act1,), (dq1, dkv1))
        r2.theirs()
    grad, low_mid, dgain_mid = order(
        qkv_back_second, dq1, dkv1, w_attn1, grad, z, sum1, gains
    )
    if direct:
        r2.mine()
    out_got = at.mirror(after(out_send, *order.last))
    dgu0, grad, low0, do0, dgain_a0 = order(
        lambda *v: ffn_back(True, *v), grad, silu0, slope0, w_down0, w_gu0, w_out0, sum0, gains
    )
    layer_out = order(lambda *v: merge(y, *v), out_own, out_got)
    if direct:
        r3 = reduce(gu_group, True, False, (act0,), (dgu0,))
        s3 = reduce(rest_group, False, False, (hidden0, o0), (low_mid, low0))
        r3.theirs()
        s3.theirs()
        r3.mine()
        s3.mine()
    dq0, dkv0, *dkv0_other = order(
        lambda *v: attn_backward(role, *v, tables),
        q0, *kv0, *kv0_other, lse0, o0, do0,
    )
    dkv0_got = in_parts(at.over_core, dkv0_other)
    if direct:
        r2.deal()
        r3.split()
    dkv0 = order(join_parts, dkv0, *dkv0_got, *tables)
    dgains = jnp.concatenate([dgain_a0, dgain_mid, dgain_f1])
    if direct:
        extra = dgains.reshape(4, at.count, p).transpose(1, 0, 2).reshape(at.count, -1, LANES)
        extra = jnp.pad(extra, ((0, 0), (0, 16 - extra.shape[1]), (0, 0)))
        extra = extra.reshape(at.count * 16, LANES)
        r4 = reduce(qkv_group, False, False, (act,), (dq0, dkv0), (extra,))
        r4.theirs()
        s3.deal()
    in_own, in_send = order(
        lambda *v: qkv_back_first(own_start, *v), dq0, dkv0, w_attn0, grad
    )
    in_got = at.mirror(in_send)

    if direct:
        r4.mine()
        input_grad = order(lambda *v: merge(y, *v), in_own, in_got)
        r3.deal()
        r2.gather()
        r1.gather()
        r2.finish()
        r1.finish()
        s3.gather()
        r4.deal()
        s3.finish()
        r3.gather()
        r3.finish()
        grad_gate, grad_up, grad_down, grad_out = unpack(
            at, order, [r3, s3, r1],
            [[(0, 0), (2, 0)], [(0, 1), (2, 1)], [(1, 0), (2, 2)], [(1, 1), (2, 3)]],
        )
        r4.gather()
        r4.finish()
        *grad_qkv, gain_rows = unpack(
            at, order, [r4, r2], [[(0, i), (1, i)] for i in range(3)], 0
        )
        gain_grads = gain_rows.reshape(-1)[: 4 * p].reshape(4, p)
    else:
        input_grad = merge(y, in_own, in_got)

        def sums(*values):
            total = jnp.stack(values).astype(bf16)
            total = lax.psum_scatter(total, "fsdp", scatter_dimension=1, tiled=True)
            return lax.psum(total, "seq").astype(f32)

        grad_qkv = [
            sums(dot_tn(act, dq0), dot_tn(act1, dq1)),
            sums(dot_tn(act, dkv0[0]), dot_tn(act1, dkv1[0])),
            sums(dot_tn(act, dkv0[1]), dot_tn(act1, dkv1[1])),
        ]
        grad_gate = sums(dot_tn(act0, dgu0[0]), dot_tn(act2, dgu1[0]))
        grad_up = sums(dot_tn(act0, dgu0[1]), dot_tn(act2, dgu1[1]))
        grad_down = sums(dot_tn(hidden0, low_mid), dot_tn(hidden1, cot))
        grad_out = sums(dot_tn(o0, low0), dot_tn(o1, low1))
        gain_grads = lax.psum_scatter(dgains, "fsdp", scatter_dimension=1, tiled=True)
        gain_grads = lax.psum(gain_grads, "seq")
    return (
        layer_out,
        input_grad,
        gain_grads[:2],
        *grad_qkv,
        grad_out,
        gain_grads[2:],
        grad_gate,
        grad_up,
        grad_down,
    )


def solution(mesh):
    tokens = P(None, "fsdp", "seq", None)
    gain = P(None, "fsdp")
    weight = P(None, "fsdp", None)
    return jax.shard_map(
        per_device,
        mesh=mesh,
        in_specs=(tokens, tokens, gain) + (weight,) * 4 + (gain,) + (weight,) * 3,
        out_specs=(tokens, tokens, gain) + (weight,) * 4 + (gain,) + (weight,) * 3,
        check_vma=False,
    )
```
